32 devices in a mesh: dp: 16 (over z, y, core), pos: 2 (over x).
Axes of the slice: x: 2, y: 2, z: 4, core: 2. Of those that a mesh axis runs over, the one named last changes fastest.
Arguments:
- inputs: bfloat16 [32, 512, 512], P('dp', 'pos'), may hold values from -6 to 6
- pre_act: bfloat16 [32, 512, 512], P('dp', 'pos'), may hold values from -6 to 6
- grad_out: bfloat16 [32, 512, 512], P('dp', 'pos'), may hold values from -6 to 6
- weight: bfloat16 [512, 9, 512], P(('dp', 'pos')), may hold values from -0.09375 to 0.09375
Outputs:
- grad_input: bfloat16 [32, 512, 512], P('dp', 'pos')
- grad_weight: float32 [512, 9, 512], P(('dp', 'pos'))
The draws below stay inside these ranges and needn't reach their ends.
All inputs are finite; a program needn't handle non-finite values.
Results may differ from the reference program's by a relative error of at most 0.005.
Values may be sent and summed in bfloat16 or wider, within the bound.
No kernel may reach another device: no remote copies, remote signals or barrier semaphores. Data moves between devices by JAX's collectives and lax.ppermute only.
A program may use at most 128 MiB of HBM per device.

```python
import jax
import jax.numpy as jnp
from jax import lax

C = 512
K = 9
SEQS = 32
L = 512


def raised(array, rng, source, target, blocks, factor):
    def block_of(dim):
        return (jnp.arange(array.shape[dim]) // (array.shape[dim] // blocks)).reshape((-1,) + (1,) * (array.ndim - 1 - dim))

    one_side = jax.random.permutation(rng, blocks)[block_of(target)]
    second = (block_of(target) + blocks // 2) % blocks
    return jnp.where((block_of(source) == one_side) | (block_of(source) == second), factor * array, array)


def levels(stream_key, extent, pieces, least, top_value):
    level = 1.0
    for axis_at, blocks in pieces:
        draws = jax.random.uniform(jax.random.fold_in(jax.random.fold_in(stream_key, 6), axis_at), (blocks,), jnp.float32, least / len(pieces), top_value / len(pieces))
        level = level * jnp.repeat(jnp.exp(draws), extent[axis_at] // blocks).reshape((-1,) + (1,) * (len(extent) - 1 - axis_at))
    return level


def normal_values(key, dims, width, limit, cuts=(), dtype=jnp.bfloat16):
    gain = levels(key, dims, cuts, -0.22, 0.18) if cuts else 1.0
    result = jax.random.normal(key, dims, jnp.float32) * width * gain
    return jnp.minimum(jnp.maximum(result, -limit), limit).astype(dtype)


def heavy_noise(rng, dims, deviation, limit, cuts, heavy, held_as=jnp.bfloat16):
    array = deviation * jax.random.normal(rng, dims, jnp.float32)
    if cuts:
        array = array * levels(rng, dims, cuts, -0.22, 0.18)
    return jnp.clip(raised(array, jax.random.fold_in(rng, 3), *heavy), -limit, limit).astype(held_as)


def setup_inputs(seed: int = 0) -> dict:
    keys = jax.random.split(jax.random.key(seed), 5)
    return {
        "inputs": heavy_noise(keys[0], (SEQS, L, C), 1.0, 6.0, ((0, 16), (1, 2)), (1, 2, 2, 2.0)),
        "pre_act": normal_values(keys[1], (SEQS, L, C), 1.0, 6.0, ((0, 16), (1, 2))),
        "grad_out": normal_values(keys[2], (SEQS, L, C), 1.0, 6.0, ((0, 16), (1, 2))),
        "weight": normal_values(keys[3], (C, K, C), (K * C) ** -0.5, 0.09375, ((0, 32),)),
    }


def gelu_slope(values):
    cdf = 0.5 * (1.0 + lax.erf(values * 0.7071067811865476))
    return cdf + values * jnp.exp(-0.5 * values * values) * 0.3989422804014327


def transpose_conv(grad_pre, weight):
    half_width = (K - 1) // 2
    padded = jnp.pad(grad_pre, ((half_width, half_width), (0, 0)))
    total = jnp.zeros((L, C), jnp.float32)
    for offset in range(K):
        begin = K - 1 - offset
        total = total + jnp.dot(padded[begin:begin + L], weight[:, offset, :].T, preferred_element_type=jnp.float32)
    return total


def weight_terms(values, grad_pre):
    half_width = (K - 1) // 2
    padded = jnp.pad(values, ((half_width, half_width), (0, 0)))
    return jnp.stack([jnp.dot(padded[offset:offset + L].T, grad_pre, preferred_element_type=jnp.float32) for offset in range(K)], axis=1)


def reference(inputs, pre_act, grad_out, weight):
    def per_sequence(carry, sequence):
        x_seq, pre_seq, out_seq = sequence
        grad_pre = (out_seq.astype(jnp.float32) * gelu_slope(pre_seq.astype(jnp.float32))).astype(jnp.bfloat16)
        rev_in = x_seq[::-1, ::-1]
        rev_grad = grad_pre[::-1, ::-1]
        grad_in = transpose_conv(grad_pre, weight) + transpose_conv(rev_grad, weight)[::-1, ::-1]
        carry = carry + weight_terms(x_seq, grad_pre) + weight_terms(rev_in, rev_grad)
        return carry, grad_in.astype(jnp.bfloat16)

    total, grad_input = lax.scan(per_sequence, jnp.zeros((C, K, C), jnp.float32), (inputs, pre_act, grad_out))
    return grad_input, total
```

```python
import functools

import jax
import jax.numpy as jnp
from jax import lax
from jax.experimental import pallas as pl
from jax.experimental.pallas import tpu as pltpu
from jax.sharding import PartitionSpec as P

AXES = ("dp", "pos")
F32 = jnp.float32
BF16 = jnp.bfloat16
NT = (((1,), (1,)), ((), ()))


def gelu_slope(values):
    cdf = 0.5 * (1.0 + lax.erf(values * 0.7071067811865476))
    return cdf + values * jnp.exp(-0.5 * values * values) * 0.3989422804014327


def grad_pre_of(pre_act, grad_out):
    return (grad_out.astype(F32) * gelu_slope(pre_act.astype(F32))).astype(BF16)


class Plan:
    def __init__(self, dp, pos):
        self.dp, self.pos, self.count = dp, pos, dp * pos
        assert self.count & (self.count - 1) == 0
        dp_bits = [pos << b for b in range(dp.bit_length() - 1)]
        pos_bits = [1 << b for b in range(pos.bit_length() - 1)]
        self.core = dp_bits[0]
        self.cross = (dp_bits[1], pos_bits[0])
        rest = dp_bits[2:] + pos_bits[1:]
        self.groups = [rest[i : i + 2] for i in range(0, len(rest), 2)]

    def mask(self, device, stage):
        if stage == "core":
            return self.core
        parity = 1 if device & self.core else 0
        return self.cross[parity if stage == "a" else 1 - parity]

    def swap(self, block, stage):
        route = [(d, d ^ self.mask(d, stage)) for d in range(self.count)]
        return lax.ppermute(block, AXES, route)

    def group_masks(self, group):
        masks = [0]
        for bit in group:
            masks += [m | bit for m in masks]
        return masks

    def shift(self, block, mask):
        return lax.ppermute(block, AXES, [(d, d ^ mask) for d in range(self.count)])

    def complement(self, block):
        return self.shift(block, self.count - 1)

    def source(self, position, device, rows):
        shift = rows.bit_length() - 1
        slot, low = position >> shift, position & (rows - 1)
        bit = self.count.bit_length() - 2
        flag = (slot >> bit) & 1
        owner = device ^ (flag * self.core)
        parity = jnp.where((owner & self.core) != 0, 1, 0)
        first = parity * self.cross[1] + (1 - parity) * self.cross[0]
        second = parity * self.cross[0] + (1 - parity) * self.cross[1]
        owner = owner ^ (((slot >> (bit - 1)) & 1) * first)
        owner = owner ^ (((slot >> (bit - 2)) & 1) * second)
        bit -= 3
        for group in self.groups:
            for mask in reversed(group):
                owner = owner ^ (((slot >> bit) & 1) * mask)
                bit -= 1
        return (owner << shift) + low


def anti_identity(size):
    row = lax.broadcasted_iota(jnp.int32, (size, size), 0)
    col = lax.broadcasted_iota(jnp.int32, (size, size), 1)
    return jnp.where(row + col == size - 1, 1.0, 0.0).astype(BF16)


def selection(plan, device, rows, width):
    position = lax.broadcasted_iota(jnp.int32, (width, 128), 0)
    lane = lax.broadcasted_iota(jnp.int32, (width, 128), 1)
    source = plan.source(position, device, rows)
    mirror = width - 1 - source
    def one_hot(index):
        return jnp.concatenate(
            [jnp.where(index == lane + start, 1.0, 0.0).astype(BF16) for start in range(0, width, 128)],
            axis=1,
        )
    return one_hot(source), one_hot(mirror)


def dot(left, right, dims=(((1,), (0,)), ((), ()))):
    return lax.dot_general(left, right, dims, preferred_element_type=F32)


def order_kernel(plan, rows, device_ref, values_ref, out_ref):
    width, count = values_ref.shape[1], values_ref.shape[0]
    direct, mirror = selection(plan, device_ref[0], rows, width)
    values = values_ref[...]
    out_ref[:, :count] = dot(direct, values, NT).astype(BF16)
    out_ref[:, count:] = dot(mirror, values, NT).astype(BF16)


def fill_windows(grads_ref, halo_ref, padded, windows, taps):
    seqs, length, width = grads_ref.shape
    half, reach = width // 2, (taps - 1) // 2
    flip = anti_identity(half)
    for b in range(seqs):
        block, edge = grads_ref[b], halo_ref[b]
        for strand in range(2):
            if strand == 0:
                inner, outer = block[:, :half].astype(F32), edge[:, :half].astype(F32)
            else:
                inner, outer = dot(block[:, half:], flip), dot(edge[:, half:], flip)
            padded[8 - reach : 8, :] = outer[:reach]
            padded[8 : 8 + length, :] = inner
            padded[8 + length : 8 + length + reach, :] = outer[reach:]
            base = (strand * seqs + b) * length
            for k in range(taps):
                start = 8 + reach - k if strand == 0 else 8 - reach + k
                windows[base : base + length, k * half : (k + 1) * half] = padded[
                    start : start + length, :
                ].astype(BF16)


def weight_kernel(taps, order_ref, grads_ref, halo_ref, out_ref, padded, windows):
    fill_windows(grads_ref, halo_ref, padded, windows, taps)
    out_ref[...] = dot(order_ref[...], windows[...]).astype(out_ref.dtype)


def input_kernel(plan, rows, taps, device_ref, grads_ref, halo_ref, own_ref, other_ref, out_ref, padded, windows):
    seqs, length, width = grads_ref.shape
    fill_windows(grads_ref, halo_ref, padded, windows, taps)
    direct, mirror = selection(plan, device_ref[0], rows, width)
    count = seqs * length
    total = jnp.zeros((count, width), F32)
    for strand, chosen in ((0, direct), (1, mirror)):
        part = windows[strand * count : (strand + 1) * count, :]
        sums = jnp.concatenate([dot(part, own_ref[...], NT), dot(part, other_ref[...], NT)], axis=1)
        high = sums.astype(BF16)
        low = (sums - high.astype(F32)).astype(BF16)
        total = total + dot(high, chosen) + dot(low, chosen)
    out_ref[...] = total.astype(BF16)


def tied_kernel(taps, near_ref, far_ref, out_ref):
    rows, half = near_ref.shape[0], near_ref.shape[1] // taps
    flip, turn = anti_identity(half), anti_identity(rows)
    for k in range(taps):
        far = far_ref[:, (taps - 1 - k) * half : (taps - k) * half]
        far = dot(turn, dot(far, flip).astype(BF16))
        near = near_ref[:, k * half : (k + 1) * half]
        out_ref[:, k * half : (k + 1) * half] = (near.astype(F32) + far).astype(BF16)


def finish_kernel(taps, *refs):
    part_refs, far_ref, out_ref = refs[:-2], refs[-2], refs[-1]
    rows, half = far_ref.shape[0], far_ref.shape[1] // taps
    flip, turn = anti_identity(half), anti_identity(rows)
    for k in range(taps):
        cut = slice(k * half, (k + 1) * half)
        out_ref[:, k, :half] = part_refs[0][:, cut]
        far = far_ref[:, (taps - 1 - k) * half : (taps - k) * half]
        out_ref[:, k, half:] = dot(turn, dot(far, flip).astype(BF16))


def call(kernel, shape, dtype, args, scalars=0, scratch=()):
    specs = [pl.BlockSpec(memory_space=pltpu.SMEM)] * scalars
    specs += [pl.BlockSpec(memory_space=pltpu.VMEM)] * (len(args) - scalars)
    return pl.pallas_call(
        kernel,
        out_shape=jax.ShapeDtypeStruct(shape, dtype),
        in_specs=specs,
        out_specs=pl.BlockSpec(memory_space=pltpu.VMEM),
        scratch_shapes=list(scratch),
    )(*args)


def edges(block, reach):
    count, where = lax.axis_size("pos"), lax.axis_index("pos")
    top, bottom = block[:, -reach:], block[:, :reach]
    if count == 2:
        got = lax.ppermute(jnp.where(where == 0, top, bottom), "pos", [(0, 1), (1, 0)])
        none = jnp.zeros_like(got)
        low, high = jnp.where(where == 0, none, got), jnp.where(where == 0, got, none)
    else:
        forward = [(i, i + 1) for i in range(count - 1)]
        low = lax.ppermute(top, "pos", forward)
        high = lax.ppermute(bottom, "pos", [(b, a) for a, b in forward])
    return jnp.concatenate([low, high], axis=1)


def on_device(plan, inputs, pre_act, grad_out, weight):
    seqs, length, width = inputs.shape
    rows, taps, _ = weight.shape
    half, reach = width // 2, (taps - 1) // 2
    depth = taps * half
    device = (lax.axis_index("dp") * plan.pos + lax.axis_index("pos")).astype(jnp.int32).reshape(1)
    scratch = (
        pltpu.VMEM((length + 16, half), F32),
        pltpu.VMEM((2 * seqs * length, depth), BF16),
    )

    ends = jnp.concatenate(
        [
            grad_pre_of(pre_act[:, :reach], grad_out[:, :reach]),
            grad_pre_of(pre_act[:, -reach:], grad_out[:, -reach:]),
        ],
        axis=1,
    )
    halo = edges(ends, reach)
    far_weight = plan.complement(weight[:, :, half:].reshape(rows, depth))
    near_weight = weight[:, :, :half].reshape(rows, depth)

    grads = grad_pre_of(pre_act, grad_out)
    ordered = call(
        functools.partial(order_kernel, plan, rows),
        (width, 2 * seqs * length), BF16,
        (device, inputs.reshape(seqs * length, width)), scalars=1,
    )

    tied = call(functools.partial(tied_kernel, taps), (rows, depth), BF16, (near_weight, far_weight))

    weights_of = functools.partial(weight_kernel, taps)
    sent = call(weights_of, (half, depth), BF16, (ordered[half:], grads, halo), scratch=scratch)
    received = plan.swap(sent, "core")
    kept = call(weights_of, (half, depth), F32, (ordered[:half], grads, halo), scratch=scratch)
    for stage in ("a", "b"):
        middle = kept.shape[0] // 2
        sent = (kept[middle:] + received[middle:].astype(F32)).astype(BF16)
        kept = kept[:middle] + received[:middle].astype(F32)
        received = plan.swap(sent, stage)
    kept = kept + received.astype(F32)
    for group in plan.groups:
        masks = plan.group_masks(group)
        size = kept.shape[0] // len(masks)
        pieces = [
            plan.shift(kept[j * size : (j + 1) * size].astype(BF16), masks[j]).astype(F32)
            for j in range(1, len(masks))
        ]
        kept = functools.reduce(jnp.add, pieces, kept[:size])
    far_sum = plan.complement(kept.astype(BF16))
    grad_weight = call(functools.partial(finish_kernel, taps), (rows, taps, width), F32, (kept, far_sum))

    gathered = tied
    for group in reversed(plan.groups):
        gathered = jnp.concatenate(
            [gathered] + [plan.shift(gathered, m) for m in plan.group_masks(group)[1:]], axis=0
        )
    for stage in ("b", "a"):
        gathered = jnp.concatenate([gathered, plan.swap(gathered, stage)], axis=0)
    other = plan.swap(gathered, "core")
    grad_input = call(
        functools.partial(input_kernel, plan, rows, taps),
        (seqs * length, width), BF16,
        (device, grads, halo, gathered, other), scalars=1, scratch=scratch,
    ).reshape(seqs, length, width)
    return grad_input, grad_weight


def solution(mesh):
    plan = Plan(mesh.shape["dp"], mesh.shape["pos"])
    placed = (
        P("dp", "pos", None),
        P("dp", "pos", None),
        P("dp", "pos", None),
        P(("dp", "pos"), None, None),
    )
    return jax.shard_map(
        functools.partial(on_device, plan),
        mesh=mesh,
        in_specs=placed,
        out_specs=(P("dp", "pos", None), P(("dp", "pos"), None, None)),
        check_vma=False,
    )
```

```python
import functools
import math

import jax
import jax.numpy as jnp
from jax import lax
from jax.experimental import pallas as pl
from jax.experimental.pallas import tpu as pltpu
from jax.sharding import PartitionSpec as P

AXES = ("dp", "pos")
F32 = jnp.float32
BF16 = jnp.bfloat16
NT = (((1,), (1,)), ((), ()))


def gelu_slope(values):
    cdf = 0.5 * (1.0 + lax.erf(values * 0.7071067811865476))
    return cdf + values * jnp.exp(-0.5 * values * values) * 0.3989422804014327


def grad_pre_of(pre_act, grad_out):
    return (grad_out.astype(F32) * gelu_slope(pre_act.astype(F32))).astype(BF16)


class Plan:
    def __init__(self, dp, pos):
        self.dp, self.pos, self.count = dp, pos, dp * pos
        assert self.count & (self.count - 1) == 0
        dp_bits = [pos << b for b in range(dp.bit_length() - 1)]
        pos_bits = [1 << b for b in range(pos.bit_length() - 1)]
        self.core = dp_bits[0]
        self.cross = (dp_bits[1], pos_bits[0])
        rest = dp_bits[2:] + pos_bits[1:]
        self.groups = [rest[i : i + 2] for i in range(0, len(rest), 2)]

    def mask(self, device, stage):
        if stage == "core":
            return self.core
        parity = 1 if device & self.core else 0
        return self.cross[parity if stage == "a" else 1 - parity]

    def swap(self, block, stage):
        route = [(d, d ^ self.mask(d, stage)) for d in range(self.count)]
        return lax.ppermute(block, AXES, route)

    def group_masks(self, group):
        masks = [0]
        for bit in group:
            masks += [m | bit for m in masks]
        return masks

    def shift(self, block, mask):
        return lax.ppermute(block, AXES, [(d, d ^ mask) for d in range(self.count)])

    def complement(self, block):
        return self.shift(block, self.count - 1)

    def source(self, position, device, rows):
        shift = rows.bit_length() - 1
        slot, low = position >> shift, position & (rows - 1)
        bit = self.count.bit_length() - 2
        flag = (slot >> bit) & 1
        owner = device ^ (flag * self.core)
        parity = jnp.where((owner & self.core) != 0, 1, 0)
        first = parity * self.cross[1] + (1 - parity) * self.cross[0]
        second = parity * self.cross[0] + (1 - parity) * self.cross[1]
        owner = owner ^ (((slot >> (bit - 1)) & 1) * first)
        owner = owner ^ (((slot >> (bit - 2)) & 1) * second)
        bit -= 3
        for group in self.groups:
            for mask in reversed(group):
                owner = owner ^ (((slot >> bit) & 1) * mask)
                bit -= 1
        return (owner << shift) + low


def anti_identity(size):
    row = lax.broadcasted_iota(jnp.int32, (size, size), 0)
    col = lax.broadcasted_iota(jnp.int32, (size, size), 1)
    return jnp.where(row + col == size - 1, 1.0, 0.0).astype(BF16)


def selection(plan, device, rows, width):
    position = lax.broadcasted_iota(jnp.int32, (width, 128), 0)
    lane = lax.broadcasted_iota(jnp.int32, (width, 128), 1)
    source = plan.source(position, device, rows)

    def one_hot(index):
        return jnp.concatenate(
            [jnp.where(index == lane + start, 1.0, 0.0).astype(BF16) for start in range(0, width, 128)],
            axis=1,
        )

    return one_hot(source), one_hot(width - 1 - source)


def dot(left, right, dims=(((1,), (0,)), ((), ()))):
    return lax.dot_general(left, right, dims, preferred_element_type=F32)


EDGE = 8


def window_start(strand, tap, taps):
    reach = (taps - 1) // 2
    return EDGE + reach - tap if strand == 0 else EDGE - reach + tap


def prepare_kernel(
    plan, rows, taps, device_ref, values_ref, pre_ref, out_grad_ref,
    kept_ref, sent_ref, direct_ref, mirror_ref, padded_ref, windows_ref,
):
    seqs, length, width = pre_ref.shape
    half, count = width // 2, seqs * length
    direct_ref[...], mirror_ref[...] = selection(plan, device_ref[0], rows, width)
    values = values_ref[...]
    for out_ref, cut in ((kept_ref, slice(0, half)), (sent_ref, slice(half, width))):
        out_ref[:, :count] = dot(direct_ref[cut, :], values, NT).astype(BF16)
        out_ref[:, count:] = dot(mirror_ref[cut, :], values, NT).astype(BF16)
    flip = anti_identity(half)
    for b in range(seqs):
        grads = grad_pre_of(pre_ref[b], out_grad_ref[b])
        for strand in range(2):
            place = strand * seqs + b
            inner = grads[:, :half].astype(F32) if strand == 0 else dot(grads[:, half:], flip)
            padded_ref[place, :EDGE, :] = jnp.zeros((EDGE, half), F32)
            padded_ref[place, EDGE + length :, :] = jnp.zeros((EDGE, half), F32)
            padded_ref[place, EDGE : EDGE + length, :] = inner
            for tap in range(taps):
                start = window_start(strand, tap, taps)
                windows_ref[place * length : (place + 1) * length, tap * half : (tap + 1) * half] = (
                    padded_ref[place, start : start + length, :].astype(BF16)
                )


def first_sums_kernel(taps, order_ref, halo_ref, _, __, out_ref, padded_ref, windows_ref):
    seqs, both, width = halo_ref.shape
    half, reach = width // 2, both // 2
    length = padded_ref.shape[1] - 2 * EDGE
    strip = 16
    flip = anti_identity(half)
    for b in range(seqs):
        for strand in range(2):
            place = strand * seqs + b
            edge = halo_ref[b]
            outer = edge[:, :half].astype(F32) if strand == 0 else dot(edge[:, half:], flip)
            padded_ref[place, EDGE - reach : EDGE, :] = outer[:reach]
            padded_ref[place, EDGE + length : EDGE + length + reach, :] = outer[reach:]
            for tap in range(taps):
                start = window_start(strand, tap, taps)
                for begin in (0, length - strip):
                    windows_ref[
                        place * length + begin : place * length + begin + strip, tap * half : (tap + 1) * half
                    ] = padded_ref[place, start + begin : start + begin + strip, :].astype(BF16)
    out_ref[...] = dot(order_ref[...], windows_ref[...]).astype(out_ref.dtype)


def sums_kernel(order_ref, windows_ref, out_ref):
    out_ref[...] = dot(order_ref[...], windows_ref[...])


def placed_sums(windows_ref, weights_ref, direct, mirror):
    count = windows_ref.shape[0] // 2
    total = None
    for strand, chosen in ((0, direct), (1, mirror)):
        sums = dot(windows_ref[strand * count : (strand + 1) * count, :], weights_ref[...], NT)
        high = sums.astype(BF16)
        low = (sums - high.astype(F32)).astype(BF16)
        both = dot(high, chosen) + dot(low, chosen)
        total = both if total is None else total + both
    return total


def own_input_kernel(direct_ref, mirror_ref, windows_ref, weights_ref, out_ref):
    half = weights_ref.shape[0]
    out_ref[...] = placed_sums(windows_ref, weights_ref, direct_ref[:half, :], mirror_ref[:half, :])


def other_input_kernel(direct_ref, mirror_ref, windows_ref, weights_ref, first_ref, out_ref):
    half = weights_ref.shape[0]
    total = placed_sums(windows_ref, weights_ref, direct_ref[half:, :], mirror_ref[half:, :])
    out_ref[...] = (first_ref[...] + total).astype(BF16)


def reversed_taps(blocks):
    rows, half = blocks[0].shape
    far = dot(jnp.concatenate(blocks, axis=0), anti_identity(half)).astype(BF16)
    far = dot(anti_identity(len(blocks) * rows), far)
    return [far[k * rows : (k + 1) * rows] for k in range(len(blocks))]


def tied_kernel(weight_ref, far_ref, out_ref):
    taps, _, half = far_ref.shape
    far = reversed_taps([far_ref[k] for k in range(taps)])
    for k in range(taps):
        near = weight_ref[k, :, :half].astype(F32)
        out_ref[:, k * half : (k + 1) * half] = (near + far[k]).astype(BF16)


def finish_kernel(near_ref, far_ref, out_ref):
    taps, _, width = out_ref.shape
    half = width // 2
    cuts = [slice(k * half, (k + 1) * half) for k in range(taps)]
    far = reversed_taps([far_ref[:, cut] for cut in cuts])
    for k, cut in enumerate(cuts):
        out_ref[k, :, :half] = near_ref[:, cut]
        out_ref[k, :, half:] = far[k]


ON_CHIP = pltpu.VMEM


def call(kernel, outs, args, scalars=0, flops=0, aliases=None, given=(), limit=24):
    held = pl.BlockSpec(memory_space=ON_CHIP)
    args = [pltpu.with_memory_space_constraint(a, ON_CHIP) if i in given else a for i, a in enumerate(args)]
    result = pl.pallas_call(
        kernel,
        out_shape=[(ON_CHIP if stays else jax.ShapeDtypeStruct)(shape, dtype) for shape, dtype, stays in outs],
        in_specs=[pl.BlockSpec(memory_space=pltpu.SMEM)] * scalars + [held] * (len(args) - scalars),
        out_specs=[held] * len(outs),
        input_output_aliases=aliases or {},
        cost_estimate=pl.CostEstimate(
            flops=flops,
            transcendentals=0,
            bytes_accessed=sum(math.prod(out[0]) * jnp.dtype(out[1]).itemsize for out in outs)
            + sum(a.size * a.dtype.itemsize for a in args[scalars:]),
        ),
        compiler_params=pltpu.CompilerParams(vmem_limit_bytes=limit << 20),
    )(*args)
    return result if len(outs) > 1 else result[0]


def edges(block, reach):
    count, where = lax.axis_size("pos"), lax.axis_index("pos")
    top, bottom = block[:, -reach:], block[:, :reach]
    if count == 2:
        got = lax.ppermute(jnp.where(where == 0, top, bottom), "pos", [(0, 1), (1, 0)])
        none = jnp.zeros_like(got)
        low, high = jnp.where(where == 0, none, got), jnp.where(where == 0, got, none)
    else:
        forward = [(i, i + 1) for i in range(count - 1)]
        low = lax.ppermute(top, "pos", forward)
        high = lax.ppermute(bottom, "pos", [(b, a) for a, b in forward])
    return jnp.concatenate([low, high], axis=1)


def on_device(plan, inputs, pre_act, grad_out, weight):
    seqs, length, width = inputs.shape
    rows, taps, _ = weight.shape
    half, reach = width // 2, (taps - 1) // 2
    depth, count = taps * half, seqs * length
    work = 4 * count * depth * half
    device = (lax.axis_index("dp") * plan.pos + lax.axis_index("pos")).astype(jnp.int32).reshape(1)

    by_tap = jnp.transpose(weight, (1, 0, 2))
    far_weight = plan.complement(by_tap[:, :, half:])
    ends = jnp.concatenate(
        [
            grad_pre_of(pre_act[:, :reach], grad_out[:, :reach]),
            grad_pre_of(pre_act[:, -reach:], grad_out[:, -reach:]),
        ],
        axis=1,
    )
    halo = edges(ends, reach)

    kept_order, sent_order, direct, mirror, padded, windows = call(
        functools.partial(prepare_kernel, plan, rows, taps),
        [((half, 2 * count), BF16, True)] * 2
        + [((width, width), BF16, True)] * 2
        + [((2 * seqs, length + 2 * EDGE, half), F32, True), ((2 * count, depth), BF16, True)],
        (device, inputs.reshape(count, width), pre_act, grad_out),
        scalars=1, flops=4 * count * width * width,
    )
    tied = call(
        tied_kernel, [((rows, depth), BF16, True)], (by_tap, far_weight),
        flops=2 * rows * depth * half, given=(1,),
    )
    sent, _, windows = call(
        functools.partial(first_sums_kernel, taps),
        [((half, depth), BF16, True), (padded.shape, F32, True), (windows.shape, BF16, True)],
        (sent_order, halo, padded, windows), flops=work, aliases={2: 1, 3: 2}, given=(0, 1, 2, 3),
    )
    received = plan.swap(sent, "core")
    kept = call(sums_kernel, [((half, depth), F32, True)], (kept_order, windows), flops=work, given=(0, 1))
    for stage in ("a", "b"):
        middle = kept.shape[0] // 2
        sent = (kept[middle:] + received[middle:].astype(F32)).astype(BF16)
        kept = kept[:middle] + received[:middle].astype(F32)
        received = plan.swap(sent, stage)
    kept = kept + received.astype(F32)
    for group in plan.groups:
        masks = plan.group_masks(group)
        size = kept.shape[0] // len(masks)
        pieces = [
            plan.shift(kept[j * size : (j + 1) * size].astype(BF16), masks[j]).astype(F32)
            for j in range(1, len(masks))
        ]
        kept = functools.reduce(jnp.add, pieces, kept[:size])
    far_sum = plan.complement(kept.astype(BF16))
    grad_weight = jnp.transpose(
        call(
            finish_kernel, [((taps, rows, width), F32, False)], (kept, far_sum),
            flops=2 * rows * depth * half, given=(0, 1),
        ),
        (1, 0, 2),
    )

    gathered = tied
    for group in reversed(plan.groups):
        gathered = jnp.concatenate(
            [gathered] + [plan.shift(gathered, m) for m in plan.group_masks(group)[1:]], axis=0
        )
    for stage in ("b", "a"):
        gathered = jnp.concatenate([gathered, plan.swap(gathered, stage)], axis=0)
    other = plan.swap(gathered, "core")
    first = call(
        own_input_kernel, [((count, width), F32, True)], (direct, mirror, windows, gathered),
        flops=work, given=(0, 1, 2, 3),
    )
    grad_input = call(
        other_input_kernel, [((count, width), BF16, False)], (direct, mirror, windows, other, first),
        flops=work, given=(0, 1, 2, 3, 4),
    ).reshape(seqs, length, width)
    return grad_input, grad_weight


def solution(mesh):
    plan = Plan(mesh.shape["dp"], mesh.shape["pos"])
    placed = (
        P("dp", "pos", None),
        P("dp", "pos", None),
        P("dp", "pos", None),
        P(("dp", "pos"), None, None),
    )
    return jax.shard_map(
        functools.partial(on_device, plan),
        mesh=mesh,
        in_specs=placed,
        out_specs=(P("dp", "pos", None), P(("dp", "pos"), None, None)),
        check_vma=False,
    )
```

```python
import functools
import math

import jax
import jax.numpy as jnp
from jax import lax
from jax.experimental import pallas as pl
from jax.experimental.pallas import tpu as pltpu
from jax.sharding import PartitionSpec as P


AXES = ("dp", "pos")
F32 = jnp.float32
BF16 = jnp.bfloat16
NT = (((1,), (1,)), ((), ()))


def gelu_slope(values):
    cdf = 0.5 * (1.0 + lax.erf(values * 0.7071067811865476))
    return cdf + values * jnp.exp(-0.5 * values * values) * 0.3989422804014327


def grad_pre_of(pre_act, grad_out):
    return (grad_out.astype(F32) * gelu_slope(pre_act.astype(F32))).astype(BF16)


class Plan:
    def __init__(self, dp, pos):
        self.dp, self.pos, self.count = dp, pos, dp * pos
        assert self.count & (self.count - 1) == 0
        dp_bits = [pos << b for b in range(dp.bit_length() - 1)]
        pos_bits = [1 << b for b in range(pos.bit_length() - 1)]
        self.core = dp_bits[0]
        self.cross = (dp_bits[1], pos_bits[0])
        rest = (dp_bits[2:] + pos_bits[1:])[:-1]
        self.groups = [rest[i : i + 2] for i in range(0, len(rest), 2)]

    def mask(self, device, stage):
        if stage == "core":
            return self.core
        parity = 1 if device & self.core else 0
        return self.cross[parity if stage == "a" else 1 - parity]

    def swap(self, block, stage):
        route = [(d, d ^ self.mask(d, stage)) for d in range(self.count)]
        return lax.ppermute(block, AXES, route)

    def group_masks(self, group):
        masks = [0]
        for bit in group:
            masks += [m | bit for m in masks]
        return masks

    def shift(self, block, mask):
        return lax.ppermute(block, AXES, [(d, d ^ mask) for d in range(self.count)])

    def complement(self, block):
        return self.shift(block, self.count - 1)

    def source(self, position, device, rows):
        shift = rows.bit_length() - 1
        slot, low = position >> shift, position & (rows - 1)
        bit = self.count.bit_length() - 2
        flag = (slot >> bit) & 1
        owner = device ^ (flag * self.core)
        parity = jnp.where((owner & self.core) != 0, 1, 0)
        first = parity * self.cross[1] + (1 - parity) * self.cross[0]
        second = parity * self.cross[0] + (1 - parity) * self.cross[1]
        owner = owner ^ (((slot >> (bit - 1)) & 1) * first)
        owner = owner ^ (((slot >> (bit - 2)) & 1) * second)
        bit -= 3
        for group in self.groups:
            for mask in reversed(group):
                owner = owner ^ (((slot >> bit) & 1) * mask)
                bit -= 1
        owner = owner ^ ((slot & 1) * (self.count - 1))
        return (owner << shift) + low


def anti_identity(size):
    row = lax.broadcasted_iota(jnp.int32, (size, size), 0)
    col = lax.broadcasted_iota(jnp.int32, (size, size), 1)
    return jnp.where(row + col == size - 1, 1.0, 0.0).astype(BF16)


def selection(plan, device, rows, width):
    position = lax.broadcasted_iota(jnp.int32, (width, 128), 0)
    lane = lax.broadcasted_iota(jnp.int32, (width, 128), 1)
    source = plan.source(position, device, rows)

    def one_hot(index):
        return jnp.concatenate(
            [jnp.where(index == lane + start, 1.0, 0.0).astype(BF16) for start in range(0, width, 128)],
            axis=1,
        )

    return one_hot(source), one_hot(width - 1 - source)


def dot(left, right, dims=(((1,), (0,)), ((), ()))):
    return lax.dot_general(left, right, dims, preferred_element_type=F32)


EDGE = 8


def window_start(strand, tap, taps):
    reach = (taps - 1) // 2
    return EDGE + reach - tap if strand == 0 else EDGE - reach + tap


def prepare_kernel(
    plan, rows, taps, device_ref, values_hbm, pre_hbm, out_grad_hbm,
    kept_ref, sent_ref, direct_ref, mirror_ref, padded_ref, windows_ref,
    values_ref, pre_ref, out_grad_ref, arrived,
):
    seqs, length, width = pre_ref.shape
    half, count = width // 2, seqs * length
    pairs = ((pre_hbm, pre_ref), (out_grad_hbm, out_grad_ref), (values_hbm, values_ref))
    copies = [pltpu.make_async_copy(far, near, arrived.at[i]) for i, (far, near) in enumerate(pairs)]
    for copy in copies:
        copy.start()
    direct_ref[...], mirror_ref[...] = selection(plan, device_ref[0], rows, width)
    for copy in copies:
        copy.wait()
    values = values_ref[...]
    for out_ref, cut in ((kept_ref, slice(0, half)), (sent_ref, slice(half, width))):
        out_ref[:, :count] = dot(direct_ref[cut, :], values, NT).astype(BF16)
        out_ref[:, count:] = dot(mirror_ref[cut, :], values, NT).astype(BF16)
    flip = anti_identity(half)
    for b in range(seqs):
        grads = grad_pre_of(pre_ref[b], out_grad_ref[b])
        for strand in range(2):
            place = strand * seqs + b
            inner = grads[:, :half].astype(F32) if strand == 0 else dot(grads[:, half:], flip)
            padded_ref[place, :EDGE, :] = jnp.zeros((EDGE, half), F32)
            padded_ref[place, EDGE + length :, :] = jnp.zeros((EDGE, half), F32)
            padded_ref[place, EDGE : EDGE + length, :] = inner
            for tap in range(taps):
                start = window_start(strand, tap, taps)
                windows_ref[place * length : (place + 1) * length, tap * half : (tap + 1) * half] = (
                    padded_ref[place, start : start + length, :].astype(BF16)
                )


def first_sums_kernel(taps, order_ref, halo_ref, _, __, out_ref, padded_ref, windows_ref):
    seqs, both, width = halo_ref.shape
    half, reach = width // 2, both // 2
    length = padded_ref.shape[1] - 2 * EDGE
    strip = 16
    flip = anti_identity(half)
    for b in range(seqs):
        for strand in range(2):
            place = strand * seqs + b
            edge = halo_ref[b]
            outer = edge[:, :half].astype(F32) if strand == 0 else dot(edge[:, half:], flip)
            padded_ref[place, EDGE - reach : EDGE, :] = outer[:reach]
            padded_ref[place, EDGE + length : EDGE + length + reach, :] = outer[reach:]
            for tap in range(taps):
                start = window_start(strand, tap, taps)
                for begin in (0, length - strip):
                    windows_ref[
                        place * length + begin : place * length + begin + strip, tap * half : (tap + 1) * half
                    ] = padded_ref[place, start + begin : start + begin + strip, :].astype(BF16)
    out_ref[...] = dot(order_ref[...], windows_ref[...]).astype(out_ref.dtype)


def sums_kernel(order_ref, windows_ref, out_ref):
    out_ref[...] = dot(order_ref[...], windows_ref[...])


def placed_sums(windows_ref, weights_ref, direct, mirror):
    count = windows_ref.shape[0] // 2
    total = None
    for strand, chosen in ((0, direct), (1, mirror)):
        sums = dot(windows_ref[strand * count : (strand + 1) * count, :], weights_ref[...], NT)
        high = sums.astype(BF16)
        low = (sums - high.astype(F32)).astype(BF16)
        both = dot(high, chosen) + dot(low, chosen)
        total = both if total is None else total + both
    return total


def own_input_kernel(direct_ref, mirror_ref, windows_ref, weights_ref, out_ref):
    half = weights_ref.shape[0]
    out_ref[...] = placed_sums(windows_ref, weights_ref, direct_ref[:half, :], mirror_ref[:half, :])


def other_input_kernel(direct_ref, mirror_ref, windows_ref, weights_ref, first_ref, out_ref):
    half = weights_ref.shape[0]
    total = placed_sums(windows_ref, weights_ref, direct_ref[half:, :], mirror_ref[half:, :])
    out_ref[...] = (first_ref[...] + total).astype(BF16)


def reversed_taps(blocks):
    rows, half = blocks[0].shape
    far = dot(jnp.concatenate(blocks, axis=0), anti_identity(half)).astype(BF16)
    far = dot(anti_identity(len(blocks) * rows), far)
    return [far[k * rows : (k + 1) * rows] for k in range(len(blocks))]


def tied_kernel(own_ref, far_ref, out_ref):
    taps, rows, width = far_ref.shape
    half = width // 2
    for place, near_ref, other_ref in ((0, own_ref, far_ref), (1, far_ref, own_ref)):
        other = reversed_taps([other_ref[k, :, half:] for k in range(taps)])
        for k in range(taps):
            out_ref[place * rows : (place + 1) * rows, k * half : (k + 1) * half] = (
                near_ref[k, :, :half].astype(F32) + other[k]
            ).astype(BF16)


def finish_kernel(own_ref, got_ref, out_ref):
    taps, rows, width = out_ref.shape
    half = width // 2
    cuts = [slice(k * half, (k + 1) * half) for k in range(taps)]
    far = own_ref[rows:, :] + got_ref[:rows, :].astype(F32)
    high = far.astype(BF16)
    low = (far - high.astype(F32)).astype(BF16)
    high, low = (reversed_taps([part[:, cut] for cut in cuts]) for part in (high, low))
    near = own_ref[:rows, :] + got_ref[rows:, :].astype(F32)
    for k, cut in enumerate(cuts):
        out_ref[k, :, :half] = near[:, cut]
        out_ref[k, :, half:] = high[k] + low[k]


ON_CHIP = pltpu.VMEM


def call(kernel, outs, args, scalars=0, flops=0, aliases=None, given=(), limit=24, off_chip=(), scratch=()):
    held = pl.BlockSpec(memory_space=ON_CHIP)
    spaces = {i: ON_CHIP for i in given} | {i: pltpu.HBM for i in off_chip}
    args = [pltpu.with_memory_space_constraint(a, spaces[i]) if i in spaces else a for i, a in enumerate(args)]
    result = pl.pallas_call(
        kernel,
        out_shape=[(ON_CHIP if stays else jax.ShapeDtypeStruct)(shape, dtype) for shape, dtype, stays in outs],
        in_specs=[pl.BlockSpec(memory_space=pltpu.SMEM)] * scalars
        + [pl.BlockSpec(memory_space=pltpu.HBM) if i in off_chip else held for i in range(scalars, len(args))],
        scratch_shapes=list(scratch),
        out_specs=[held] * len(outs),
        input_output_aliases=aliases or {},
        cost_estimate=pl.CostEstimate(
            flops=flops,
            transcendentals=0,
            bytes_accessed=sum(math.prod(out[0]) * jnp.dtype(out[1]).itemsize for out in outs)
            + sum(a.size * a.dtype.itemsize for a in args[scalars:]),
        ),
        compiler_params=pltpu.CompilerParams(vmem_limit_bytes=limit << 20),
    )(*args)
    return result if len(outs) > 1 else result[0]


def edges(block, reach):
    count, where = lax.axis_size("pos"), lax.axis_index("pos")
    top, bottom = block[:, -reach:], block[:, :reach]
    if count == 2:
        got = lax.ppermute(jnp.where(where == 0, top, bottom), "pos", [(0, 1), (1, 0)])
        none = jnp.zeros_like(got)
        low, high = jnp.where(where == 0, none, got), jnp.where(where == 0, got, none)
    else:
        forward = [(i, i + 1) for i in range(count - 1)]
        low = lax.ppermute(top, "pos", forward)
        high = lax.ppermute(bottom, "pos", [(b, a) for a, b in forward])
    return jnp.concatenate([low, high], axis=1)


def on_device(plan, inputs, pre_act, grad_out, weight):
    return both_gradients(plan, inputs, pre_act, grad_out, weight)


def both_gradients(plan, inputs, pre_act, grad_out, weight):
    seqs, length, width = inputs.shape
    rows, taps, _ = weight.shape
    half, reach = width // 2, (taps - 1) // 2
    depth, count = taps * half, seqs * length
    work = 4 * count * depth * half
    device = (lax.axis_index("dp") * plan.pos + lax.axis_index("pos")).astype(jnp.int32).reshape(1)

    by_tap = jnp.transpose(weight, (1, 0, 2))
    far_weight = plan.complement(by_tap)
    ends = jnp.concatenate(
        [grad_pre_of(pre_act[:, :reach], grad_out[:, :reach]), grad_pre_of(pre_act[:, -reach:], grad_out[:, -reach:])],
        axis=1,
    )
    halo = edges(ends, reach)
    kept_order, sent_order, direct, mirror, padded, windows = call(
        functools.partial(prepare_kernel, plan, rows, taps),
        [((half, 2 * count), BF16, True)] * 2
        + [((width, width), BF16, True)] * 2
        + [((2 * seqs, length + 2 * EDGE, half), F32, True), ((2 * count, depth), BF16, True)],
        (device, inputs.reshape(count, width), pre_act, grad_out),
        scalars=1, flops=4 * count * width * width, off_chip=(1, 2, 3),
        scratch=(
            pltpu.VMEM((count, width), BF16), pltpu.VMEM((seqs, length, width), BF16),
            pltpu.VMEM((seqs, length, width), BF16), pltpu.SemaphoreType.DMA((3,)),
        ),
    )
    sent, _, windows = call(
        functools.partial(first_sums_kernel, taps),
        [((half, depth), BF16, True), (padded.shape, F32, True), (windows.shape, BF16, True)],
        (sent_order, halo, padded, windows), flops=work, aliases={2: 1, 3: 2}, given=(0, 1, 2, 3),
    )
    received = plan.swap(sent, "core")
    kept = call(sums_kernel, [((half, depth), F32, True)], (kept_order, windows), flops=work, given=(0, 1))
    for stage in ("a", "b"):
        middle = kept.shape[0] // 2
        sent = (kept[middle:] + received[middle:].astype(F32)).astype(BF16)
        kept = kept[:middle] + received[:middle].astype(F32)
        received = plan.swap(sent, stage)
    for place, group in enumerate(plan.groups):
        if place == 0:
            kept = kept + received.astype(F32)
        masks = plan.group_masks(group)
        size = kept.shape[0] // len(masks)
        pieces = [
            plan.shift(kept[j * size : (j + 1) * size].astype(BF16), masks[j]).astype(F32)
            for j in range(1, len(masks))
        ]
        kept = functools.reduce(jnp.add, pieces, kept[:size])
    got = plan.complement(kept.astype(BF16))
    grad_weight = jnp.transpose(
        call(
            finish_kernel, [((taps, rows, width), F32, False)], (kept, got),
            flops=4 * rows * depth * half, given=(0, 1),
        ),
        (1, 0, 2),
    )

    gathered = call(
        tied_kernel, [((2 * rows, depth), BF16, True)], (by_tap, far_weight),
        flops=4 * rows * depth * half, given=(1,),
    )
    for place, group in reversed(list(enumerate(plan.groups))):
        gathered = jnp.concatenate([gathered] + [plan.shift(gathered, m) for m in plan.group_masks(group)[1:]], axis=0)
    for stage in ("b", "a"):
        gathered = jnp.concatenate([gathered, plan.swap(gathered, stage)], axis=0)
    other = plan.swap(gathered, "core")
    first = call(
        own_input_kernel, [((count, width), F32, True)], (direct, mirror, windows, gathered),
        flops=work, given=(0, 1, 2, 3),
    )
    grad_input = call(
        other_input_kernel, [((count, width), BF16, False)], (direct, mirror, windows, other, first),
        flops=work, given=(0, 1, 2, 3, 4),
    ).reshape(seqs, length, width)
    return grad_input, grad_weight


def solution(mesh):
    plan = Plan(mesh.shape["dp"], mesh.shape["pos"])
    placed = (
        P("dp", "pos", None),
        P("dp", "pos", None),
        P("dp", "pos", None),
        P(("dp", "pos"), None, None),
    )
    return jax.shard_map(
        functools.partial(on_device, plan),
        mesh=mesh,
        in_specs=placed,
        out_specs=(P("dp", "pos", None), P(("dp", "pos"), None, None)),
        check_vma=False,
    )
```

```python
import functools
import math

import jax
import jax.numpy as jnp
from jax import lax
from jax.experimental import pallas as pl
from jax.experimental.pallas import tpu as pltpu
from jax.sharding import PartitionSpec as P


AXES = ("dp", "pos")
F32 = jnp.float32
BF16 = jnp.bfloat16
NT = (((1,), (1,)), ((), ()))


def gelu_slope(values):
    cdf = 0.5 * (1.0 + lax.erf(values * 0.7071067811865476))
    return cdf + values * jnp.exp(-0.5 * values * values) * 0.3989422804014327


def grad_pre_of(pre_act, grad_out):
    return (grad_out.astype(F32) * gelu_slope(pre_act.astype(F32))).astype(BF16)


class Plan:
    def __init__(self, dp, pos):
        self.dp, self.pos, self.count = dp, pos, dp * pos
        assert self.count & (self.count - 1) == 0
        dp_bits = [pos << b for b in range(dp.bit_length() - 1)]
        pos_bits = [1 << b for b in range(pos.bit_length() - 1)]
        self.core = dp_bits[0]
        self.cross = (dp_bits[1], pos_bits[0])
        rest = (dp_bits[2:] + pos_bits[1:])[:-1]
        self.groups = [rest[i : i + 2] for i in range(0, len(rest), 2)]

    def mask(self, device, stage):
        if stage == "core":
            return self.core
        parity = 1 if device & self.core else 0
        return self.cross[parity if stage == "a" else 1 - parity]

    def swap(self, block, stage):
        route = [(d, d ^ self.mask(d, stage)) for d in range(self.count)]
        return lax.ppermute(block, AXES, route)

    def group_masks(self, group):
        masks = [0]
        for bit in group:
            masks += [m | bit for m in masks]
        return masks

    def shift(self, block, mask):
        return lax.ppermute(block, AXES, [(d, d ^ mask) for d in range(self.count)])

    def complement(self, block):
        return self.shift(block, self.count - 1)

    def source(self, position, device, rows):
        shift = rows.bit_length() - 1
        slot, low = position >> shift, position & (rows - 1)
        bit = self.count.bit_length() - 2
        flag = (slot >> bit) & 1
        owner = device ^ (flag * self.core)
        parity = jnp.where((owner & self.core) != 0, 1, 0)
        first = parity * self.cross[1] + (1 - parity) * self.cross[0]
        second = parity * self.cross[0] + (1 - parity) * self.cross[1]
        owner = owner ^ (((slot >> (bit - 1)) & 1) * first)
        owner = owner ^ (((slot >> (bit - 2)) & 1) * second)
        bit -= 3
        for group in self.groups:
            for mask in reversed(group):
                owner = owner ^ (((slot >> bit) & 1) * mask)
                bit -= 1
        owner = owner ^ ((slot & 1) * (self.count - 1))
        return (owner << shift) + low


def anti_identity(size):
    row = lax.broadcasted_iota(jnp.int32, (size, size), 0)
    col = lax.broadcasted_iota(jnp.int32, (size, size), 1)
    return jnp.where(row + col == size - 1, 1.0, 0.0).astype(BF16)


def selection(plan, device, rows, width):
    position = lax.broadcasted_iota(jnp.int32, (width, 128), 0)
    lane = lax.broadcasted_iota(jnp.int32, (width, 128), 1)
    source = plan.source(position, device, rows)

    def one_hot(index):
        return jnp.concatenate(
            [jnp.where(index == lane + start, 1.0, 0.0).astype(BF16) for start in range(0, width, 128)],
            axis=1,
        )

    return one_hot(source), one_hot(width - 1 - source)


def dot(left, right, dims=(((1,), (0,)), ((), ()))):
    return lax.dot_general(left, right, dims, preferred_element_type=F32)


EDGE = 8


def window_start(strand, tap, taps):
    reach = (taps - 1) // 2
    return EDGE + reach - tap if strand == 0 else EDGE - reach + tap


def prepare_kernel(
    plan, rows, taps, device_ref, values_hbm, pre_hbm, out_grad_hbm,
    kept_ref, sent_ref, direct_ref, padded_ref, windows_ref,
    values_ref, pre_ref, out_grad_ref, arrived,
):
    seqs, length, width = pre_ref.shape
    half, count = width // 2, seqs * length
    pairs = ((pre_hbm, pre_ref), (out_grad_hbm, out_grad_ref), (values_hbm, values_ref))
    copies = [pltpu.make_async_copy(far, near, arrived.at[i]) for i, (far, near) in enumerate(pairs)]
    for copy in copies:
        copy.start()
    direct, mirror = selection(plan, device_ref[0], rows, width)
    direct_ref[...] = direct
    for copy in copies:
        copy.wait()
    values = values_ref[...]
    for out_ref, cut in ((kept_ref, slice(0, half)), (sent_ref, slice(half, width))):
        out_ref[:, :count] = dot(direct[cut], values, NT).astype(BF16)
        out_ref[:, count:] = dot(mirror[cut], values, NT).astype(BF16)
    flip = anti_identity(half)
    for b in range(seqs):
        grads = grad_pre_of(pre_ref[b], out_grad_ref[b])
        for strand in range(2):
            place = strand * seqs + b
            inner = grads[:, :half].astype(F32) if strand == 0 else dot(grads[:, half:], flip)
            padded_ref[place, :EDGE, :] = jnp.zeros((EDGE, half), F32)
            padded_ref[place, EDGE + length :, :] = jnp.zeros((EDGE, half), F32)
            padded_ref[place, EDGE : EDGE + length, :] = inner
            for tap in range(taps):
                start = window_start(strand, tap, taps)
                windows_ref[place * length : (place + 1) * length, tap * half : (tap + 1) * half] = (
                    padded_ref[place, start : start + length, :].astype(BF16)
                )


def first_sums_kernel(taps, order_ref, halo_ref, _, __, out_ref, padded_ref, windows_ref):
    seqs, both, width = halo_ref.shape
    half, reach = width // 2, both // 2
    length = padded_ref.shape[1] - 2 * EDGE
    strip = 16
    flip = anti_identity(half)
    for b in range(seqs):
        for strand in range(2):
            place = strand * seqs + b
            edge = halo_ref[b]
            outer = edge[:, :half].astype(F32) if strand == 0 else dot(edge[:, half:], flip)
            padded_ref[place, EDGE - reach : EDGE, :] = outer[:reach]
            padded_ref[place, EDGE + length : EDGE + length + reach, :] = outer[reach:]
            for tap in range(taps):
                start = window_start(strand, tap, taps)
                for begin in (0, length - strip):
                    windows_ref[
                        place * length + begin : place * length + begin + strip, tap * half : (tap + 1) * half
                    ] = padded_ref[place, start + begin : start + begin + strip, :].astype(BF16)
    out_ref[...] = dot(order_ref[...], windows_ref[...]).astype(out_ref.dtype)


def sums_kernel(order_ref, windows_ref, out_ref):
    out_ref[...] = dot(order_ref[...], windows_ref[...])


def placed_sums(group, windows_ref, direct_ref, weight_refs, begins):
    count = windows_ref.shape[0] // 2
    weights = jnp.concatenate([ref[...] for ref in weight_refs], axis=0)
    chosen = jnp.concatenate(
        [direct_ref[begin : begin + ref.shape[0], :] for ref, begin in zip(weight_refs, begins)], axis=0
    )
    size = weights.shape[0]
    row = lax.broadcasted_iota(jnp.int32, (size, size), 0)
    col = lax.broadcasted_iota(jnp.int32, (size, size), 1)
    turn = jnp.where(row == (col ^ (group - 1)), 1.0, 0.0).astype(BF16)
    mirrored = dot(turn, weights).astype(BF16)
    sums = dot(windows_ref[:count, :], weights, NT) + dot(windows_ref[count:, :], mirrored, NT)
    return dot(sums.astype(BF16), chosen)


def early_input_kernel(group, begins, direct_ref, windows_ref, own_ref, other_ref, out_ref):
    out_ref[...] = placed_sums(group, windows_ref, direct_ref, (own_ref, other_ref), begins).astype(BF16)


def late_input_kernel(group, begins, direct_ref, windows_ref, own_ref, other_ref, early_ref, out_ref):
    late = placed_sums(group, windows_ref, direct_ref, (own_ref, other_ref), begins)
    out_ref[...] = (early_ref[...].astype(F32) + late).astype(BF16)


def reversed_taps(blocks):
    rows, half = blocks[0].shape
    far = dot(jnp.concatenate(blocks, axis=0), anti_identity(half)).astype(BF16)
    far = dot(anti_identity(len(blocks) * rows), far)
    return [far[k * rows : (k + 1) * rows] for k in range(len(blocks))]


def tied_kernel(own_ref, far_ref, out_ref):
    taps, rows, width = far_ref.shape
    half = width // 2
    for place, near_ref, other_ref in ((0, own_ref, far_ref), (1, far_ref, own_ref)):
        other = reversed_taps([other_ref[k, :, half:] for k in range(taps)])
        for k in range(taps):
            out_ref[place * rows : (place + 1) * rows, k * half : (k + 1) * half] = (
                near_ref[k, :, :half].astype(F32) + other[k]
            ).astype(BF16)


def finish_kernel(own_ref, got_ref, out_ref):
    taps, rows, width = out_ref.shape
    half = width // 2
    cuts = [slice(k * half, (k + 1) * half) for k in range(taps)]
    far = own_ref[rows:, :] + got_ref[:rows, :].astype(F32)
    high = far.astype(BF16)
    low = (far - high.astype(F32)).astype(BF16)
    high, low = (reversed_taps([part[:, cut] for cut in cuts]) for part in (high, low))
    near = own_ref[:rows, :] + got_ref[rows:, :].astype(F32)
    for k, cut in enumerate(cuts):
        out_ref[k, :, :half] = near[:, cut]
        out_ref[k, :, half:] = high[k] + low[k]


ON_CHIP = pltpu.VMEM


def call(kernel, outs, args, scalars=0, flops=0, aliases=None, given=(), limit=24, off_chip=(), scratch=()):
    held = pl.BlockSpec(memory_space=ON_CHIP)
    spaces = {i: ON_CHIP for i in given} | {i: pltpu.HBM for i in off_chip}
    args = [pltpu.with_memory_space_constraint(a, spaces[i]) if i in spaces else a for i, a in enumerate(args)]
    result = pl.pallas_call(
        kernel,
        out_shape=[(ON_CHIP if stays else jax.ShapeDtypeStruct)(shape, dtype) for shape, dtype, stays in outs],
        in_specs=[pl.BlockSpec(memory_space=pltpu.SMEM)] * scalars
        + [pl.BlockSpec(memory_space=pltpu.HBM) if i in off_chip else held for i in range(scalars, len(args))],
        scratch_shapes=list(scratch),
        out_specs=[held] * len(outs),
        input_output_aliases=aliases or {},
        cost_estimate=pl.CostEstimate(
            flops=flops,
            transcendentals=0,
            bytes_accessed=sum(math.prod(out[0]) * jnp.dtype(out[1]).itemsize for out in outs)
            + sum(a.size * a.dtype.itemsize for a in args[scalars:]),
        ),
        compiler_params=pltpu.CompilerParams(vmem_limit_bytes=limit << 20),
    )(*args)
    return result if len(outs) > 1 else result[0]


def edges(block, reach):
    count, where = lax.axis_size("pos"), lax.axis_index("pos")
    top, bottom = block[:, -reach:], block[:, :reach]
    if count == 2:
        got = lax.ppermute(jnp.where(where == 0, top, bottom), "pos", [(0, 1), (1, 0)])
        none = jnp.zeros_like(got)
        low, high = jnp.where(where == 0, none, got), jnp.where(where == 0, got, none)
    else:
        forward = [(i, i + 1) for i in range(count - 1)]
        low = lax.ppermute(top, "pos", forward)
        high = lax.ppermute(bottom, "pos", [(b, a) for a, b in forward])
    return jnp.concatenate([low, high], axis=1)


def on_device(plan, inputs, pre_act, grad_out, weight):
    return both_gradients(plan, inputs, pre_act, grad_out, weight)


def both_gradients(plan, inputs, pre_act, grad_out, weight):
    seqs, length, width = inputs.shape
    rows, taps, _ = weight.shape
    half, reach = width // 2, (taps - 1) // 2
    depth, count = taps * half, seqs * length
    work = 4 * count * depth * half
    device = (lax.axis_index("dp") * plan.pos + lax.axis_index("pos")).astype(jnp.int32).reshape(1)

    by_tap = jnp.transpose(weight, (1, 0, 2))
    far_weight = plan.complement(by_tap)
    ends = jnp.concatenate(
        [grad_pre_of(pre_act[:, :reach], grad_out[:, :reach]), grad_pre_of(pre_act[:, -reach:], grad_out[:, -reach:])],
        axis=1,
    )
    halo = edges(ends, reach)
    kept_order, sent_order, direct, padded, windows = call(
        functools.partial(prepare_kernel, plan, rows, taps),
        [((half, 2 * count), BF16, True)] * 2
        + [((width, width), BF16, True)]
        + [((2 * seqs, length + 2 * EDGE, half), F32, True), ((2 * count, depth), BF16, True)],
        (device, inputs.reshape(count, width), pre_act, grad_out),
        scalars=1, flops=4 * count * width * width, off_chip=(1, 2, 3),
        scratch=(
            pltpu.VMEM((count, width), BF16), pltpu.VMEM((seqs, length, width), BF16),
            pltpu.VMEM((seqs, length, width), BF16), pltpu.SemaphoreType.DMA((3,)),
        ),
    )
    sent, _, windows = call(
        functools.partial(first_sums_kernel, taps),
        [((half, depth), BF16, True), (padded.shape, F32, True), (windows.shape, BF16, True)],
        (sent_order, halo, padded, windows), flops=work, aliases={2: 1, 3: 2}, given=(0, 1, 2, 3),
    )
    received = plan.swap(sent, "core")
    kept = call(sums_kernel, [((half, depth), F32, True)], (kept_order, windows), flops=work, given=(0, 1))
    for stage in ("a", "b"):
        middle = kept.shape[0] // 2
        sent = (kept[middle:] + received[middle:].astype(F32)).astype(BF16)
        kept = kept[:middle] + received[:middle].astype(F32)
        received = plan.swap(sent, stage)
    for place, group in enumerate(plan.groups):
        if place == 0:
            kept = kept + received.astype(F32)
        masks = plan.group_masks(group)
        size = kept.shape[0] // len(masks)
        pieces = [
            plan.shift(kept[j * size : (j + 1) * size].astype(BF16), masks[j]).astype(F32)
            for j in range(1, len(masks))
        ]
        kept = functools.reduce(jnp.add, pieces, kept[:size])
    got = plan.complement(kept.astype(BF16))
    grad_weight = jnp.transpose(
        call(
            finish_kernel, [((taps, rows, width), F32, False)], (kept, got),
            flops=4 * rows * depth * half, given=(0, 1),
        ),
        (1, 0, 2),
    )

    gathered = call(
        tied_kernel, [((2 * rows, depth), BF16, True)], (by_tap, far_weight),
        flops=4 * rows * depth * half, given=(1,),
    )
    for place, group in reversed(list(enumerate(plan.groups))):
        gathered = jnp.concatenate([gathered] + [plan.shift(gathered, m) for m in plan.group_masks(group)[1:]], axis=0)
    gathered = jnp.concatenate([gathered, plan.swap(gathered, "b")], axis=0)
    other = plan.swap(gathered, "core")
    late = plan.swap(gathered, "a")
    late_other = plan.swap(late, "core")
    size = gathered.shape[0]
    early = call(
        functools.partial(early_input_kernel, 2 * rows, (0, 2 * size)),
        [((count, width), BF16, True)], (direct, windows, gathered, other),
        flops=work, given=(0, 1, 2, 3),
    )
    grad_input = call(
        functools.partial(late_input_kernel, 2 * rows, (size, 3 * size)),
        [((count, width), BF16, False)], (direct, windows, late, late_other, early),
        flops=work, given=(0, 1, 2, 3, 4),
    ).reshape(seqs, length, width)
    return grad_input, grad_weight


def solution(mesh):
    plan = Plan(mesh.shape["dp"], mesh.shape["pos"])
    placed = (
        P("dp", "pos", None),
        P("dp", "pos", None),
        P("dp", "pos", None),
        P(("dp", "pos"), None, None),
    )
    return jax.shard_map(
        functools.partial(on_device, plan),
        mesh=mesh,
        in_specs=placed,
        out_specs=(P("dp", "pos", None), P(("dp", "pos"), None, None)),
        check_vma=False,
    )
```

```python
import functools
import math

import jax
import jax.numpy as jnp
from jax import lax
from jax.experimental import pallas as pl
from jax.experimental.pallas import tpu as pltpu
from jax.sharding import PartitionSpec as P


AXES = ("dp", "pos")
F32 = jnp.float32
BF16 = jnp.bfloat16
NT = (((1,), (1,)), ((), ()))


def gelu_slope(values):
    cdf = 0.5 * (1.0 + lax.erf(values * 0.7071067811865476))
    return cdf + values * jnp.exp(-0.5 * values * values) * 0.3989422804014327


def grad_pre_of(pre_act, grad_out):
    return (grad_out.astype(F32) * gelu_slope(pre_act.astype(F32))).astype(BF16)


class Plan:
    def __init__(self, dp, pos):
        self.dp, self.pos, self.count = dp, pos, dp * pos
        assert self.count & (self.count - 1) == 0
        dp_bits = [pos << b for b in range(dp.bit_length() - 1)]
        pos_bits = [1 << b for b in range(pos.bit_length() - 1)]
        self.core = dp_bits[0]
        self.cross = (dp_bits[1], pos_bits[0])
        rest = (dp_bits[2:] + pos_bits[1:])[:-1]
        self.groups = [rest[i : i + 2] for i in range(0, len(rest), 2)]

    def mask(self, device, stage):
        if stage == "core":
            return self.core
        parity = 1 if device & self.core else 0
        return self.cross[parity if stage == "a" else 1 - parity]

    def swap(self, block, stage):
        route = [(d, d ^ self.mask(d, stage)) for d in range(self.count)]
        return lax.ppermute(block, AXES, route)

    def group_masks(self, group):
        masks = [0]
        for bit in group:
            masks += [m | bit for m in masks]
        return masks

    def shift(self, block, mask):
        return lax.ppermute(block, AXES, [(d, d ^ mask) for d in range(self.count)])

    def complement(self, block):
        return self.shift(block, self.count - 1)

    def source(self, position, device, rows):
        shift = rows.bit_length() - 1
        slot, low = position >> shift, position & (rows - 1)
        bit = self.count.bit_length() - 2
        flag = (slot >> bit) & 1
        owner = device ^ (flag * self.core)
        parity = jnp.where((owner & self.core) != 0, 1, 0)
        first = parity * self.cross[1] + (1 - parity) * self.cross[0]
        second = parity * self.cross[0] + (1 - parity) * self.cross[1]
        owner = owner ^ (((slot >> (bit - 1)) & 1) * first)
        owner = owner ^ (((slot >> (bit - 2)) & 1) * second)
        bit -= 3
        for group in self.groups:
            for mask in reversed(group):
                owner = owner ^ (((slot >> bit) & 1) * mask)
                bit -= 1
        owner = owner ^ ((slot & 1) * (self.count - 1))
        return (owner << shift) + low


def anti_identity(size):
    row = lax.broadcasted_iota(jnp.int32, (size, size), 0)
    col = lax.broadcasted_iota(jnp.int32, (size, size), 1)
    return jnp.where(row + col == size - 1, 1.0, 0.0).astype(BF16)


def selection(plan, device, rows, width):
    position = lax.broadcasted_iota(jnp.int32, (width, 128), 0)
    lane = lax.broadcasted_iota(jnp.int32, (width, 128), 1)
    source = plan.source(position, device, rows)

    def one_hot(index):
        return jnp.concatenate(
            [jnp.where(index == lane + start, 1.0, 0.0).astype(BF16) for start in range(0, width, 128)],
            axis=1,
        )

    return one_hot(source), one_hot(width - 1 - source)


def dot(left, right, dims=(((1,), (0,)), ((), ()))):
    return lax.dot_general(left, right, dims, preferred_element_type=F32)


EDGE = 8


def window_start(strand, tap, taps):
    reach = (taps - 1) // 2
    return EDGE + reach - tap if strand == 0 else EDGE - reach + tap


def prepare_kernel(
    plan, rows, taps, device_ref, values_hbm, pre_hbm, out_grad_hbm,
    kept_ref, sent_ref, direct_ref, padded_ref, windows_ref,
    values_ref, pre_ref, out_grad_ref, arrived,
):
    seqs, length, width = pre_ref.shape
    half, count = width // 2, seqs * length
    pairs = ((pre_hbm, pre_ref), (out_grad_hbm, out_grad_ref), (values_hbm, values_ref))
    copies = [pltpu.make_async_copy(far, near, arrived.at[i]) for i, (far, near) in enumerate(pairs)]
    for copy in copies:
        copy.start()
    direct, mirror = selection(plan, device_ref[0], rows, width)
    direct_ref[...] = direct
    for copy in copies:
        copy.wait()
    values = values_ref[...]
    for out_ref, cut in ((kept_ref, slice(0, half)), (sent_ref, slice(half, width))):
        out_ref[:, :count] = dot(direct[cut], values, NT).astype(BF16)
        out_ref[:, count:] = dot(mirror[cut], values, NT).astype(BF16)
    flip = anti_identity(half)
    for b in range(seqs):
        grads = grad_pre_of(pre_ref[b], out_grad_ref[b])
        for strand in range(2):
            place = strand * seqs + b
            inner = grads[:, :half].astype(F32) if strand == 0 else dot(grads[:, half:], flip)
            padded_ref[place, :EDGE, :] = jnp.zeros((EDGE, half), F32)
            padded_ref[place, EDGE + length :, :] = jnp.zeros((EDGE, half), F32)
            padded_ref[place, EDGE : EDGE + length, :] = inner
            for tap in range(taps):
                start = window_start(strand, tap, taps)
                windows_ref[place * length : (place + 1) * length, tap * half : (tap + 1) * half] = (
                    padded_ref[place, start : start + length, :].astype(BF16)
                )


def first_sums_kernel(taps, order_ref, halo_ref, _, __, out_ref, padded_ref, windows_ref):
    seqs, both, width = halo_ref.shape
    half, reach = width // 2, both // 2
    length = padded_ref.shape[1] - 2 * EDGE
    strip = 16
    flip = anti_identity(half)
    for b in range(seqs):
        for strand in range(2):
            place = strand * seqs + b
            edge = halo_ref[b]
            outer = edge[:, :half].astype(F32) if strand == 0 else dot(edge[:, half:], flip)
            padded_ref[place, EDGE - reach : EDGE, :] = outer[:reach]
            padded_ref[place, EDGE + length : EDGE + length + reach, :] = outer[reach:]
            for tap in range(taps):
                start = window_start(strand, tap, taps)
                for begin in (0, length - strip):
                    windows_ref[
                        place * length + begin : place * length + begin + strip, tap * half : (tap + 1) * half
                    ] = padded_ref[place, start + begin : start + begin + strip, :].astype(BF16)
    out_ref[...] = dot(order_ref[...], windows_ref[...]).astype(out_ref.dtype)


def sums_kernel(order_ref, windows_ref, out_ref):
    out_ref[...] = dot(order_ref[...], windows_ref[...])


def placed_sums(group, windows_ref, direct_ref, weight_refs, begins):
    count = windows_ref.shape[0] // 2
    weights = jnp.concatenate([ref[...] for ref in weight_refs], axis=0)
    chosen = jnp.concatenate(
        [direct_ref[begin : begin + ref.shape[0], :] for ref, begin in zip(weight_refs, begins)], axis=0
    )
    size = weights.shape[0]
    row = lax.broadcasted_iota(jnp.int32, (size, size), 0)
    col = lax.broadcasted_iota(jnp.int32, (size, size), 1)
    turn = jnp.where(row == (col ^ (group - 1)), 1.0, 0.0).astype(BF16)
    mirrored = dot(turn, weights).astype(BF16)
    sums = dot(windows_ref[:count, :], weights, NT) + dot(windows_ref[count:, :], mirrored, NT)
    return dot(sums.astype(BF16), chosen)


def early_input_kernel(group, begins, direct_ref, windows_ref, own_ref, other_ref, out_ref):
    out_ref[...] = placed_sums(group, windows_ref, direct_ref, (own_ref, other_ref), begins).astype(BF16)


def late_input_kernel(group, begins, direct_ref, windows_ref, early_ref, *refs):
    late = placed_sums(group, windows_ref, direct_ref, refs[:-1], begins)
    refs[-1][...] = (early_ref[...].astype(F32) + late).astype(BF16)


def reversed_taps(blocks):
    rows, half = blocks[0].shape
    far = dot(jnp.concatenate(blocks, axis=0), anti_identity(half)).astype(BF16)
    far = dot(anti_identity(len(blocks) * rows), far)
    return [far[k * rows : (k + 1) * rows] for k in range(len(blocks))]


def tied_kernel(own_ref, far_ref, out_ref):
    taps, rows, width = far_ref.shape
    half = width // 2
    for place, near_ref, other_ref in ((0, own_ref, far_ref), (1, far_ref, own_ref)):
        other = reversed_taps([other_ref[k, :, half:] for k in range(taps)])
        for k in range(taps):
            out_ref[place * rows : (place + 1) * rows, k * half : (k + 1) * half] = (
                near_ref[k, :, :half].astype(F32) + other[k]
            ).astype(BF16)


def finish_kernel(own_ref, got_ref, out_ref):
    taps, rows, width = out_ref.shape
    half = width // 2
    cuts = [slice(k * half, (k + 1) * half) for k in range(taps)]
    far = own_ref[rows:, :] + got_ref[:rows, :].astype(F32)
    high = far.astype(BF16)
    low = (far - high.astype(F32)).astype(BF16)
    high, low = (reversed_taps([part[:, cut] for cut in cuts]) for part in (high, low))
    near = own_ref[:rows, :] + got_ref[rows:, :].astype(F32)
    for k, cut in enumerate(cuts):
        out_ref[k, :, :half] = near[:, cut]
        out_ref[k, :, half:] = high[k] + low[k]


ON_CHIP = pltpu.VMEM


def call(kernel, outs, args, scalars=0, flops=0, aliases=None, given=(), limit=24, off_chip=(), scratch=()):
    held = pl.BlockSpec(memory_space=ON_CHIP)
    spaces = {i: ON_CHIP for i in given} | {i: pltpu.HBM for i in off_chip}
    args = [pltpu.with_memory_space_constraint(a, spaces[i]) if i in spaces else a for i, a in enumerate(args)]
    result = pl.pallas_call(
        kernel,
        out_shape=[(ON_CHIP if stays else jax.ShapeDtypeStruct)(shape, dtype) for shape, dtype, stays in outs],
        in_specs=[pl.BlockSpec(memory_space=pltpu.SMEM)] * scalars
        + [pl.BlockSpec(memory_space=pltpu.HBM) if i in off_chip else held for i in range(scalars, len(args))],
        scratch_shapes=list(scratch),
        out_specs=[held] * len(outs),
        input_output_aliases=aliases or {},
        cost_estimate=pl.CostEstimate(
            flops=flops,
            transcendentals=0,
            bytes_accessed=sum(math.prod(out[0]) * jnp.dtype(out[1]).itemsize for out in outs)
            + sum(a.size * a.dtype.itemsize for a in args[scalars:]),
        ),
        compiler_params=pltpu.CompilerParams(vmem_limit_bytes=limit << 20),
    )(*args)
    return result if len(outs) > 1 else result[0]


def edges(block, reach):
    count, where = lax.axis_size("pos"), lax.axis_index("pos")
    top, bottom = block[:, -reach:], block[:, :reach]
    if count == 2:
        got = lax.ppermute(jnp.where(where == 0, top, bottom), "pos", [(0, 1), (1, 0)])
        none = jnp.zeros_like(got)
        low, high = jnp.where(where == 0, none, got), jnp.where(where == 0, got, none)
    else:
        forward = [(i, i + 1) for i in range(count - 1)]
        low = lax.ppermute(top, "pos", forward)
        high = lax.ppermute(bottom, "pos", [(b, a) for a, b in forward])
    return jnp.concatenate([low, high], axis=1)


def on_device(plan, inputs, pre_act, grad_out, weight):
    return both_gradients(plan, inputs, pre_act, grad_out, weight)


def both_gradients(plan, inputs, pre_act, grad_out, weight):
    seqs, length, width = inputs.shape
    rows, taps, _ = weight.shape
    half, reach = width // 2, (taps - 1) // 2
    depth, count = taps * half, seqs * length
    work = 4 * count * depth * half
    device = (lax.axis_index("dp") * plan.pos + lax.axis_index("pos")).astype(jnp.int32).reshape(1)

    by_tap = jnp.transpose(weight, (1, 0, 2))
    far_weight = plan.complement(by_tap)
    ends = jnp.concatenate(
        [grad_pre_of(pre_act[:, :reach], grad_out[:, :reach]), grad_pre_of(pre_act[:, -reach:], grad_out[:, -reach:])],
        axis=1,
    )
    halo = edges(ends, reach)
    kept_order, sent_order, direct, padded, windows = call(
        functools.partial(prepare_kernel, plan, rows, taps),
        [((half, 2 * count), BF16, True)] * 2
        + [((width, width), BF16, True)]
        + [((2 * seqs, length + 2 * EDGE, half), F32, True), ((2 * count, depth), BF16, True)],
        (device, inputs.reshape(count, width), pre_act, grad_out),
        scalars=1, flops=4 * count * width * width, off_chip=(1, 2, 3),
        scratch=(
            pltpu.VMEM((count, width), BF16), pltpu.VMEM((seqs, length, width), BF16),
            pltpu.VMEM((seqs, length, width), BF16), pltpu.SemaphoreType.DMA((3,)),
        ),
    )
    sent, _, windows = call(
        functools.partial(first_sums_kernel, taps),
        [((half, depth), BF16, True), (padded.shape, F32, True), (windows.shape, BF16, True)],
        (sent_order, halo, padded, windows), flops=work, aliases={2: 1, 3: 2}, given=(0, 1, 2, 3),
    )
    received = plan.swap(sent, "core")
    kept = call(sums_kernel, [((half, depth), F32, True)], (kept_order, windows), flops=work, given=(0, 1))
    for stage in ("a", "b"):
        middle = kept.shape[0] // 2
        sent = (kept[middle:] + received[middle:].astype(F32)).astype(BF16)
        kept = kept[:middle] + received[:middle].astype(F32)
        received = plan.swap(sent, stage)
    for place, group in enumerate(plan.groups):
        if place == 0:
            kept = kept + received.astype(F32)
        masks = plan.group_masks(group)
        size = kept.shape[0] // len(masks)
        pieces = [
            plan.shift(kept[j * size : (j + 1) * size].astype(BF16), masks[j]).astype(F32)
            for j in range(1, len(masks))
        ]
        kept = functools.reduce(jnp.add, pieces, kept[:size])
    got = plan.complement(kept.astype(BF16))
    grad_weight = jnp.transpose(
        call(
            finish_kernel, [((taps, rows, width), F32, False)], (kept, got),
            flops=4 * rows * depth * half, given=(0, 1),
        ),
        (1, 0, 2),
    )

    gathered = call(
        tied_kernel, [((2 * rows, depth), BF16, True)], (by_tap, far_weight),
        flops=4 * rows * depth * half, given=(1,),
    )
    for place, group in reversed(list(enumerate(plan.groups))):
        gathered = jnp.concatenate([gathered] + [plan.shift(gathered, m) for m in plan.group_masks(group)[1:]], axis=0)
    size = gathered.shape[0]
    relayed = plan.swap(gathered, "b")
    late = [plan.swap(gathered, "a")]
    late.append(plan.swap(relayed, "a"))
    gathered = jnp.concatenate([gathered, relayed], axis=0)
    other = plan.swap(gathered, "core")
    for place in range(2):
        late.append(plan.swap(late[place], "core"))
    early = call(
        functools.partial(early_input_kernel, 2 * rows, (0, 4 * size)),
        [((count, width), BF16, True)], (direct, windows, gathered, other),
        flops=work, given=(0, 1, 2, 3),
    )
    grad_input = call(
        functools.partial(late_input_kernel, 2 * rows, (2 * size, 3 * size, 6 * size, 7 * size)),
        [((count, width), BF16, False)], (direct, windows, early, *late),
        flops=work, given=range(7),
    ).reshape(seqs, length, width)
    return grad_input, grad_weight


def solution(mesh):
    plan = Plan(mesh.shape["dp"], mesh.shape["pos"])
    placed = (
        P("dp", "pos", None),
        P("dp", "pos", None),
        P("dp", "pos", None),
        P(("dp", "pos"), None, None),
    )
    return jax.shard_map(
        functools.partial(on_device, plan),
        mesh=mesh,
        in_specs=placed,
        out_specs=(P("dp", "pos", None), P(("dp", "pos"), None, None)),
        check_vma=False,
    )
```

```python
import functools
import math

import jax
import jax.numpy as jnp
from jax import lax
from jax.experimental import pallas as pl
from jax.experimental.pallas import tpu as pltpu
from jax.sharding import PartitionSpec as P


AXES = ("dp", "pos")
F32 = jnp.float32
BF16 = jnp.bfloat16
NT = (((1,), (1,)), ((), ()))


def gelu_slope(values):
    cdf = 0.5 * (1.0 + lax.erf(values * 0.7071067811865476))
    return cdf + values * jnp.exp(-0.5 * values * values) * 0.3989422804014327


def grad_pre_of(pre_act, grad_out):
    return (grad_out.astype(F32) * gelu_slope(pre_act.astype(F32))).astype(BF16)


class Plan:
    def __init__(self, dp, pos):
        self.dp, self.pos, self.count = dp, pos, dp * pos
        assert self.count & (self.count - 1) == 0
        dp_bits = [pos << b for b in range(dp.bit_length() - 1)]
        pos_bits = [1 << b for b in range(pos.bit_length() - 1)]
        self.core = dp_bits[0]
        self.cross = (dp_bits[1], pos_bits[0])
        rest = (dp_bits[2:] + pos_bits[1:])[:-1]
        self.groups = [rest[i : i + 2] for i in range(0, len(rest), 2)]

    def mask(self, device, stage):
        if stage == "core":
            return self.core
        parity = 1 if device & self.core else 0
        return self.cross[parity if stage == "a" else 1 - parity]

    def swap(self, block, stage):
        route = [(d, d ^ self.mask(d, stage)) for d in range(self.count)]
        return lax.ppermute(block, AXES, route)

    def group_masks(self, group):
        masks = [0]
        for bit in group:
            masks += [m | bit for m in masks]
        return masks

    def shift(self, block, mask):
        return lax.ppermute(block, AXES, [(d, d ^ mask) for d in range(self.count)])

    def complement(self, block):
        return self.shift(block, self.count - 1)

    def source(self, position, device, rows):
        shift = rows.bit_length() - 1
        slot, low = position >> shift, position & (rows - 1)
        bit = self.count.bit_length() - 2
        flag = (slot >> bit) & 1
        owner = device ^ (flag * self.core)
        parity = jnp.where((owner & self.core) != 0, 1, 0)
        first = parity * self.cross[1] + (1 - parity) * self.cross[0]
        second = parity * self.cross[0] + (1 - parity) * self.cross[1]
        owner = owner ^ (((slot >> (bit - 1)) & 1) * first)
        owner = owner ^ (((slot >> (bit - 2)) & 1) * second)
        bit -= 3
        for group in self.groups:
            for mask in reversed(group):
                owner = owner ^ (((slot >> bit) & 1) * mask)
                bit -= 1
        owner = owner ^ ((slot & 1) * (self.count - 1))
        return (owner << shift) + low


def anti_identity(size):
    row = lax.broadcasted_iota(jnp.int32, (size, size), 0)
    col = lax.broadcasted_iota(jnp.int32, (size, size), 1)
    return jnp.where(row + col == size - 1, 1.0, 0.0).astype(BF16)


def selection(plan, device, rows, width):
    position = lax.broadcasted_iota(jnp.int32, (width, 128), 0)
    lane = lax.broadcasted_iota(jnp.int32, (width, 128), 1)
    source = plan.source(position, device, rows)

    def one_hot(index):
        return jnp.concatenate(
            [jnp.where(index == lane + start, 1.0, 0.0).astype(BF16) for start in range(0, width, 128)],
            axis=1,
        )

    return one_hot(source), one_hot(width - 1 - source)


def dot(left, right, dims=(((1,), (0,)), ((), ()))):
    return lax.dot_general(left, right, dims, preferred_element_type=F32)


EDGE = 8


def window_start(strand, tap, taps):
    reach = (taps - 1) // 2
    return EDGE + reach - tap if strand == 0 else EDGE - reach + tap


def prepare_kernel(
    plan, rows, taps, device_ref, values_hbm, pre_hbm, out_grad_hbm,
    first_ref, second_ref, padded_ref, windows_ref,
    values_ref, pre_ref, out_grad_ref, arrived,
):
    seqs, length, width = pre_ref.shape
    half, count = width // 2, seqs * length
    pairs = []
    for b in range(seqs):
        pairs += [(pre_hbm.at[b], pre_ref.at[b]), (out_grad_hbm.at[b], out_grad_ref.at[b])]
        if b == 0:
            pairs.append((values_hbm, values_ref))
    copies = [pltpu.make_async_copy(far, near, arrived.at[i]) for i, (far, near) in enumerate(pairs)]
    for copy in copies:
        copy.start()
    direct, mirror = selection(plan, device_ref[0], rows, width)
    flip = anti_identity(half)
    for b in range(seqs):
        for copy in copies[:2]:
            copy.wait()
        copies = copies[2:]
        grads = grad_pre_of(pre_ref[b], out_grad_ref[b])
        for strand in range(2):
            place = strand * seqs + b
            inner = grads[:, :half].astype(F32) if strand == 0 else dot(grads[:, half:], flip)
            padded_ref[place, :EDGE, :] = jnp.zeros((EDGE, half), F32)
            padded_ref[place, EDGE + length :, :] = jnp.zeros((EDGE, half), F32)
            padded_ref[place, EDGE : EDGE + length, :] = inner
            for tap in range(taps):
                start = window_start(strand, tap, taps)
                windows_ref[place * length : (place + 1) * length, tap * half : (tap + 1) * half] = (
                    padded_ref[place, start : start + length, :].astype(BF16)
                )
        if b == 0:
            copies.pop(0).wait()
            values = values_ref[...]
            quarter = width // 4
            for out_ref, begins in ((first_ref, (3, 1)), (second_ref, (2, 0))):
                for place, begin in enumerate(begins):
                    cut = slice(begin * quarter, (begin + 1) * quarter)
                    out = slice(place * quarter, (place + 1) * quarter)
                    out_ref[out, :count] = dot(direct[cut], values, NT).astype(BF16)
                    out_ref[out, count:] = dot(mirror[cut], values, NT).astype(BF16)


def first_sums_kernel(taps, order_ref, halo_ref, _, __, sent_ref, kept_ref, padded_ref, windows_ref):
    seqs, both, width = halo_ref.shape
    half, reach = width // 2, both // 2
    length = padded_ref.shape[1] - 2 * EDGE
    strip = 16
    flip = anti_identity(half)
    for b in range(seqs):
        for strand in range(2):
            place = strand * seqs + b
            edge = halo_ref[b]
            outer = edge[:, :half].astype(F32) if strand == 0 else dot(edge[:, half:], flip)
            padded_ref[place, EDGE - reach : EDGE, :] = outer[:reach]
            padded_ref[place, EDGE + length : EDGE + length + reach, :] = outer[reach:]
            for tap in range(taps):
                start = window_start(strand, tap, taps)
                for begin in (0, length - strip):
                    windows_ref[
                        place * length + begin : place * length + begin + strip, tap * half : (tap + 1) * half
                    ] = padded_ref[place, start + begin : start + begin + strip, :].astype(BF16)
    sums_kernel(order_ref, windows_ref, sent_ref, kept_ref)


def sums_kernel(order_ref, windows_ref, sent_ref, kept_ref):
    sums = dot(order_ref[...], windows_ref[...])
    size = sent_ref.shape[0]
    sent_ref[...] = sums[:size].astype(BF16)
    kept_ref[...] = sums[size:]


def rounded_sums(group, windows_ref, weight_refs):
    count = windows_ref.shape[0] // 2
    weights = jnp.concatenate([ref[...] for ref in weight_refs], axis=0)
    size = weights.shape[0]
    row = lax.broadcasted_iota(jnp.int32, (size, size), 0)
    col = lax.broadcasted_iota(jnp.int32, (size, size), 1)
    turn = jnp.where(row == (col ^ (group - 1)), 1.0, 0.0).astype(BF16)
    mirrored = dot(turn, weights).astype(BF16)
    return (dot(windows_ref[:count, :], weights, NT) + dot(windows_ref[count:, :], mirrored, NT)).astype(BF16)


def chosen_rows(direct, weight_refs, begins):
    return jnp.concatenate([direct[a : a + ref.shape[0], :] for ref, a in zip(weight_refs, begins)], axis=0)


def early_input_kernel(plan, rows, begins, late_begins, device_ref, windows_ref, own_ref, other_ref, out_ref, late_ref):
    refs = (own_ref, other_ref)
    direct, _ = selection(plan, device_ref[0], rows, out_ref.shape[1])
    out_ref[...] = dot(rounded_sums(2 * rows, windows_ref, refs), chosen_rows(direct, refs, begins)).astype(BF16)
    size = late_ref.shape[0] // len(late_begins)
    for place, begin in enumerate(late_begins):
        late_ref[place * size : (place + 1) * size, :] = direct[begin : begin + size, :]


def late_input_kernel(group, windows_ref, early_ref, chosen_ref, *refs):
    weight_refs, (out_hbm, out_ref, stored) = refs[:-3], refs[-3:]
    sums = rounded_sums(group, windows_ref, weight_refs)
    half, copies = out_ref.shape[0] // 2, []
    for place in range(2):
        cut = slice(place * half, (place + 1) * half)
        out_ref[cut, :] = (early_ref[cut, :].astype(F32) + dot(sums[cut], chosen_ref[...])).astype(BF16)
        copies.append(pltpu.make_async_copy(out_ref.at[cut, :], out_hbm.at[cut, :], stored.at[place]))
        copies[-1].start()
    for copy in copies:
        copy.wait()


def reversed_taps(blocks):
    rows, half = blocks[0].shape
    far = dot(jnp.concatenate(blocks, axis=0), anti_identity(half)).astype(BF16)
    far = dot(anti_identity(len(blocks) * rows), far)
    return [far[k * rows : (k + 1) * rows] for k in range(len(blocks))]


def tied_kernel(own_ref, far_ref, out_ref):
    taps, rows, width = far_ref.shape
    half = width // 2
    for place, near_ref, other_ref in ((0, own_ref, far_ref), (1, far_ref, own_ref)):
        other = reversed_taps([other_ref[k, :, half:] for k in range(taps)])
        for k in range(taps):
            out_ref[place * rows : (place + 1) * rows, k * half : (k + 1) * half] = (
                near_ref[k, :, :half].astype(F32) + other[k]
            ).astype(BF16)


def finish_kernel(own_ref, got_ref, out_ref):
    taps, rows, width = out_ref.shape
    half = width // 2
    cuts = [slice(k * half, (k + 1) * half) for k in range(taps)]
    far = own_ref[rows:, :] + got_ref[:rows, :].astype(F32)
    high = far.astype(BF16)
    low = (far - high.astype(F32)).astype(BF16)
    high, low = (reversed_taps([part[:, cut] for cut in cuts]) for part in (high, low))
    near = own_ref[:rows, :] + got_ref[rows:, :].astype(F32)
    for k, cut in enumerate(cuts):
        out_ref[k, :, :half] = near[:, cut]
        out_ref[k, :, half:] = high[k] + low[k]


ON_CHIP = pltpu.VMEM


def call(kernel, outs, args, scalars=0, flops=0, aliases=None, given=(), limit=24, off_chip=(), scratch=()):
    held = pl.BlockSpec(memory_space=ON_CHIP)
    spaces = {i: ON_CHIP for i in given} | {i: pltpu.HBM for i in off_chip}
    args = [pltpu.with_memory_space_constraint(a, spaces[i]) if i in spaces else a for i, a in enumerate(args)]
    result = pl.pallas_call(
        kernel,
        out_shape=[(ON_CHIP if stays else jax.ShapeDtypeStruct)(shape, dtype) for shape, dtype, stays in outs],
        in_specs=[pl.BlockSpec(memory_space=pltpu.SMEM)] * scalars
        + [pl.BlockSpec(memory_space=pltpu.HBM) if i in off_chip else held for i in range(scalars, len(args))],
        scratch_shapes=list(scratch),
        out_specs=[pl.BlockSpec(memory_space=pltpu.HBM) if out[2] is None else held for out in outs],
        input_output_aliases=aliases or {},
        cost_estimate=pl.CostEstimate(
            flops=flops,
            transcendentals=0,
            bytes_accessed=sum(math.prod(out[0]) * jnp.dtype(out[1]).itemsize for out in outs)
            + sum(a.size * a.dtype.itemsize for a in args[scalars:]),
        ),
        compiler_params=pltpu.CompilerParams(vmem_limit_bytes=limit << 20),
    )(*args)
    return result if len(outs) > 1 else result[0]


def edges(block, reach):
    count, where = lax.axis_size("pos"), lax.axis_index("pos")
    top, bottom = block[:, -reach:], block[:, :reach]
    if count == 2:
        got = lax.ppermute(jnp.where(where == 0, top, bottom), "pos", [(0, 1), (1, 0)])
        none = jnp.zeros_like(got)
        low, high = jnp.where(where == 0, none, got), jnp.where(where == 0, got, none)
    else:
        forward = [(i, i + 1) for i in range(count - 1)]
        low = lax.ppermute(top, "pos", forward)
        high = lax.ppermute(bottom, "pos", [(b, a) for a, b in forward])
    return jnp.concatenate([low, high], axis=1)


def on_device(plan, inputs, pre_act, grad_out, weight):
    return both_gradients(plan, inputs, pre_act, grad_out, weight)


def both_gradients(plan, inputs, pre_act, grad_out, weight):
    seqs, length, width = inputs.shape
    rows, taps, _ = weight.shape
    half, reach = width // 2, (taps - 1) // 2
    depth, count = taps * half, seqs * length
    work = 4 * count * depth * half
    device = (lax.axis_index("dp") * plan.pos + lax.axis_index("pos")).astype(jnp.int32).reshape(1)

    by_tap = jnp.transpose(weight, (1, 0, 2))
    far_weight = plan.complement(by_tap)
    ends = jnp.concatenate(
        [grad_pre_of(pre_act[:, :reach], grad_out[:, :reach]), grad_pre_of(pre_act[:, -reach:], grad_out[:, -reach:])],
        axis=1,
    )
    halo = edges(ends, reach)
    first_order, second_order, padded, windows = call(
        functools.partial(prepare_kernel, plan, rows, taps),
        [((half, 2 * count), BF16, True)] * 2
        + [((2 * seqs, length + 2 * EDGE, half), F32, True), ((2 * count, depth), BF16, True)],
        (device, inputs.reshape(count, width), pre_act, grad_out),
        scalars=1, flops=4 * count * width * width, off_chip=(1, 2, 3),
        scratch=(
            pltpu.VMEM((count, width), BF16), pltpu.VMEM((seqs, length, width), BF16),
            pltpu.VMEM((seqs, length, width), BF16), pltpu.SemaphoreType.DMA((2 * seqs + 1,)),
        ),
    )
    sums = [((half // 2, depth), BF16, True), ((half // 2, depth), F32, True)]
    sent, kept, _, windows = call(
        functools.partial(first_sums_kernel, taps),
        sums + [(padded.shape, F32, True), (windows.shape, BF16, True)],
        (first_order, halo, padded, windows), flops=work, aliases={2: 2, 3: 3}, given=(0, 1, 2, 3),
    )
    received = plan.swap(sent, "core")
    second_sent, second_kept = call(sums_kernel, sums, (second_order, windows), flops=work, given=(0, 1))
    received = plan.swap((kept + received.astype(F32)).astype(BF16), "a")
    kept = second_kept + plan.swap(second_sent, "core").astype(F32)
    middle = kept.shape[0] // 2
    sent = (kept[middle:] + received[middle:].astype(F32)).astype(BF16)
    kept = kept[:middle] + received[:middle].astype(F32)
    received = plan.swap(sent, "b")
    for place, group in enumerate(plan.groups):
        if place == 0:
            kept = kept + received.astype(F32)
        masks = plan.group_masks(group)
        size = kept.shape[0] // len(masks)
        pieces = [
            plan.shift(kept[j * size : (j + 1) * size].astype(BF16), masks[j]).astype(F32)
            for j in range(1, len(masks))
        ]
        kept = functools.reduce(jnp.add, pieces, kept[:size])
    got = plan.complement(kept.astype(BF16))
    grad_weight = jnp.transpose(
        call(
            finish_kernel, [((taps, rows, width), F32, False)], (kept, got),
            flops=4 * rows * depth * half, given=(0, 1),
        ),
        (1, 0, 2),
    )

    gathered = call(
        tied_kernel, [((2 * rows, depth), BF16, True)], (by_tap, far_weight),
        flops=4 * rows * depth * half, given=(1,),
    )
    for place, group in reversed(list(enumerate(plan.groups))):
        gathered = jnp.concatenate([gathered] + [plan.shift(gathered, m) for m in plan.group_masks(group)[1:]], axis=0)
    size = gathered.shape[0]
    relayed = plan.swap(gathered, "b")
    late = [plan.swap(gathered, "a")]
    late.append(plan.swap(relayed, "a"))
    gathered = jnp.concatenate([gathered, relayed], axis=0)
    other = plan.swap(gathered, "core")
    for place in range(2):
        late.append(plan.swap(late[place], "core"))
    begins = (2 * size, 3 * size, 6 * size, 7 * size)
    early, chosen = call(
        functools.partial(early_input_kernel, plan, rows, (0, 4 * size), begins),
        [((count, width), BF16, True), ((half, width), BF16, True)], (device, windows, gathered, other),
        scalars=1, flops=work, given=(1, 2, 3),
    )
    grad_input = call(
        functools.partial(late_input_kernel, 2 * rows),
        [((count, width), BF16, None)], (windows, early, chosen, *late),
        flops=work, given=range(7),
        scratch=(pltpu.VMEM((count, width), BF16), pltpu.SemaphoreType.DMA((2,))),
    ).reshape(seqs, length, width)
    return grad_input, grad_weight


def solution(mesh):
    plan = Plan(mesh.shape["dp"], mesh.shape["pos"])
    placed = (
        P("dp", "pos", None),
        P("dp", "pos", None),
        P("dp", "pos", None),
        P(("dp", "pos"), None, None),
    )
    return jax.shard_map(
        functools.partial(on_device, plan),
        mesh=mesh,
        in_specs=placed,
        out_specs=(P("dp", "pos", None), P(("dp", "pos"), None, None)),
        check_vma=False,
    )
```

```python
import functools
import math

import jax
import jax.numpy as jnp
from jax import lax
from jax.experimental import pallas as pl
from jax.experimental.pallas import tpu as pltpu
from jax.sharding import PartitionSpec as P


AXES = ("dp", "pos")
F32 = jnp.float32
BF16 = jnp.bfloat16
NT = (((1,), (1,)), ((), ()))


def gelu_slope(values):
    cdf = 0.5 * (1.0 + lax.erf(values * 0.7071067811865476))
    return cdf + values * jnp.exp(-0.5 * values * values) * 0.3989422804014327


def grad_pre_of(pre_act, grad_out):
    return (grad_out.astype(F32) * gelu_slope(pre_act.astype(F32))).astype(BF16)


class Plan:
    def __init__(self, dp, pos):
        self.dp, self.pos, self.count = dp, pos, dp * pos
        assert self.count & (self.count - 1) == 0
        dp_bits = [pos << b for b in range(dp.bit_length() - 1)]
        pos_bits = [1 << b for b in range(pos.bit_length() - 1)]
        self.core = dp_bits[0]
        self.cross = (dp_bits[1], pos_bits[0])
        rest = (dp_bits[2:] + pos_bits[1:])[:-1]
        self.groups = [rest[i : i + 2] for i in range(0, len(rest), 2)]

    def mask(self, device, stage):
        if stage == "core":
            return self.core
        parity = 1 if device & self.core else 0
        return self.cross[parity if stage == "a" else 1 - parity]

    def swap(self, block, stage):
        route = [(d, d ^ self.mask(d, stage)) for d in range(self.count)]
        return lax.ppermute(block, AXES, route)

    def group_masks(self, group):
        masks = [0]
        for bit in group:
            masks += [m | bit for m in masks]
        return masks

    def shift(self, block, mask):
        return lax.ppermute(block, AXES, [(d, d ^ mask) for d in range(self.count)])

    def complement(self, block):
        return self.shift(block, self.count - 1)

    def source(self, position, device, rows):
        shift = rows.bit_length() - 1
        slot, low = position >> shift, position & (rows - 1)
        bit = self.count.bit_length() - 2
        flag = (slot >> bit) & 1
        owner = device ^ (flag * self.core)
        parity = jnp.where((owner & self.core) != 0, 1, 0)
        first = parity * self.cross[1] + (1 - parity) * self.cross[0]
        second = parity * self.cross[0] + (1 - parity) * self.cross[1]
        owner = owner ^ (((slot >> (bit - 1)) & 1) * first)
        owner = owner ^ (((slot >> (bit - 2)) & 1) * second)
        bit -= 3
        for group in self.groups:
            for mask in reversed(group):
                owner = owner ^ (((slot >> bit) & 1) * mask)
                bit -= 1
        owner = owner ^ ((slot & 1) * (self.count - 1))
        return (owner << shift) + low


def anti_identity(size):
    row = lax.broadcasted_iota(jnp.int32, (size, size), 0)
    col = lax.broadcasted_iota(jnp.int32, (size, size), 1)
    return jnp.where(row + col == size - 1, 1.0, 0.0).astype(BF16)


def selection(plan, device, rows, width):
    position = lax.broadcasted_iota(jnp.int32, (width, 128), 0)
    lane = lax.broadcasted_iota(jnp.int32, (width, 128), 1)
    source = plan.source(position, device, rows)

    def one_hot(index):
        return jnp.concatenate(
            [jnp.where(index == lane + start, 1.0, 0.0).astype(BF16) for start in range(0, width, 128)],
            axis=1,
        )

    return one_hot(source), one_hot(width - 1 - source)


def dot(left, right, dims=(((1,), (0,)), ((), ()))):
    return lax.dot_general(left, right, dims, preferred_element_type=F32)


EDGE = 8


def window_start(strand, tap, taps):
    reach = (taps - 1) // 2
    return EDGE + reach - tap if strand == 0 else EDGE - reach + tap


def prepare_kernel(
    plan, rows, taps, device_ref, values_hbm, pre_hbm, out_grad_hbm,
    first_ref, second_ref, padded_ref, windows_ref,
    values_ref, pre_ref, out_grad_ref, arrived,
):
    seqs, length, width = pre_ref.shape
    half, count = width // 2, seqs * length
    pairs = ((pre_hbm, pre_ref), (out_grad_hbm, out_grad_ref), (values_hbm, values_ref))
    copies = [pltpu.make_async_copy(far, near, arrived.at[i]) for i, (far, near) in enumerate(pairs)]
    for copy in copies:
        copy.start()
    direct, mirror = selection(plan, device_ref[0], rows, width)
    for copy in copies:
        copy.wait()
    values = values_ref[...]
    quarter = width // 4
    for out_ref, begins in ((first_ref, (3, 1)), (second_ref, (2, 0))):
        for place, begin in enumerate(begins):
            cut = slice(begin * quarter, (begin + 1) * quarter)
            out = slice(place * quarter, (place + 1) * quarter)
            out_ref[out, :count] = dot(direct[cut], values, NT).astype(BF16)
            out_ref[out, count:] = dot(mirror[cut], values, NT).astype(BF16)
    flip = anti_identity(half)
    for b in range(seqs):
        grads = grad_pre_of(pre_ref[b], out_grad_ref[b])
        for strand in range(2):
            place = strand * seqs + b
            inner = grads[:, :half].astype(F32) if strand == 0 else dot(grads[:, half:], flip)
            padded_ref[place, :EDGE, :] = jnp.zeros((EDGE, half), F32)
            padded_ref[place, EDGE + length :, :] = jnp.zeros((EDGE, half), F32)
            padded_ref[place, EDGE : EDGE + length, :] = inner
            for tap in range(taps):
                start = window_start(strand, tap, taps)
                windows_ref[place * length : (place + 1) * length, tap * half : (tap + 1) * half] = (
                    padded_ref[place, start : start + length, :].astype(BF16)
                )


def first_sums_kernel(taps, order_ref, halo_ref, _, __, sent_ref, kept_ref, padded_ref, windows_ref):
    seqs, both, width = halo_ref.shape
    half, reach = width // 2, both // 2
    length = padded_ref.shape[1] - 2 * EDGE
    strip = 16
    flip = anti_identity(half)
    for b in range(seqs):
        for strand in range(2):
            place = strand * seqs + b
            edge = halo_ref[b]
            outer = edge[:, :half].astype(F32) if strand == 0 else dot(edge[:, half:], flip)
            padded_ref[place, EDGE - reach : EDGE, :] = outer[:reach]
            padded_ref[place, EDGE + length : EDGE + length + reach, :] = outer[reach:]
            for tap in range(taps):
                start = window_start(strand, tap, taps)
                for begin in (0, length - strip):
                    windows_ref[
                        place * length + begin : place * length + begin + strip, tap * half : (tap + 1) * half
                    ] = padded_ref[place, start + begin : start + begin + strip, :].astype(BF16)
    sums_kernel(order_ref, windows_ref, sent_ref, kept_ref)


def sums_kernel(order_ref, windows_ref, sent_ref, kept_ref):
    sums = dot(order_ref[...], windows_ref[...])
    size = sent_ref.shape[0]
    sent_ref[...] = sums[:size].astype(BF16)
    kept_ref[...] = sums[size:]


def rounded_sums(group, windows_ref, weight_refs):
    count = windows_ref.shape[0] // 2
    weights = jnp.concatenate([ref[...] for ref in weight_refs], axis=0)
    size = weights.shape[0]
    row = lax.broadcasted_iota(jnp.int32, (size, size), 0)
    col = lax.broadcasted_iota(jnp.int32, (size, size), 1)
    turn = jnp.where(row == (col ^ (group - 1)), 1.0, 0.0).astype(BF16)
    mirrored = dot(turn, weights).astype(BF16)
    return (dot(windows_ref[:count, :], weights, NT) + dot(windows_ref[count:, :], mirrored, NT)).astype(BF16)


def chosen_rows(direct, weight_refs, begins):
    return jnp.concatenate([direct[a : a + ref.shape[0], :] for ref, a in zip(weight_refs, begins)], axis=0)


def early_input_kernel(plan, rows, begins, late_begins, device_ref, windows_ref, own_ref, other_ref, out_ref, late_ref):
    refs = (own_ref, other_ref)
    direct, _ = selection(plan, device_ref[0], rows, out_ref.shape[1])
    out_ref[...] = dot(rounded_sums(2 * rows, windows_ref, refs), chosen_rows(direct, refs, begins)).astype(BF16)
    size = late_ref.shape[0] // len(late_begins)
    for place, begin in enumerate(late_begins):
        late_ref[place * size : (place + 1) * size, :] = direct[begin : begin + size, :]


def late_input_kernel(group, windows_ref, early_ref, chosen_ref, *refs):
    weight_refs, (out_hbm, out_ref, stored) = refs[:-3], refs[-3:]
    sums = rounded_sums(group, windows_ref, weight_refs)
    half, copies = out_ref.shape[0] // 2, []
    for place in range(2):
        cut = slice(place * half, (place + 1) * half)
        out_ref[cut, :] = (early_ref[cut, :].astype(F32) + dot(sums[cut], chosen_ref[...])).astype(BF16)
        copies.append(pltpu.make_async_copy(out_ref.at[cut, :], out_hbm.at[cut, :], stored.at[place]))
        copies[-1].start()
    for copy in copies:
        copy.wait()


def reversed_taps(blocks):
    rows, half = blocks[0].shape
    far = dot(jnp.concatenate(blocks, axis=0), anti_identity(half)).astype(BF16)
    far = dot(anti_identity(len(blocks) * rows), far)
    return [far[k * rows : (k + 1) * rows] for k in range(len(blocks))]


def tied_kernel(own_ref, far_ref, out_ref):
    taps, rows, width = far_ref.shape
    half = width // 2
    for place, near_ref, other_ref in ((0, own_ref, far_ref), (1, far_ref, own_ref)):
        other = reversed_taps([other_ref[k, :, half:] for k in range(taps)])
        for k in range(taps):
            out_ref[place * rows : (place + 1) * rows, k * half : (k + 1) * half] = (
                near_ref[k, :, :half].astype(F32) + other[k]
            ).astype(BF16)


def finish_kernel(own_ref, got_ref, out_ref):
    taps, rows, width = out_ref.shape
    half = width // 2
    cuts = [slice(k * half, (k + 1) * half) for k in range(taps)]
    far = own_ref[rows:, :] + got_ref[:rows, :].astype(F32)
    high = far.astype(BF16)
    low = (far - high.astype(F32)).astype(BF16)
    high, low = (reversed_taps([part[:, cut] for cut in cuts]) for part in (high, low))
    near = own_ref[:rows, :] + got_ref[rows:, :].astype(F32)
    for k, cut in enumerate(cuts):
        out_ref[k, :, :half] = near[:, cut]
        out_ref[k, :, half:] = high[k] + low[k]


ON_CHIP = pltpu.VMEM


def call(kernel, outs, args, scalars=0, flops=0, aliases=None, given=(), limit=24, off_chip=(), scratch=()):
    held = pl.BlockSpec(memory_space=ON_CHIP)
    spaces = {i: ON_CHIP for i in given} | {i: pltpu.HBM for i in off_chip}
    args = [pltpu.with_memory_space_constraint(a, spaces[i]) if i in spaces else a for i, a in enumerate(args)]
    result = pl.pallas_call(
        kernel,
        out_shape=[(ON_CHIP if stays else jax.ShapeDtypeStruct)(shape, dtype) for shape, dtype, stays in outs],
        in_specs=[pl.BlockSpec(memory_space=pltpu.SMEM)] * scalars
        + [pl.BlockSpec(memory_space=pltpu.HBM) if i in off_chip else held for i in range(scalars, len(args))],
        scratch_shapes=list(scratch),
        out_specs=[pl.BlockSpec(memory_space=pltpu.HBM) if out[2] is None else held for out in outs],
        input_output_aliases=aliases or {},
        cost_estimate=pl.CostEstimate(
            flops=flops,
            transcendentals=0,
            bytes_accessed=sum(math.prod(out[0]) * jnp.dtype(out[1]).itemsize for out in outs)
            + sum(a.size * a.dtype.itemsize for a in args[scalars:]),
        ),
        compiler_params=pltpu.CompilerParams(vmem_limit_bytes=limit << 20),
    )(*args)
    return result if len(outs) > 1 else result[0]


def edges(block, reach):
    count, where = lax.axis_size("pos"), lax.axis_index("pos")
    top, bottom = block[:, -reach:], block[:, :reach]
    if count == 2:
        got = lax.ppermute(jnp.where(where == 0, top, bottom), "pos", [(0, 1), (1, 0)])
        none = jnp.zeros_like(got)
        low, high = jnp.where(where == 0, none, got), jnp.where(where == 0, got, none)
    else:
        forward = [(i, i + 1) for i in range(count - 1)]
        low = lax.ppermute(top, "pos", forward)
        high = lax.ppermute(bottom, "pos", [(b, a) for a, b in forward])
    return jnp.concatenate([low, high], axis=1)


def on_device(plan, inputs, pre_act, grad_out, weight):
    return both_gradients(plan, inputs, pre_act, grad_out, weight)


def both_gradients(plan, inputs, pre_act, grad_out, weight):
    seqs, length, width = inputs.shape
    rows, taps, _ = weight.shape
    half, reach = width // 2, (taps - 1) // 2
    depth, count = taps * half, seqs * length
    work = 4 * count * depth * half
    device = (lax.axis_index("dp") * plan.pos + lax.axis_index("pos")).astype(jnp.int32).reshape(1)

    by_tap = jnp.transpose(weight, (1, 0, 2))
    far_weight = plan.complement(by_tap)
    ends = jnp.concatenate(
        [grad_pre_of(pre_act[:, :reach], grad_out[:, :reach]), grad_pre_of(pre_act[:, -reach:], grad_out[:, -reach:])],
        axis=1,
    )
    halo = edges(ends, reach)
    first_order, second_order, padded, windows = call(
        functools.partial(prepare_kernel, plan, rows, taps),
        [((half, 2 * count), BF16, True)] * 2
        + [((2 * seqs, length + 2 * EDGE, half), F32, True), ((2 * count, depth), BF16, True)],
        (device, inputs.reshape(count, width), pre_act, grad_out),
        scalars=1, flops=4 * count * width * width, off_chip=(1, 2, 3),
        scratch=(
            pltpu.VMEM((count, width), BF16), pltpu.VMEM((seqs, length, width), BF16),
            pltpu.VMEM((seqs, length, width), BF16), pltpu.SemaphoreType.DMA((3,)),
        ),
    )
    sums = [((half // 2, depth), BF16, True), ((half // 2, depth), F32, True)]
    sent, kept, _, windows = call(
        functools.partial(first_sums_kernel, taps),
        sums + [(padded.shape, F32, True), (windows.shape, BF16, True)],
        (first_order, halo, padded, windows), flops=work, aliases={2: 2, 3: 3}, given=(0, 1, 2, 3),
    )
    received = plan.swap(sent, "core")
    second_sent, second_kept = call(sums_kernel, sums, (second_order, windows), flops=work, given=(0, 1))
    received = plan.swap((kept + received.astype(F32)).astype(BF16), "a")
    kept = second_kept + plan.swap(second_sent, "core").astype(F32)
    middle = kept.shape[0] // 2
    sent = (kept[middle:] + received[middle:].astype(F32)).astype(BF16)
    kept = kept[:middle] + received[:middle].astype(F32)
    received = plan.swap(sent, "b")
    for place, group in enumerate(plan.groups):
        if place == 0:
            kept = kept + received.astype(F32)
        masks = plan.group_masks(group)
        size = kept.shape[0] // len(masks)
        pieces = [
            plan.shift(kept[j * size : (j + 1) * size].astype(BF16), masks[j]).astype(F32)
            for j in range(1, len(masks))
        ]
        kept = functools.reduce(jnp.add, pieces, kept[:size])
    got = plan.complement(kept.astype(BF16))
    grad_weight = jnp.transpose(
        call(
            finish_kernel, [((taps, rows, width), F32, False)], (kept, got),
            flops=4 * rows * depth * half, given=(0, 1),
        ),
        (1, 0, 2),
    )

    gathered = call(
        tied_kernel, [((2 * rows, depth), BF16, True)], (by_tap, far_weight),
        flops=4 * rows * depth * half, given=(1,),
    )
    for place, group in reversed(list(enumerate(plan.groups))):
        gathered = jnp.concatenate([gathered] + [plan.shift(gathered, m) for m in plan.group_masks(group)[1:]], axis=0)
    size = gathered.shape[0]
    relayed = plan.swap(gathered, "b")
    late = [plan.swap(gathered, "a")]
    late.append(plan.swap(relayed, "a"))
    gathered = jnp.concatenate([gathered, relayed], axis=0)
    other = plan.swap(gathered, "core")
    for place in range(2):
        late.append(plan.swap(late[place], "core"))
    begins = (2 * size, 3 * size, 6 * size, 7 * size)
    early, chosen = call(
        functools.partial(early_input_kernel, plan, rows, (0, 4 * size), begins),
        [((count, width), BF16, True), ((half, width), BF16, True)], (device, windows, gathered, other),
        scalars=1, flops=work, given=(1, 2, 3),
    )
    grad_input = call(
        functools.partial(late_input_kernel, 2 * rows),
        [((count, width), BF16, None)], (windows, early, chosen, *late),
        flops=work, given=range(7),
        scratch=(pltpu.VMEM((count, width), BF16), pltpu.SemaphoreType.DMA((2,))),
    ).reshape(seqs, length, width)
    return grad_input, grad_weight


def solution(mesh):
    plan = Plan(mesh.shape["dp"], mesh.shape["pos"])
    placed = (
        P("dp", "pos", None),
        P("dp", "pos", None),
        P("dp", "pos", None),
        P(("dp", "pos"), None, None),
    )
    return jax.shard_map(
        functools.partial(on_device, plan),
        mesh=mesh,
        in_specs=placed,
        out_specs=(P("dp", "pos", None), P(("dp", "pos"), None, None)),
        check_vma=False,
    )
```

```python
import functools
import math

import jax
import jax.numpy as jnp
from jax import lax
from jax.experimental import pallas as pl
from jax.experimental.pallas import tpu as pltpu
from jax.sharding import PartitionSpec as P


AXES = ("dp", "pos")
F32 = jnp.float32
BF16 = jnp.bfloat16
NT = (((1,), (1,)), ((), ()))


def gelu_slope(values):
    cdf = 0.5 * (1.0 + lax.erf(values * 0.7071067811865476))
    return cdf + values * jnp.exp(-0.5 * values * values) * 0.3989422804014327


def grad_pre_of(pre_act, grad_out):
    return (grad_out.astype(F32) * gelu_slope(pre_act.astype(F32))).astype(BF16)


class Plan:
    def __init__(self, dp, pos):
        self.dp, self.pos, self.count = dp, pos, dp * pos
        assert self.count & (self.count - 1) == 0
        dp_bits = [pos << b for b in range(dp.bit_length() - 1)]
        pos_bits = [1 << b for b in range(pos.bit_length() - 1)]
        self.core = dp_bits[0]
        self.cross = (dp_bits[1], pos_bits[0])
        rest = (dp_bits[2:] + pos_bits[1:])[:-1]
        self.groups = [rest[i : i + 2] for i in range(0, len(rest), 2)]

    def mask(self, device, stage):
        if stage == "core":
            return self.core
        parity = 1 if device & self.core else 0
        return self.cross[parity if stage == "a" else 1 - parity]

    def swap(self, block, stage):
        route = [(d, d ^ self.mask(d, stage)) for d in range(self.count)]
        return lax.ppermute(block, AXES, route)

    def group_masks(self, group):
        masks = [0]
        for bit in group:
            masks += [m | bit for m in masks]
        return masks

    def shift(self, block, mask):
        return lax.ppermute(block, AXES, [(d, d ^ mask) for d in range(self.count)])

    def complement(self, block):
        return self.shift(block, self.count - 1)

    def source(self, position, device, rows):
        shift = rows.bit_length() - 1
        slot, low = position >> shift, position & (rows - 1)
        bit = self.count.bit_length() - 2
        flag = (slot >> bit) & 1
        owner = device ^ (flag * self.core)
        parity = jnp.where((owner & self.core) != 0, 1, 0)
        first = parity * self.cross[1] + (1 - parity) * self.cross[0]
        second = parity * self.cross[0] + (1 - parity) * self.cross[1]
        owner = owner ^ (((slot >> (bit - 1)) & 1) * first)
        owner = owner ^ (((slot >> (bit - 2)) & 1) * second)
        bit -= 3
        for group in self.groups:
            for mask in reversed(group):
                owner = owner ^ (((slot >> bit) & 1) * mask)
                bit -= 1
        owner = owner ^ ((slot & 1) * (self.count - 1))
        return (owner << shift) + low


def anti_identity(size):
    row = lax.broadcasted_iota(jnp.int32, (size, size), 0)
    col = lax.broadcasted_iota(jnp.int32, (size, size), 1)
    return jnp.where(row + col == size - 1, 1.0, 0.0).astype(BF16)


def selection(plan, device, rows, width):
    position = lax.broadcasted_iota(jnp.int32, (width, 128), 0)
    lane = lax.broadcasted_iota(jnp.int32, (width, 128), 1)
    source = plan.source(position, device, rows)

    def one_hot(index):
        return jnp.concatenate(
            [jnp.where(index == lane + start, 1.0, 0.0).astype(BF16) for start in range(0, width, 128)],
            axis=1,
        )

    return one_hot(source), one_hot(width - 1 - source)


def dot(left, right, dims=(((1,), (0,)), ((), ()))):
    return lax.dot_general(left, right, dims, preferred_element_type=F32)


EDGE = 8


def window_start(strand, tap, taps):
    reach = (taps - 1) // 2
    return EDGE + reach - tap if strand == 0 else EDGE - reach + tap


def prepare_kernel(
    plan, rows, taps, device_ref, values_hbm, pre_hbm, out_grad_hbm,
    first_ref, second_ref, padded_ref, windows_ref,
    values_ref, pre_ref, out_grad_ref, arrived,
):
    seqs, length, width = pre_ref.shape
    half, count = width // 2, seqs * length
    pairs = ((pre_hbm, pre_ref), (out_grad_hbm, out_grad_ref), (values_hbm, values_ref))
    copies = [pltpu.make_async_copy(far, near, arrived.at[i]) for i, (far, near) in enumerate(pairs)]
    for copy in copies:
        copy.start()
    direct, mirror = selection(plan, device_ref[0], rows, width)
    for copy in copies:
        copy.wait()
    values = values_ref[...]
    quarter = width // 4
    for chosen, cols in ((direct, slice(0, count)), (mirror, slice(count, 2 * count))):
        ordered = dot(chosen, values, NT).astype(BF16)
        for out_ref, begins in ((first_ref, (3, 1)), (second_ref, (2, 0))):
            for place, begin in enumerate(begins):
                out_ref[place * quarter : (place + 1) * quarter, cols] = ordered[begin * quarter : (begin + 1) * quarter]
    flip = anti_identity(half)
    for b in range(seqs):
        grads = grad_pre_of(pre_ref[b], out_grad_ref[b])
        for strand in range(2):
            place = strand * seqs + b
            inner = grads[:, :half].astype(F32) if strand == 0 else dot(grads[:, half:], flip)
            padded_ref[place, :EDGE, :] = jnp.zeros((EDGE, half), F32)
            padded_ref[place, EDGE + length :, :] = jnp.zeros((EDGE, half), F32)
            padded_ref[place, EDGE : EDGE + length, :] = inner
            for tap in range(taps):
                start = window_start(strand, tap, taps)
                windows_ref[place * length : (place + 1) * length, tap * half : (tap + 1) * half] = (
                    padded_ref[place, start : start + length, :].astype(BF16)
                )


def first_sums_kernel(taps, order_ref, halo_ref, _, __, sent_ref, kept_ref, padded_ref, windows_ref):
    seqs, both, width = halo_ref.shape
    half, reach = width // 2, both // 2
    length = padded_ref.shape[1] - 2 * EDGE
    strip = 16
    flip = anti_identity(half)
    for b in range(seqs):
        for strand in range(2):
            place = strand * seqs + b
            edge = halo_ref[b]
            outer = edge[:, :half].astype(F32) if strand == 0 else dot(edge[:, half:], flip)
            padded_ref[place, EDGE - reach : EDGE, :] = outer[:reach]
            padded_ref[place, EDGE + length : EDGE + length + reach, :] = outer[reach:]
            for tap in range(taps):
                start = window_start(strand, tap, taps)
                for begin in (0, length - strip):
                    windows_ref[
                        place * length + begin : place * length + begin + strip, tap * half : (tap + 1) * half
                    ] = padded_ref[place, start + begin : start + begin + strip, :].astype(BF16)
    sums_kernel(order_ref, windows_ref, sent_ref, kept_ref)


def sums_kernel(order_ref, windows_ref, sent_ref, kept_ref):
    sums = dot(order_ref[...], windows_ref[...])
    size = sent_ref.shape[0]
    sent_ref[...] = sums[:size].astype(BF16)
    kept_ref[...] = sums[size:]


def rounded_sums(group, windows_ref, weight_refs):
    count = windows_ref.shape[0] // 2
    weights = jnp.concatenate([ref[...] for ref in weight_refs], axis=0)
    size = weights.shape[0]
    row = lax.broadcasted_iota(jnp.int32, (size, size), 0)
    col = lax.broadcasted_iota(jnp.int32, (size, size), 1)
    turn = jnp.where(row == (col ^ (group - 1)), 1.0, 0.0).astype(BF16)
    mirrored = dot(turn, weights).astype(BF16)
    return (dot(windows_ref[:count, :], weights, NT) + dot(windows_ref[count:, :], mirrored, NT)).astype(BF16)


def chosen_rows(direct, weight_refs, begins):
    return jnp.concatenate([direct[a : a + ref.shape[0], :] for ref, a in zip(weight_refs, begins)], axis=0)


def early_input_kernel(plan, rows, begins, late_begins, device_ref, windows_ref, own_ref, other_ref, out_ref, late_ref):
    refs = (own_ref, other_ref)
    direct, _ = selection(plan, device_ref[0], rows, out_ref.shape[1])
    out_ref[...] = dot(rounded_sums(2 * rows, windows_ref, refs), chosen_rows(direct, refs, begins)).astype(BF16)
    size = late_ref.shape[0] // len(late_begins)
    for place, begin in enumerate(late_begins):
        late_ref[place * size : (place + 1) * size, :] = direct[begin : begin + size, :]


def late_input_kernel(group, windows_ref, early_ref, chosen_ref, *refs):
    weight_refs, (out_hbm, out_ref, stored) = refs[:-3], refs[-3:]
    sums = rounded_sums(group, windows_ref, weight_refs)
    half, copies = out_ref.shape[0] // 2, []
    for place in range(2):
        cut = slice(place * half, (place + 1) * half)
        out_ref[cut, :] = (early_ref[cut, :].astype(F32) + dot(sums[cut], chosen_ref[...])).astype(BF16)
        copies.append(pltpu.make_async_copy(out_ref.at[cut, :], out_hbm.at[cut, :], stored.at[place]))
        copies[-1].start()
    for copy in copies:
        copy.wait()


def reversed_taps(blocks):
    rows, half = blocks[0].shape
    far = dot(jnp.concatenate(blocks, axis=0), anti_identity(half)).astype(BF16)
    far = dot(anti_identity(len(blocks) * rows), far)
    return [far[k * rows : (k + 1) * rows] for k in range(len(blocks))]


def tied_kernel(own_ref, far_ref, out_ref):
    taps, rows, width = far_ref.shape
    half = width // 2
    for place, near_ref, other_ref in ((0, own_ref, far_ref), (1, far_ref, own_ref)):
        other = reversed_taps([other_ref[k, :, half:] for k in range(taps)])
        for k in range(taps):
            out_ref[place * rows : (place + 1) * rows, k * half : (k + 1) * half] = (
                near_ref[k, :, :half].astype(F32) + other[k]
            ).astype(BF16)


def finish_kernel(own_ref, got_ref, out_ref):
    taps, rows, width = out_ref.shape
    half = width // 2
    cuts = [slice(k * half, (k + 1) * half) for k in range(taps)]
    far = own_ref[rows:, :] + got_ref[:rows, :].astype(F32)
    high = far.astype(BF16)
    low = (far - high.astype(F32)).astype(BF16)
    high, low = (reversed_taps([part[:, cut] for cut in cuts]) for part in (high, low))
    near = own_ref[:rows, :] + got_ref[rows:, :].astype(F32)
    for k, cut in enumerate(cuts):
        out_ref[k, :, :half] = near[:, cut]
        out_ref[k, :, half:] = high[k] + low[k]


ON_CHIP = pltpu.VMEM


def call(kernel, outs, args, scalars=0, flops=0, aliases=None, given=(), limit=24, off_chip=(), scratch=()):
    held = pl.BlockSpec(memory_space=ON_CHIP)
    spaces = {i: ON_CHIP for i in given} | {i: pltpu.HBM for i in off_chip}
    args = [pltpu.with_memory_space_constraint(a, spaces[i]) if i in spaces else a for i, a in enumerate(args)]
    result = pl.pallas_call(
        kernel,
        out_shape=[(ON_CHIP if stays else jax.ShapeDtypeStruct)(shape, dtype) for shape, dtype, stays in outs],
        in_specs=[pl.BlockSpec(memory_space=pltpu.SMEM)] * scalars
        + [pl.BlockSpec(memory_space=pltpu.HBM) if i in off_chip else held for i in range(scalars, len(args))],
        scratch_shapes=list(scratch),
        out_specs=[pl.BlockSpec(memory_space=pltpu.HBM) if out[2] is None else held for out in outs],
        input_output_aliases=aliases or {},
        cost_estimate=pl.CostEstimate(
            flops=flops,
            transcendentals=0,
            bytes_accessed=sum(math.prod(out[0]) * jnp.dtype(out[1]).itemsize for out in outs)
            + sum(a.size * a.dtype.itemsize for a in args[scalars:]),
        ),
        compiler_params=pltpu.CompilerParams(vmem_limit_bytes=limit << 20),
    )(*args)
    return result if len(outs) > 1 else result[0]


def edges(block, reach):
    count, where = lax.axis_size("pos"), lax.axis_index("pos")
    top, bottom = block[:, -reach:], block[:, :reach]
    if count == 2:
        got = lax.ppermute(jnp.where(where == 0, top, bottom), "pos", [(0, 1), (1, 0)])
        none = jnp.zeros_like(got)
        low, high = jnp.where(where == 0, none, got), jnp.where(where == 0, got, none)
    else:
        forward = [(i, i + 1) for i in range(count - 1)]
        low = lax.ppermute(top, "pos", forward)
        high = lax.ppermute(bottom, "pos", [(b, a) for a, b in forward])
    return jnp.concatenate([low, high], axis=1)


def on_device(plan, inputs, pre_act, grad_out, weight):
    return both_gradients(plan, inputs, pre_act, grad_out, weight)


def both_gradients(plan, inputs, pre_act, grad_out, weight):
    seqs, length, width = inputs.shape
    rows, taps, _ = weight.shape
    half, reach = width // 2, (taps - 1) // 2
    depth, count = taps * half, seqs * length
    work = 4 * count * depth * half
    device = (lax.axis_index("dp") * plan.pos + lax.axis_index("pos")).astype(jnp.int32).reshape(1)

    by_tap = jnp.transpose(weight, (1, 0, 2))
    far_weight = plan.complement(by_tap)
    ends = jnp.concatenate(
        [grad_pre_of(pre_act[:, :reach], grad_out[:, :reach]), grad_pre_of(pre_act[:, -reach:], grad_out[:, -reach:])],
        axis=1,
    )
    halo = edges(ends, reach)
    first_order, second_order, padded, windows = call(
        functools.partial(prepare_kernel, plan, rows, taps),
        [((half, 2 * count), BF16, True)] * 2
        + [((2 * seqs, length + 2 * EDGE, half), F32, True), ((2 * count, depth), BF16, True)],
        (device, inputs.reshape(count, width), pre_act, grad_out),
        scalars=1, flops=4 * count * width * width, off_chip=(1, 2, 3),
        scratch=(
            pltpu.VMEM((count, width), BF16), pltpu.VMEM((seqs, length, width), BF16),
            pltpu.VMEM((seqs, length, width), BF16), pltpu.SemaphoreType.DMA((3,)),
        ),
    )
    sums = [((half // 2, depth), BF16, True), ((half // 2, depth), F32, True)]
    sent, kept, _, windows = call(
        functools.partial(first_sums_kernel, taps),
        sums + [(padded.shape, F32, True), (windows.shape, BF16, True)],
        (first_order, halo, padded, windows), flops=work, aliases={2: 2, 3: 3}, given=(0, 1, 2, 3),
    )
    received = plan.swap(sent, "core")
    second_sent, second_kept = call(sums_kernel, sums, (second_order, windows), flops=work, given=(0, 1))
    received = plan.swap((kept + received.astype(F32)).astype(BF16), "a")
    kept = second_kept + plan.swap(second_sent, "core").astype(F32)
    middle = kept.shape[0] // 2
    sent = (kept[middle:] + received[middle:].astype(F32)).astype(BF16)
    kept = kept[:middle] + received[:middle].astype(F32)
    received = plan.swap(sent, "b")
    for place, group in enumerate(plan.groups):
        if place == 0:
            kept = kept + received.astype(F32)
        masks = plan.group_masks(group)
        size = kept.shape[0] // len(masks)
        pieces = [
            plan.shift(kept[j * size : (j + 1) * size].astype(BF16), masks[j]).astype(F32)
            for j in range(1, len(masks))
        ]
        kept = functools.reduce(jnp.add, pieces, kept[:size])
    got = plan.complement(kept.astype(BF16))
    grad_weight = jnp.transpose(
        call(
            finish_kernel, [((taps, rows, width), F32, False)], (kept, got),
            flops=4 * rows * depth * half, given=(0, 1),
        ),
        (1, 0, 2),
    )

    gathered = call(
        tied_kernel, [((2 * rows, depth), BF16, True)], (by_tap, far_weight),
        flops=4 * rows * depth * half, given=(1,),
    )
    for place, group in reversed(list(enumerate(plan.groups))):
        gathered = jnp.concatenate([gathered] + [plan.shift(gathered, m) for m in plan.group_masks(group)[1:]], axis=0)
    size = gathered.shape[0]
    relayed = plan.swap(gathered, "b")
    late = [plan.swap(gathered, "a")]
    late.append(plan.swap(relayed, "a"))
    gathered = jnp.concatenate([gathered, relayed], axis=0)
    other = plan.swap(gathered, "core")
    for place in range(2):
        late.append(plan.swap(late[place], "core"))
    begins = (2 * size, 3 * size, 6 * size, 7 * size)
    early, chosen = call(
        functools.partial(early_input_kernel, plan, rows, (0, 4 * size), begins),
        [((count, width), BF16, True), ((half, width), BF16, True)], (device, windows, gathered, other),
        scalars=1, flops=work, given=(1, 2, 3),
    )
    grad_input = call(
        functools.partial(late_input_kernel, 2 * rows),
        [((count, width), BF16, None)], (windows, early, chosen, *late),
        flops=work, given=range(7),
        scratch=(pltpu.VMEM((count, width), BF16), pltpu.SemaphoreType.DMA((2,))),
    ).reshape(seqs, length, width)
    return grad_input, grad_weight


def solution(mesh):
    plan = Plan(mesh.shape["dp"], mesh.shape["pos"])
    placed = (
        P("dp", "pos", None),
        P("dp", "pos", None),
        P("dp", "pos", None),
        P(("dp", "pos"), None, None),
    )
    return jax.shard_map(
        functools.partial(on_device, plan),
        mesh=mesh,
        in_specs=placed,
        out_specs=(P("dp", "pos", None), P(("dp", "pos"), None, None)),
        check_vma=False,
    )
```

```python
import functools
import math

import jax
import jax.numpy as jnp
from jax import lax
from jax.experimental import pallas as pl
from jax.experimental.pallas import tpu as pltpu
from jax.sharding import PartitionSpec as P


AXES = ("dp", "pos")
F32 = jnp.float32
BF16 = jnp.bfloat16
NT = (((1,), (1,)), ((), ()))


def gelu_slope(values):
    cdf = 0.5 * (1.0 + lax.erf(values * 0.7071067811865476))
    return cdf + values * jnp.exp(-0.5 * values * values) * 0.3989422804014327


def grad_pre_of(pre_act, grad_out):
    return (grad_out.astype(F32) * gelu_slope(pre_act.astype(F32))).astype(BF16)


class Plan:
    def __init__(self, dp, pos):
        self.dp, self.pos, self.count = dp, pos, dp * pos
        assert self.count & (self.count - 1) == 0
        dp_bits = [pos << b for b in range(dp.bit_length() - 1)]
        pos_bits = [1 << b for b in range(pos.bit_length() - 1)]
        self.core = dp_bits[0]
        self.cross = (dp_bits[1], pos_bits[0])
        rest = (dp_bits[2:] + pos_bits[1:])[:-1]
        self.groups = [rest[i : i + 2] for i in range(0, len(rest), 2)]

    def mask(self, device, stage):
        if stage == "core":
            return self.core
        parity = 1 if device & self.core else 0
        return self.cross[parity if stage == "a" else 1 - parity]

    def swap(self, block, stage):
        route = [(d, d ^ self.mask(d, stage)) for d in range(self.count)]
        return lax.ppermute(block, AXES, route)

    def group_masks(self, group):
        masks = [0]
        for bit in group:
            masks += [m | bit for m in masks]
        return masks

    def shift(self, block, mask):
        return lax.ppermute(block, AXES, [(d, d ^ mask) for d in range(self.count)])

    def complement(self, block):
        return self.shift(block, self.count - 1)

    def source(self, position, device, rows, turns):
        shift = rows.bit_length() - 1
        slot, low = position >> shift, position & (rows - 1)
        bit = self.count.bit_length() - 2
        owner = device
        for turn in turns:
            if turn == "rest":
                masks = [mask for group in self.groups for mask in reversed(group)]
            elif turn == "core":
                masks = [self.core]
            elif turn == "mirror":
                masks = [self.count - 1]
            else:
                odd = jnp.where((owner & self.core) != 0, 1, 0)
                odd = odd if turn == "a" else 1 - odd
                masks = [odd * self.cross[1] + (1 - odd) * self.cross[0]]
            for mask in masks:
                owner = owner ^ (((slot >> bit) & 1) * mask)
                bit -= 1
        return (owner << shift) + low


SUM_TURNS = ("core", "a", "b", "rest", "mirror")
GET_TURNS = ("core", "a", "rest", "b", "mirror")


def anti_identity(size):
    row = lax.broadcasted_iota(jnp.int32, (size, size), 0)
    col = lax.broadcasted_iota(jnp.int32, (size, size), 1)
    return jnp.where(row + col == size - 1, 1.0, 0.0).astype(BF16)


def selection(plan, device, rows, width, turns):
    position = lax.broadcasted_iota(jnp.int32, (width, 128), 0)
    lane = lax.broadcasted_iota(jnp.int32, (width, 128), 1)
    source = plan.source(position, device, rows, turns)

    def one_hot(index):
        return jnp.concatenate(
            [jnp.where(index == lane + start, 1.0, 0.0).astype(BF16) for start in range(0, width, 128)],
            axis=1,
        )

    return one_hot(source), one_hot(width - 1 - source)


def dot(left, right, dims=(((1,), (0,)), ((), ()))):
    return lax.dot_general(left, right, dims, preferred_element_type=F32)


EDGE = 8


def window_start(strand, tap, taps):
    reach = (taps - 1) // 2
    return EDGE + reach - tap if strand == 0 else EDGE - reach + tap


def prepare_kernel(
    plan, rows, taps, device_ref, values_hbm, pre_hbm, out_grad_hbm,
    first_ref, second_ref, padded_ref, windows_ref,
    values_ref, pre_ref, out_grad_ref, arrived,
):
    seqs, length, width = pre_ref.shape
    half, count = width // 2, seqs * length
    pairs = ((pre_hbm, pre_ref), (out_grad_hbm, out_grad_ref), (values_hbm, values_ref))
    copies = [pltpu.make_async_copy(far, near, arrived.at[i]) for i, (far, near) in enumerate(pairs)]
    for copy in copies:
        copy.start()
    direct, mirror = selection(plan, device_ref[0], rows, width, SUM_TURNS)
    for copy in copies:
        copy.wait()
    values = values_ref[...]
    quarter = width // 4
    for chosen, cols in ((direct, slice(0, count)), (mirror, slice(count, 2 * count))):
        ordered = dot(chosen, values, NT).astype(BF16)
        for out_ref, begins in ((first_ref, (3, 1)), (second_ref, (2, 0))):
            for place, begin in enumerate(begins):
                out_ref[place * quarter : (place + 1) * quarter, cols] = ordered[begin * quarter : (begin + 1) * quarter]
    flip = anti_identity(half)
    for b in range(seqs):
        grads = grad_pre_of(pre_ref[b], out_grad_ref[b])
        for strand in range(2):
            place = strand * seqs + b
            inner = grads[:, :half].astype(F32) if strand == 0 else dot(grads[:, half:], flip)
            padded_ref[place, :EDGE, :] = jnp.zeros((EDGE, half), F32)
            padded_ref[place, EDGE + length :, :] = jnp.zeros((EDGE, half), F32)
            padded_ref[place, EDGE : EDGE + length, :] = inner
            for tap in range(taps):
                start = window_start(strand, tap, taps)
                windows_ref[place * length : (place + 1) * length, tap * half : (tap + 1) * half] = (
                    padded_ref[place, start : start + length, :].astype(BF16)
                )


def first_sums_kernel(taps, order_ref, halo_ref, _, __, sent_ref, kept_ref, padded_ref, windows_ref):
    seqs, both, width = halo_ref.shape
    half, reach = width // 2, both // 2
    length = padded_ref.shape[1] - 2 * EDGE
    strip = 16
    flip = anti_identity(half)
    for b in range(seqs):
        for strand in range(2):
            place = strand * seqs + b
            edge = halo_ref[b]
            outer = edge[:, :half].astype(F32) if strand == 0 else dot(edge[:, half:], flip)
            padded_ref[place, EDGE - reach : EDGE, :] = outer[:reach]
            padded_ref[place, EDGE + length : EDGE + length + reach, :] = outer[reach:]
            for tap in range(taps):
                start = window_start(strand, tap, taps)
                for begin in (0, length - strip):
                    windows_ref[
                        place * length + begin : place * length + begin + strip, tap * half : (tap + 1) * half
                    ] = padded_ref[place, start + begin : start + begin + strip, :].astype(BF16)
    sums_kernel(order_ref, windows_ref, sent_ref, kept_ref)


def sums_kernel(order_ref, windows_ref, sent_ref, kept_ref):
    sums = dot(order_ref[...], windows_ref[...])
    size = sent_ref.shape[0]
    sent_ref[...] = sums[:size].astype(BF16)
    kept_ref[...] = sums[size:]


def rounded_sums(group, windows_ref, weight_refs):
    count = windows_ref.shape[0] // 2
    weights = jnp.concatenate([ref[...] for ref in weight_refs], axis=0)
    size = weights.shape[0]
    row = lax.broadcasted_iota(jnp.int32, (size, size), 0)
    col = lax.broadcasted_iota(jnp.int32, (size, size), 1)
    turn = jnp.where(row == (col ^ (group - 1)), 1.0, 0.0).astype(BF16)
    mirrored = dot(turn, weights).astype(BF16)
    return (dot(windows_ref[:count, :], weights, NT) + dot(windows_ref[count:, :], mirrored, NT)).astype(BF16)


def chosen_rows(direct, weight_refs, begins):
    return jnp.concatenate([direct[a : a + ref.shape[0], :] for ref, a in zip(weight_refs, begins)], axis=0)


def early_input_kernel(plan, rows, begins, late_begins, device_ref, windows_ref, own_ref, other_ref, out_ref, late_ref):
    refs = (own_ref, other_ref)
    direct, _ = selection(plan, device_ref[0], rows, out_ref.shape[1], GET_TURNS)
    out_ref[...] = dot(rounded_sums(2 * rows, windows_ref, refs), chosen_rows(direct, refs, begins)).astype(BF16)
    place = 0
    for begin, size in late_begins:
        late_ref[place : place + size, :] = direct[begin : begin + size, :]
        place += size


def late_input_kernel(group, windows_ref, early_ref, chosen_ref, *refs):
    weight_refs, (out_hbm, out_ref, stored) = refs[:-3], refs[-3:]
    sums = rounded_sums(group, windows_ref, weight_refs)
    half, copies = out_ref.shape[0] // 2, []
    for place in range(2):
        cut = slice(place * half, (place + 1) * half)
        out_ref[cut, :] = (early_ref[cut, :].astype(F32) + dot(sums[cut], chosen_ref[...])).astype(BF16)
        copies.append(pltpu.make_async_copy(out_ref.at[cut, :], out_hbm.at[cut, :], stored.at[place]))
        copies[-1].start()
    for copy in copies:
        copy.wait()


def reversed_taps(blocks):
    rows, half = blocks[0].shape
    far = dot(jnp.concatenate(blocks, axis=0), anti_identity(half)).astype(BF16)
    far = dot(anti_identity(len(blocks) * rows), far)
    return [far[k * rows : (k + 1) * rows] for k in range(len(blocks))]


def tied_kernel(own_ref, far_ref, out_ref):
    taps, rows, width = far_ref.shape
    half = width // 2
    for place, near_ref, other_ref in ((0, own_ref, far_ref), (1, far_ref, own_ref)):
        other = reversed_taps([other_ref[k, :, half:] for k in range(taps)])
        for k in range(taps):
            out_ref[place * rows : (place + 1) * rows, k * half : (k + 1) * half] = (
                near_ref[k, :, :half].astype(F32) + other[k]
            ).astype(BF16)


def finish_kernel(own_ref, got_ref, out_ref):
    taps, rows, width = out_ref.shape
    half = width // 2
    cuts = [slice(k * half, (k + 1) * half) for k in range(taps)]
    far = own_ref[rows:, :] + got_ref[:rows, :].astype(F32)
    high = far.astype(BF16)
    low = (far - high.astype(F32)).astype(BF16)
    high, low = (reversed_taps([part[:, cut] for cut in cuts]) for part in (high, low))
    near = own_ref[:rows, :] + got_ref[rows:, :].astype(F32)
    for k, cut in enumerate(cuts):
        out_ref[k, :, :half] = near[:, cut]
        out_ref[k, :, half:] = high[k] + low[k]


ON_CHIP = pltpu.VMEM


def call(kernel, outs, args, scalars=0, flops=0, aliases=None, given=(), limit=24, off_chip=(), scratch=()):
    held = pl.BlockSpec(memory_space=ON_CHIP)
    spaces = {i: ON_CHIP for i in given} | {i: pltpu.HBM for i in off_chip}
    args = [pltpu.with_memory_space_constraint(a, spaces[i]) if i in spaces else a for i, a in enumerate(args)]
    result = pl.pallas_call(
        kernel,
        out_shape=[(ON_CHIP if stays else jax.ShapeDtypeStruct)(shape, dtype) for shape, dtype, stays in outs],
        in_specs=[pl.BlockSpec(memory_space=pltpu.SMEM)] * scalars
        + [pl.BlockSpec(memory_space=pltpu.HBM) if i in off_chip else held for i in range(scalars, len(args))],
        scratch_shapes=list(scratch),
        out_specs=[pl.BlockSpec(memory_space=pltpu.HBM) if out[2] is None else held for out in outs],
        input_output_aliases=aliases or {},
        cost_estimate=pl.CostEstimate(
            flops=flops,
            transcendentals=0,
            bytes_accessed=sum(math.prod(out[0]) * jnp.dtype(out[1]).itemsize for out in outs)
            + sum(a.size * a.dtype.itemsize for a in args[scalars:]),
        ),
        compiler_params=pltpu.CompilerParams(vmem_limit_bytes=limit << 20),
    )(*args)
    return result if len(outs) > 1 else result[0]


def edges(block, reach):
    count, where = lax.axis_size("pos"), lax.axis_index("pos")
    top, bottom = block[:, -reach:], block[:, :reach]
    if count == 2:
        got = lax.ppermute(jnp.where(where == 0, top, bottom), "pos", [(0, 1), (1, 0)])
        none = jnp.zeros_like(got)
        low, high = jnp.where(where == 0, none, got), jnp.where(where == 0, got, none)
    else:
        forward = [(i, i + 1) for i in range(count - 1)]
        low = lax.ppermute(top, "pos", forward)
        high = lax.ppermute(bottom, "pos", [(b, a) for a, b in forward])
    return jnp.concatenate([low, high], axis=1)


def on_device(plan, inputs, pre_act, grad_out, weight):
    return both_gradients(plan, inputs, pre_act, grad_out, weight)


def both_gradients(plan, inputs, pre_act, grad_out, weight):
    seqs, length, width = inputs.shape
    rows, taps, _ = weight.shape
    half, reach = width // 2, (taps - 1) // 2
    depth, count = taps * half, seqs * length
    work = 4 * count * depth * half
    device = (lax.axis_index("dp") * plan.pos + lax.axis_index("pos")).astype(jnp.int32).reshape(1)

    by_tap = jnp.transpose(weight, (1, 0, 2))
    far_weight = plan.complement(by_tap)
    ends = jnp.concatenate(
        [grad_pre_of(pre_act[:, :reach], grad_out[:, :reach]), grad_pre_of(pre_act[:, -reach:], grad_out[:, -reach:])],
        axis=1,
    )
    halo = edges(ends, reach)
    first_order, second_order, padded, windows = call(
        functools.partial(prepare_kernel, plan, rows, taps),
        [((half, 2 * count), BF16, True)] * 2
        + [((2 * seqs, length + 2 * EDGE, half), F32, True), ((2 * count, depth), BF16, True)],
        (device, inputs.reshape(count, width), pre_act, grad_out),
        scalars=1, flops=4 * count * width * width, off_chip=(1, 2, 3),
        scratch=(
            pltpu.VMEM((count, width), BF16), pltpu.VMEM((seqs, length, width), BF16),
            pltpu.VMEM((seqs, length, width), BF16), pltpu.SemaphoreType.DMA((3,)),
        ),
    )
    sums = [((half // 2, depth), BF16, True), ((half // 2, depth), F32, True)]
    sent, kept, _, windows = call(
        functools.partial(first_sums_kernel, taps),
        sums + [(padded.shape, F32, True), (windows.shape, BF16, True)],
        (first_order, halo, padded, windows), flops=work, aliases={2: 2, 3: 3}, given=(0, 1, 2, 3),
    )
    received = plan.swap(sent, "core")
    second_sent, second_kept = call(sums_kernel, sums, (second_order, windows), flops=work, given=(0, 1))
    received = plan.swap((kept + received.astype(F32)).astype(BF16), "a")
    kept = second_kept + plan.swap(second_sent, "core").astype(F32)
    middle = kept.shape[0] // 2
    sent = (kept[middle:] + received[middle:].astype(F32)).astype(BF16)
    kept = kept[:middle] + received[:middle].astype(F32)
    received = plan.swap(sent, "b")
    for place, group in enumerate(plan.groups):
        if place == 0:
            kept = kept + received.astype(F32)
        masks = plan.group_masks(group)
        size = kept.shape[0] // len(masks)
        pieces = [
            plan.shift(kept[j * size : (j + 1) * size].astype(BF16), masks[j]).astype(F32)
            for j in range(1, len(masks))
        ]
        kept = functools.reduce(jnp.add, pieces, kept[:size])
    got = plan.complement(kept.astype(BF16))
    grad_weight = jnp.transpose(
        call(
            finish_kernel, [((taps, rows, width), F32, False)], (kept, got),
            flops=4 * rows * depth * half, given=(0, 1),
        ),
        (1, 0, 2),
    )

    gathered = call(
        tied_kernel, [((2 * rows, depth), BF16, True)], (by_tap, far_weight),
        flops=4 * rows * depth * half, given=(1,),
    )
    gathered = jnp.concatenate([gathered, plan.swap(gathered, "b")], axis=0)
    for place in range(len(plan.groups) - 1, -1, -1):
        pieces = [plan.shift(gathered, mask) for mask in plan.group_masks(plan.groups[place])[1:]]
        if place:
            gathered = jnp.concatenate([gathered] + pieces, axis=0)
        else:
            relayed = jnp.concatenate(pieces, axis=0)
    size = gathered.shape[0]
    late = [plan.swap(gathered, "a")]
    late.append(plan.swap(relayed, "a"))
    gathered = jnp.concatenate([gathered, relayed], axis=0)
    span = gathered.shape[0]
    other = plan.swap(gathered, "core")
    for place in range(2):
        late.append(plan.swap(late[place], "core"))
    late_begins = [(begin, n) for core in (span, 3 * span) for begin, n in ((core, size), (core + size, span - size))]
    early, chosen = call(
        functools.partial(early_input_kernel, plan, rows, (0, 2 * span), late_begins),
        [((count, width), BF16, True), ((half, width), BF16, True)], (device, windows, gathered, other),
        scalars=1, flops=work, given=(1, 2, 3),
    )
    grad_input = call(
        functools.partial(late_input_kernel, 2 * rows),
        [((count, width), BF16, None)], (windows, early, chosen, *late),
        flops=work, given=range(7),
        scratch=(pltpu.VMEM((count, width), BF16), pltpu.SemaphoreType.DMA((2,))),
    ).reshape(seqs, length, width)
    return grad_input, grad_weight


def solution(mesh):
    plan = Plan(mesh.shape["dp"], mesh.shape["pos"])
    placed = (
        P("dp", "pos", None),
        P("dp", "pos", None),
        P("dp", "pos", None),
        P(("dp", "pos"), None, None),
    )
    return jax.shard_map(
        functools.partial(on_device, plan),
        mesh=mesh,
        in_specs=placed,
        out_specs=(P("dp", "pos", None), P(("dp", "pos"), None, None)),
        check_vma=False,
    )
```

```python
import functools
import math

import jax
import jax.numpy as jnp
from jax import lax
from jax.experimental import pallas as pl
from jax.experimental.pallas import tpu as pltpu
from jax.sharding import PartitionSpec as P


AXES = ("dp", "pos")
F32 = jnp.float32
BF16 = jnp.bfloat16
NT = (((1,), (1,)), ((), ()))


def gelu_slope(values):
    cdf = 0.5 * (1.0 + lax.erf(values * 0.7071067811865476))
    return cdf + values * jnp.exp(-0.5 * values * values) * 0.3989422804014327


def grad_pre_of(pre_act, grad_out):
    return (grad_out.astype(F32) * gelu_slope(pre_act.astype(F32))).astype(BF16)


class Plan:
    def __init__(self, dp, pos):
        self.dp, self.pos, self.count = dp, pos, dp * pos
        assert self.count & (self.count - 1) == 0
        dp_bits = [pos << b for b in range(dp.bit_length() - 1)]
        pos_bits = [1 << b for b in range(pos.bit_length() - 1)]
        self.core = dp_bits[0]
        self.cross = (dp_bits[1], pos_bits[0])
        rest = (dp_bits[2:] + pos_bits[1:])[:-1]
        self.groups = [rest[i : i + 2] for i in range(0, len(rest), 2)]

    def mask(self, device, stage):
        if stage == "core":
            return self.core
        parity = 1 if device & self.core else 0
        return self.cross[parity if stage == "a" else 1 - parity]

    def swap(self, block, stage):
        route = [(d, d ^ self.mask(d, stage)) for d in range(self.count)]
        return lax.ppermute(block, AXES, route)

    def group_masks(self, group):
        masks = [0]
        for bit in group:
            masks += [m | bit for m in masks]
        return masks

    def shift(self, block, mask):
        return lax.ppermute(block, AXES, [(d, d ^ mask) for d in range(self.count)])

    def complement(self, block):
        return self.shift(block, self.count - 1)

    def source(self, position, device, rows, turns):
        shift = rows.bit_length() - 1
        slot, low = position >> shift, position & (rows - 1)
        bit = self.count.bit_length() - 2
        owner = device
        for turn in turns:
            if turn == "rest":
                masks = [mask for group in self.groups for mask in reversed(group)]
            elif turn == "core":
                masks = [self.core]
            elif turn == "mirror":
                masks = [self.count - 1]
            else:
                odd = jnp.where((owner & self.core) != 0, 1, 0)
                odd = odd if turn == "a" else 1 - odd
                masks = [odd * self.cross[1] + (1 - odd) * self.cross[0]]
            for mask in masks:
                owner = owner ^ (((slot >> bit) & 1) * mask)
                bit -= 1
        return (owner << shift) + low


SUM_TURNS = ("core", "a", "b", "rest", "mirror")
GET_TURNS = ("core", "a", "rest", "b", "mirror")


def anti_identity(size):
    row = lax.broadcasted_iota(jnp.int32, (size, size), 0)
    col = lax.broadcasted_iota(jnp.int32, (size, size), 1)
    return jnp.where(row + col == size - 1, 1.0, 0.0).astype(BF16)


def selection(plan, device, rows, width, turns):
    position = lax.broadcasted_iota(jnp.int32, (width, 128), 0)
    lane = lax.broadcasted_iota(jnp.int32, (width, 128), 1)
    source = plan.source(position, device, rows, turns)

    def one_hot(index):
        return jnp.concatenate(
            [jnp.where(index == lane + start, 1.0, 0.0).astype(BF16) for start in range(0, width, 128)],
            axis=1,
        )

    return one_hot(source), one_hot(width - 1 - source)


def dot(left, right, dims=(((1,), (0,)), ((), ()))):
    return lax.dot_general(left, right, dims, preferred_element_type=F32)


EDGE = 8


def window_start(strand, tap, taps):
    reach = (taps - 1) // 2
    return EDGE + reach - tap if strand == 0 else EDGE - reach + tap


def prepare_kernel(
    plan, rows, taps, device_ref, values_hbm, pre_hbm, out_grad_hbm,
    first_ref, second_ref, padded_ref, windows_ref,
    values_ref, pre_ref, out_grad_ref, arrived,
):
    seqs, length, width = pre_ref.shape
    half, count = width // 2, seqs * length
    pairs = ((pre_hbm, pre_ref), (out_grad_hbm, out_grad_ref), (values_hbm, values_ref))
    copies = [pltpu.make_async_copy(far, near, arrived.at[i]) for i, (far, near) in enumerate(pairs)]
    for copy in copies:
        copy.start()
    direct, mirror = selection(plan, device_ref[0], rows, width, SUM_TURNS)
    for copy in copies:
        copy.wait()
    values = values_ref[...]
    quarter = width // 4
    for chosen, cols in ((direct, slice(0, count)), (mirror, slice(count, 2 * count))):
        ordered = dot(chosen, values, NT).astype(BF16)
        for out_ref, begins in ((first_ref, (3, 1)), (second_ref, (2, 0))):
            for place, begin in enumerate(begins):
                out_ref[place * quarter : (place + 1) * quarter, cols] = ordered[begin * quarter : (begin + 1) * quarter]
    flip = anti_identity(half)
    for b in range(seqs):
        grads = grad_pre_of(pre_ref[b], out_grad_ref[b])
        for strand in range(2):
            place = strand * seqs + b
            inner = grads[:, :half].astype(F32) if strand == 0 else dot(grads[:, half:], flip)
            padded_ref[place, :EDGE, :] = jnp.zeros((EDGE, half), F32)
            padded_ref[place, EDGE + length :, :] = jnp.zeros((EDGE, half), F32)
            padded_ref[place, EDGE : EDGE + length, :] = inner
            for tap in range(taps):
                start = window_start(strand, tap, taps)
                windows_ref[place * length : (place + 1) * length, tap * half : (tap + 1) * half] = (
                    padded_ref[place, start : start + length, :].astype(BF16)
                )


def first_sums_kernel(taps, order_ref, halo_ref, _, __, sent_ref, kept_ref, padded_ref, windows_ref):
    seqs, both, width = halo_ref.shape
    half, reach = width // 2, both // 2
    length = padded_ref.shape[1] - 2 * EDGE
    strip = 16
    flip = anti_identity(half)
    for b in range(seqs):
        for strand in range(2):
            place = strand * seqs + b
            edge = halo_ref[b]
            outer = edge[:, :half].astype(F32) if strand == 0 else dot(edge[:, half:], flip)
            padded_ref[place, EDGE - reach : EDGE, :] = outer[:reach]
            padded_ref[place, EDGE + length : EDGE + length + reach, :] = outer[reach:]
            for tap in range(taps):
                start = window_start(strand, tap, taps)
                for begin in (0, length - strip):
                    windows_ref[
                        place * length + begin : place * length + begin + strip, tap * half : (tap + 1) * half
                    ] = padded_ref[place, start + begin : start + begin + strip, :].astype(BF16)
    sums_kernel(order_ref, windows_ref, sent_ref, kept_ref)


def sums_kernel(order_ref, windows_ref, sent_ref, kept_ref):
    sums = dot(order_ref[...], windows_ref[...])
    size = sent_ref.shape[0]
    sent_ref[...] = sums[:size].astype(BF16)
    kept_ref[...] = sums[size:]


def rounded_sums(group, windows_ref, weight_refs):
    count = windows_ref.shape[0] // 2
    weights = jnp.concatenate([ref[...] for ref in weight_refs], axis=0)
    size = weights.shape[0]
    row = lax.broadcasted_iota(jnp.int32, (size, size), 0)
    col = lax.broadcasted_iota(jnp.int32, (size, size), 1)
    turn = jnp.where(row == (col ^ (group - 1)), 1.0, 0.0).astype(BF16)
    mirrored = dot(turn, weights).astype(BF16)
    return (dot(windows_ref[:count, :], weights, NT) + dot(windows_ref[count:, :], mirrored, NT)).astype(BF16)


def chosen_rows(direct, weight_refs, begins):
    return jnp.concatenate([direct[a : a + ref.shape[0], :] for ref, a in zip(weight_refs, begins)], axis=0)


def early_input_kernel(plan, rows, begins, late_begins, device_ref, windows_ref, own_ref, other_ref, out_ref, late_ref):
    refs = (own_ref, other_ref)
    direct, _ = selection(plan, device_ref[0], rows, out_ref.shape[1], GET_TURNS)
    out_ref[...] = dot(rounded_sums(2 * rows, windows_ref, refs), chosen_rows(direct, refs, begins)).astype(BF16)
    place = 0
    for begin, size in late_begins:
        late_ref[place : place + size, :] = direct[begin : begin + size, :]
        place += size


def late_input_kernel(group, windows_ref, early_ref, chosen_ref, *refs):
    weight_refs, (out_hbm, out_ref, stored) = refs[:-3], refs[-3:]
    sums = rounded_sums(group, windows_ref, weight_refs)
    half, copies = out_ref.shape[0] // 2, []
    for place in range(2):
        cut = slice(place * half, (place + 1) * half)
        out_ref[cut, :] = (early_ref[cut, :].astype(F32) + dot(sums[cut], chosen_ref[...])).astype(BF16)
        copies.append(pltpu.make_async_copy(out_ref.at[cut, :], out_hbm.at[cut, :], stored.at[place]))
        copies[-1].start()
    for copy in copies:
        copy.wait()


def reversed_taps(blocks):
    rows, half = blocks[0].shape
    far = dot(jnp.concatenate(blocks, axis=0), anti_identity(half)).astype(BF16)
    far = dot(anti_identity(len(blocks) * rows), far)
    return [far[k * rows : (k + 1) * rows] for k in range(len(blocks))]


def tied_kernel(own_ref, far_ref, out_ref):
    taps, rows, width = far_ref.shape
    half = width // 2
    for place, near_ref, other_ref in ((0, own_ref, far_ref), (1, far_ref, own_ref)):
        other = reversed_taps([other_ref[k, :, half:] for k in range(taps)])
        for k in range(taps):
            out_ref[place * rows : (place + 1) * rows, k * half : (k + 1) * half] = (
                near_ref[k, :, :half].astype(F32) + other[k]
            ).astype(BF16)


def finish_kernel(*refs):
    out_ref = refs[-1]
    taps, rows, width = out_ref.shape
    half = width // 2
    cuts = [slice(k * half, (k + 1) * half) for k in range(taps)]
    own = jnp.concatenate([ref[...] for ref in refs[:-1:2]], axis=1)
    got = jnp.concatenate([ref[...] for ref in refs[1:-1:2]], axis=1).astype(F32)
    far, near = own[rows:] + got[:rows], own[:rows] + got[rows:]
    high = far.astype(BF16)
    low = (far - high.astype(F32)).astype(BF16)
    high, low = (reversed_taps([part[:, cut] for cut in cuts]) for part in (high, low))
    for k, cut in enumerate(cuts):
        out_ref[k, :, :half] = near[:, cut]
        out_ref[k, :, half:] = high[k] + low[k]


ON_CHIP = pltpu.VMEM


def call(kernel, outs, args, scalars=0, flops=0, aliases=None, given=(), limit=24, off_chip=(), scratch=()):
    held = pl.BlockSpec(memory_space=ON_CHIP)
    spaces = {i: ON_CHIP for i in given} | {i: pltpu.HBM for i in off_chip}
    args = [pltpu.with_memory_space_constraint(a, spaces[i]) if i in spaces else a for i, a in enumerate(args)]
    result = pl.pallas_call(
        kernel,
        out_shape=[(ON_CHIP if stays else jax.ShapeDtypeStruct)(shape, dtype) for shape, dtype, stays in outs],
        in_specs=[pl.BlockSpec(memory_space=pltpu.SMEM)] * scalars
        + [pl.BlockSpec(memory_space=pltpu.HBM) if i in off_chip else held for i in range(scalars, len(args))],
        scratch_shapes=list(scratch),
        out_specs=[pl.BlockSpec(memory_space=pltpu.HBM) if out[2] is None else held for out in outs],
        input_output_aliases=aliases or {},
        cost_estimate=pl.CostEstimate(
            flops=flops,
            transcendentals=0,
            bytes_accessed=sum(math.prod(out[0]) * jnp.dtype(out[1]).itemsize for out in outs)
            + sum(a.size * a.dtype.itemsize for a in args[scalars:]),
        ),
        compiler_params=pltpu.CompilerParams(vmem_limit_bytes=limit << 20),
    )(*args)
    return result if len(outs) > 1 else result[0]


def edges(block, reach):
    count, where = lax.axis_size("pos"), lax.axis_index("pos")
    top, bottom = block[:, -reach:], block[:, :reach]
    if count == 2:
        got = lax.ppermute(jnp.where(where == 0, top, bottom), "pos", [(0, 1), (1, 0)])
        none = jnp.zeros_like(got)
        low, high = jnp.where(where == 0, none, got), jnp.where(where == 0, got, none)
    else:
        forward = [(i, i + 1) for i in range(count - 1)]
        low = lax.ppermute(top, "pos", forward)
        high = lax.ppermute(bottom, "pos", [(b, a) for a, b in forward])
    return jnp.concatenate([low, high], axis=1)


def on_device(plan, inputs, pre_act, grad_out, weight):
    return both_gradients(plan, inputs, pre_act, grad_out, weight)


def both_gradients(plan, inputs, pre_act, grad_out, weight):
    seqs, length, width = inputs.shape
    rows, taps, _ = weight.shape
    half, reach = width // 2, (taps - 1) // 2
    depth, count = taps * half, seqs * length
    work = 4 * count * depth * half
    device = (lax.axis_index("dp") * plan.pos + lax.axis_index("pos")).astype(jnp.int32).reshape(1)

    by_tap = jnp.transpose(weight, (1, 0, 2))
    far_weight = plan.complement(by_tap)
    ends = jnp.concatenate(
        [grad_pre_of(pre_act[:, :reach], grad_out[:, :reach]), grad_pre_of(pre_act[:, -reach:], grad_out[:, -reach:])],
        axis=1,
    )
    halo = edges(ends, reach)
    first_order, second_order, padded, windows = call(
        functools.partial(prepare_kernel, plan, rows, taps),
        [((half, 2 * count), BF16, True)] * 2
        + [((2 * seqs, length + 2 * EDGE, half), F32, True), ((2 * count, depth), BF16, True)],
        (device, inputs.reshape(count, width), pre_act, grad_out),
        scalars=1, flops=4 * count * width * width, off_chip=(1, 2, 3),
        scratch=(
            pltpu.VMEM((count, width), BF16), pltpu.VMEM((seqs, length, width), BF16),
            pltpu.VMEM((seqs, length, width), BF16), pltpu.SemaphoreType.DMA((3,)),
        ),
    )
    sums = [((half // 2, depth), BF16, True), ((half // 2, depth), F32, True)]
    sent, kept, _, windows = call(
        functools.partial(first_sums_kernel, taps),
        sums + [(padded.shape, F32, True), (windows.shape, BF16, True)],
        (first_order, halo, padded, windows), flops=work, aliases={2: 2, 3: 3}, given=(0, 1, 2, 3),
    )
    received = plan.swap(sent, "core")
    second_sent, second_kept = call(sums_kernel, sums, (second_order, windows), flops=work, given=(0, 1))
    cut = (taps + 1) // 2 * half
    chunks = (slice(0, cut), slice(cut, depth))
    for place, chunk in enumerate(chunks):
        arrived = plan.swap((kept[:, chunk] + received[:, chunk].astype(F32)).astype(BF16), "a")
        late_sums = [arrived] if place == 0 else late_sums + [arrived]
    second_got = plan.swap(second_sent, "core")
    pairs = []
    for place, chunk in enumerate(chunks):
        arrived = late_sums[place]
        middle = second_kept.shape[0] // 2

        def part(rows_of):
            own = second_kept[rows_of, chunk] + second_got[rows_of, chunk].astype(F32)
            return own + arrived[rows_of].astype(F32)

        sums = part(slice(0, middle))
        arrived = plan.swap(part(slice(middle, None)).astype(BF16), "b")
        for number, group in enumerate(plan.groups):
            if number == 0:
                sums = sums + arrived.astype(F32)
            masks = plan.group_masks(group)
            size = sums.shape[0] // len(masks)
            pieces = [
                plan.shift(sums[j * size : (j + 1) * size].astype(BF16), masks[j]).astype(F32)
                for j in range(1, len(masks))
            ]
            sums = functools.reduce(jnp.add, pieces, sums[:size])
        pairs += [sums, plan.complement(sums.astype(BF16))]
    grad_weight = jnp.transpose(
        call(
            finish_kernel, [((taps, rows, width), F32, False)], pairs,
            flops=4 * rows * depth * half, given=range(4),
        ),
        (1, 0, 2),
    )

    gathered = call(
        tied_kernel, [((2 * rows, depth), BF16, True)], (by_tap, far_weight),
        flops=4 * rows * depth * half, given=(1,),
    )
    gathered = jnp.concatenate([gathered, plan.swap(gathered, "b")], axis=0)
    for place in range(len(plan.groups) - 1, -1, -1):
        pieces = [plan.shift(gathered, mask) for mask in plan.group_masks(plan.groups[place])[1:]]
        if place:
            gathered = jnp.concatenate([gathered] + pieces, axis=0)
        else:
            relayed = jnp.concatenate(pieces, axis=0)
    size = gathered.shape[0]
    late = [plan.swap(gathered, "a")]
    late.append(plan.swap(relayed, "a"))
    gathered = jnp.concatenate([gathered, relayed], axis=0)
    span = gathered.shape[0]
    other = plan.swap(gathered, "core")
    for place in range(2):
        late.append(plan.swap(late[place], "core"))
    late_begins = [(begin, n) for core in (span, 3 * span) for begin, n in ((core, size), (core + size, span - size))]
    early, chosen = call(
        functools.partial(early_input_kernel, plan, rows, (0, 2 * span), late_begins),
        [((count, width), BF16, True), ((half, width), BF16, True)], (device, windows, gathered, other),
        scalars=1, flops=work, given=(1, 2, 3),
    )
    grad_input = call(
        functools.partial(late_input_kernel, 2 * rows),
        [((count, width), BF16, None)], (windows, early, chosen, *late),
        flops=work, given=range(7),
        scratch=(pltpu.VMEM((count, width), BF16), pltpu.SemaphoreType.DMA((2,))),
    ).reshape(seqs, length, width)
    return grad_input, grad_weight


def solution(mesh):
    plan = Plan(mesh.shape["dp"], mesh.shape["pos"])
    placed = (
        P("dp", "pos", None),
        P("dp", "pos", None),
        P("dp", "pos", None),
        P(("dp", "pos"), None, None),
    )
    return jax.shard_map(
        functools.partial(on_device, plan),
        mesh=mesh,
        in_specs=placed,
        out_specs=(P("dp", "pos", None), P(("dp", "pos"), None, None)),
        check_vma=False,
    )
```

```python
import functools
import math

import jax
import jax.numpy as jnp
from jax import lax
from jax.experimental import pallas as pl
from jax.experimental.pallas import tpu as pltpu
from jax.sharding import PartitionSpec as P


AXES = ("dp", "pos")
F32 = jnp.float32
BF16 = jnp.bfloat16
NT = (((1,), (1,)), ((), ()))


def gelu_slope(values):
    cdf = 0.5 * (1.0 + lax.erf(values * 0.7071067811865476))
    return cdf + values * jnp.exp(-0.5 * values * values) * 0.3989422804014327


def grad_pre_of(pre_act, grad_out):
    return (grad_out.astype(F32) * gelu_slope(pre_act.astype(F32))).astype(BF16)


class Plan:
    def __init__(self, dp, pos):
        self.dp, self.pos, self.count = dp, pos, dp * pos
        assert self.count & (self.count - 1) == 0
        dp_bits = [pos << b for b in range(dp.bit_length() - 1)]
        pos_bits = [1 << b for b in range(pos.bit_length() - 1)]
        self.core = dp_bits[0]
        self.cross = (dp_bits[1], pos_bits[0])
        rest = (dp_bits[2:] + pos_bits[1:])[:-1]
        self.groups = [rest[i : i + 2] for i in range(0, len(rest), 2)]

    def mask(self, device, stage):
        if stage == "core":
            return self.core
        parity = 1 if device & self.core else 0
        return self.cross[parity if stage == "a" else 1 - parity]

    def swap(self, block, stage):
        route = [(d, d ^ self.mask(d, stage)) for d in range(self.count)]
        return lax.ppermute(block, AXES, route)

    def group_masks(self, group):
        masks = [0]
        for bit in group:
            masks += [m | bit for m in masks]
        return masks

    def shift(self, block, mask):
        return lax.ppermute(block, AXES, [(d, d ^ mask) for d in range(self.count)])

    def complement(self, block):
        return self.shift(block, self.count - 1)

    def source(self, position, device, rows):
        shift = rows.bit_length() - 1
        slot, low = position >> shift, position & (rows - 1)
        bit = self.count.bit_length() - 2
        owner = device
        for turn in ("core", "a", "b", "rest", "mirror"):
            if turn == "rest":
                masks = [mask for group in self.groups for mask in reversed(group)]
            elif turn == "core":
                masks = [self.core]
            elif turn == "mirror":
                masks = [self.count - 1]
            else:
                odd = jnp.where((owner & self.core) != 0, 1, 0)
                odd = odd if turn == "a" else 1 - odd
                masks = [odd * self.cross[1] + (1 - odd) * self.cross[0]]
            for mask in masks:
                owner = owner ^ (((slot >> bit) & 1) * mask)
                bit -= 1
        return (owner << shift) + low


def anti_identity(size):
    row = lax.broadcasted_iota(jnp.int32, (size, size), 0)
    col = lax.broadcasted_iota(jnp.int32, (size, size), 1)
    return jnp.where(row + col == size - 1, 1.0, 0.0).astype(BF16)


def selection(plan, device, rows, width):
    position = lax.broadcasted_iota(jnp.int32, (width, 128), 0)
    lane = lax.broadcasted_iota(jnp.int32, (width, 128), 1)
    source = plan.source(position, device, rows)

    def one_hot(index):
        return jnp.concatenate(
            [jnp.where(index == lane + start, 1.0, 0.0).astype(BF16) for start in range(0, width, 128)],
            axis=1,
        )

    return one_hot(source), one_hot(width - 1 - source)


def dot(left, right, dims=(((1,), (0,)), ((), ()))):
    return lax.dot_general(left, right, dims, preferred_element_type=F32)


EDGE = 8


def window_start(strand, tap, taps):
    reach = (taps - 1) // 2
    return EDGE + reach - tap if strand == 0 else EDGE - reach + tap


def prepare_kernel(
    plan, rows, taps, device_ref, values_hbm, pre_hbm, out_grad_hbm,
    first_ref, second_ref, padded_ref, windows_ref,
    values_ref, pre_ref, out_grad_ref, arrived,
):
    seqs, length, width = pre_ref.shape
    half, count = width // 2, seqs * length
    pairs = ((pre_hbm, pre_ref), (out_grad_hbm, out_grad_ref), (values_hbm, values_ref))
    copies = [pltpu.make_async_copy(far, near, arrived.at[i]) for i, (far, near) in enumerate(pairs)]
    for copy in copies:
        copy.start()
    direct, mirror = selection(plan, device_ref[0], rows, width)
    for copy in copies:
        copy.wait()
    values = values_ref[...]
    quarter = width // 4
    for chosen, cols in ((direct, slice(0, count)), (mirror, slice(count, 2 * count))):
        ordered = dot(chosen, values, NT).astype(BF16)
        for out_ref, begins in ((first_ref, (3, 1)), (second_ref, (2, 0))):
            for place, begin in enumerate(begins):
                out_ref[place * quarter : (place + 1) * quarter, cols] = ordered[begin * quarter : (begin + 1) * quarter]
    flip = anti_identity(half)
    for b in range(seqs):
        grads = grad_pre_of(pre_ref[b], out_grad_ref[b])
        for strand in range(2):
            place = strand * seqs + b
            inner = grads[:, :half].astype(F32) if strand == 0 else dot(grads[:, half:], flip)
            padded_ref[place, :EDGE, :] = jnp.zeros((EDGE, half), F32)
            padded_ref[place, EDGE + length :, :] = jnp.zeros((EDGE, half), F32)
            padded_ref[place, EDGE : EDGE + length, :] = inner
            for tap in range(taps):
                start = window_start(strand, tap, taps)
                windows_ref[place * length : (place + 1) * length, tap * half : (tap + 1) * half] = (
                    padded_ref[place, start : start + length, :].astype(BF16)
                )


def first_sums_kernel(taps, order_ref, halo_ref, _, __, sent_ref, kept_ref, padded_ref, windows_ref):
    seqs, both, width = halo_ref.shape
    half, reach = width // 2, both // 2
    length = padded_ref.shape[1] - 2 * EDGE
    strip = 16
    flip = anti_identity(half)
    for b in range(seqs):
        for strand in range(2):
            place = strand * seqs + b
            edge = halo_ref[b]
            outer = edge[:, :half].astype(F32) if strand == 0 else dot(edge[:, half:], flip)
            padded_ref[place, EDGE - reach : EDGE, :] = outer[:reach]
            padded_ref[place, EDGE + length : EDGE + length + reach, :] = outer[reach:]
            for tap in range(taps):
                start = window_start(strand, tap, taps)
                for begin in (0, length - strip):
                    windows_ref[
                        place * length + begin : place * length + begin + strip, tap * half : (tap + 1) * half
                    ] = padded_ref[place, start + begin : start + begin + strip, :].astype(BF16)
    sums_kernel(order_ref, windows_ref, sent_ref, kept_ref)


def sums_kernel(order_ref, windows_ref, sent_ref, kept_ref):
    sums = dot(order_ref[...], windows_ref[...])
    size = sent_ref.shape[0]
    sent_ref[...] = sums[:size].astype(BF16)
    kept_ref[...] = sums[size:]


def rounded_sums(group, windows_ref, weight_refs):
    count = windows_ref.shape[0] // 2
    weights = jnp.concatenate([ref[...] for ref in weight_refs], axis=0)
    size = weights.shape[0]
    row = lax.broadcasted_iota(jnp.int32, (size, size), 0)
    col = lax.broadcasted_iota(jnp.int32, (size, size), 1)
    turn = jnp.where(row == (col ^ (group - 1)), 1.0, 0.0).astype(BF16)
    mirrored = dot(turn, weights).astype(BF16)
    return (dot(windows_ref[:count, :], weights, NT) + dot(windows_ref[count:, :], mirrored, NT)).astype(BF16)


def chosen_rows(direct, places):
    return jnp.concatenate([direct[begin : begin + size, :] for begin, size in places], axis=0)


def early_input_kernel(plan, rows, places, late_places, device_ref, windows_ref, own_ref, other_ref, out_ref, late_ref):
    direct, _ = selection(plan, device_ref[0], rows, out_ref.shape[1])
    sums = rounded_sums(2 * rows, windows_ref, (own_ref, other_ref))
    out_ref[...] = dot(sums, chosen_rows(direct, places)).astype(BF16)
    late_ref[...] = chosen_rows(direct, late_places)


def late_input_kernel(group, windows_ref, early_ref, chosen_ref, *refs):
    weight_refs, (out_hbm, out_ref, stored) = refs[:-3], refs[-3:]
    sums = rounded_sums(group, windows_ref, weight_refs)
    half, copies = out_ref.shape[0] // 2, []
    for place in range(2):
        cut = slice(place * half, (place + 1) * half)
        out_ref[cut, :] = (early_ref[cut, :].astype(F32) + dot(sums[cut], chosen_ref[...])).astype(BF16)
        copies.append(pltpu.make_async_copy(out_ref.at[cut, :], out_hbm.at[cut, :], stored.at[place]))
        copies[-1].start()
    for copy in copies:
        copy.wait()


def reversed_taps(blocks):
    rows, half = blocks[0].shape
    far = dot(jnp.concatenate(blocks, axis=0), anti_identity(half)).astype(BF16)
    far = dot(anti_identity(len(blocks) * rows), far)
    return [far[k * rows : (k + 1) * rows] for k in range(len(blocks))]


def tied_kernel(own_ref, far_ref, out_ref):
    taps, rows, width = far_ref.shape
    half = width // 2
    for place, near_ref, other_ref in ((0, own_ref, far_ref), (1, far_ref, own_ref)):
        other = reversed_taps([other_ref[k, :, half:] for k in range(taps)])
        for k in range(taps):
            out_ref[place * rows : (place + 1) * rows, k * half : (k + 1) * half] = (
                near_ref[k, :, :half].astype(F32) + other[k]
            ).astype(BF16)


def finish_kernel(*refs):
    out_ref = refs[-1]
    taps, rows, width = out_ref.shape
    half = width // 2
    cuts = [slice(k * half, (k + 1) * half) for k in range(taps)]
    own = jnp.concatenate([ref[...] for ref in refs[:-1:2]], axis=1)
    got = jnp.concatenate([ref[...] for ref in refs[1:-1:2]], axis=1).astype(F32)
    far, near = own[rows:] + got[:rows], own[:rows] + got[rows:]
    high = far.astype(BF16)
    low = (far - high.astype(F32)).astype(BF16)
    high, low = (reversed_taps([part[:, cut] for cut in cuts]) for part in (high, low))
    for k, cut in enumerate(cuts):
        out_ref[k, :, :half] = near[:, cut]
        out_ref[k, :, half:] = high[k] + low[k]


ON_CHIP = pltpu.VMEM


def call(kernel, outs, args, scalars=0, flops=0, aliases=None, given=(), limit=24, off_chip=(), scratch=()):
    held = pl.BlockSpec(memory_space=ON_CHIP)
    spaces = {i: ON_CHIP for i in given} | {i: pltpu.HBM for i in off_chip}
    args = [pltpu.with_memory_space_constraint(a, spaces[i]) if i in spaces else a for i, a in enumerate(args)]
    result = pl.pallas_call(
        kernel,
        out_shape=[(ON_CHIP if stays else jax.ShapeDtypeStruct)(shape, dtype) for shape, dtype, stays in outs],
        in_specs=[pl.BlockSpec(memory_space=pltpu.SMEM)] * scalars
        + [pl.BlockSpec(memory_space=pltpu.HBM) if i in off_chip else held for i in range(scalars, len(args))],
        scratch_shapes=list(scratch),
        out_specs=[pl.BlockSpec(memory_space=pltpu.HBM) if out[2] is None else held for out in outs],
        input_output_aliases=aliases or {},
        cost_estimate=pl.CostEstimate(
            flops=flops,
            transcendentals=0,
            bytes_accessed=sum(math.prod(out[0]) * jnp.dtype(out[1]).itemsize for out in outs)
            + sum(a.size * a.dtype.itemsize for a in args[scalars:]),
        ),
        compiler_params=pltpu.CompilerParams(vmem_limit_bytes=limit << 20),
    )(*args)
    return result if len(outs) > 1 else result[0]


def edges(block, reach):
    count, where = lax.axis_size("pos"), lax.axis_index("pos")
    top, bottom = block[:, -reach:], block[:, :reach]
    if count == 2:
        got = lax.ppermute(jnp.where(where == 0, top, bottom), "pos", [(0, 1), (1, 0)])
        none = jnp.zeros_like(got)
        low, high = jnp.where(where == 0, none, got), jnp.where(where == 0, got, none)
    else:
        forward = [(i, i + 1) for i in range(count - 1)]
        low = lax.ppermute(top, "pos", forward)
        high = lax.ppermute(bottom, "pos", [(b, a) for a, b in forward])
    return jnp.concatenate([low, high], axis=1)


def on_device(plan, inputs, pre_act, grad_out, weight):
    return both_gradients(plan, inputs, pre_act, grad_out, weight)


def both_gradients(plan, inputs, pre_act, grad_out, weight):
    seqs, length, width = inputs.shape
    rows, taps, _ = weight.shape
    half, reach = width // 2, (taps - 1) // 2
    depth, count = taps * half, seqs * length
    work = 4 * count * depth * half
    device = (lax.axis_index("dp") * plan.pos + lax.axis_index("pos")).astype(jnp.int32).reshape(1)

    by_tap = jnp.transpose(weight, (1, 0, 2))
    far_weight = plan.complement(by_tap)
    ends = jnp.concatenate(
        [grad_pre_of(pre_act[:, :reach], grad_out[:, :reach]), grad_pre_of(pre_act[:, -reach:], grad_out[:, -reach:])],
        axis=1,
    )
    halo = edges(ends, reach)
    first_order, second_order, padded, windows = call(
        functools.partial(prepare_kernel, plan, rows, taps),
        [((half, 2 * count), BF16, True)] * 2
        + [((2 * seqs, length + 2 * EDGE, half), F32, True), ((2 * count, depth), BF16, True)],
        (device, inputs.reshape(count, width), pre_act, grad_out),
        scalars=1, flops=4 * count * width * width, off_chip=(1, 2, 3),
        scratch=(
            pltpu.VMEM((count, width), BF16), pltpu.VMEM((seqs, length, width), BF16),
            pltpu.VMEM((seqs, length, width), BF16), pltpu.SemaphoreType.DMA((3,)),
        ),
    )
    sums = [((half // 2, depth), BF16, True), ((half // 2, depth), F32, True)]
    sent, kept, _, windows = call(
        functools.partial(first_sums_kernel, taps),
        sums + [(padded.shape, F32, True), (windows.shape, BF16, True)],
        (first_order, halo, padded, windows), flops=work, aliases={2: 2, 3: 3}, given=(0, 1, 2, 3),
    )
    received = plan.swap(sent, "core")
    second_sent, second_kept = call(sums_kernel, sums, (second_order, windows), flops=work, given=(0, 1))
    cut = (taps + 1) // 2 * half
    chunks = (slice(0, cut), slice(cut, depth))
    for place, chunk in enumerate(chunks):
        arrived = plan.swap((kept[:, chunk] + received[:, chunk].astype(F32)).astype(BF16), "a")
        late_sums = [arrived] if place == 0 else late_sums + [arrived]
    second_got = plan.swap(second_sent, "core")
    pairs = []
    for place, chunk in enumerate(chunks):
        arrived = late_sums[place]
        middle = second_kept.shape[0] // 2

        def part(rows_of):
            own = second_kept[rows_of, chunk] + second_got[rows_of, chunk].astype(F32)
            return own + arrived[rows_of].astype(F32)

        sums = part(slice(0, middle))
        arrived = plan.swap(part(slice(middle, None)).astype(BF16), "b")
        for number, group in enumerate(plan.groups):
            if number == 0:
                sums = sums + arrived.astype(F32)
            masks = plan.group_masks(group)
            size = sums.shape[0] // len(masks)
            pieces = [
                plan.shift(sums[j * size : (j + 1) * size].astype(BF16), masks[j]).astype(F32)
                for j in range(1, len(masks))
            ]
            sums = functools.reduce(jnp.add, pieces, sums[:size])
        pairs += [sums, plan.complement(sums.astype(BF16))]
    grad_weight = jnp.transpose(
        call(
            finish_kernel, [((taps, rows, width), F32, False)], pairs,
            flops=4 * rows * depth * half, given=range(4),
        ),
        (1, 0, 2),
    )

    gathered = call(
        tied_kernel, [((2 * rows, depth), BF16, True)], (by_tap, far_weight),
        flops=4 * rows * depth * half, given=(1,),
    )
    parts = [gathered, plan.swap(gathered, "b")]
    for place in range(len(plan.groups) - 1, 0, -1):
        masks = plan.group_masks(plan.groups[place])[1:]
        parts = [jnp.concatenate([part] + [plan.shift(part, mask) for mask in masks], axis=0) for part in parts]
    masks = plan.group_masks(plan.groups[0])
    relayed = []
    for place in range(2):
        relayed.append(jnp.concatenate([plan.shift(parts[place], mask) for mask in masks[1:]], axis=0))
    late = [plan.swap(jnp.concatenate(parts, axis=0), "a")]
    late.append(plan.swap(jnp.concatenate(relayed, axis=0), "a"))
    gathered = jnp.concatenate(parts + relayed, axis=0)
    span, size = gathered.shape[0], parts[0].shape[0]

    def places(base):
        return [
            (base + side * span // 2 + begin, n)
            for begin, n in ((0, size), (size, span // 2 - size)) for side in range(2)
        ]

    other = plan.swap(gathered, "core")
    for place in range(2):
        late.append(plan.swap(late[place], "core"))
    early_places, late_places = places(0) + places(2 * span), places(span) + places(3 * span)
    early, chosen = call(
        functools.partial(early_input_kernel, plan, rows, early_places, late_places),
        [((count, width), BF16, True), ((half, width), BF16, True)], (device, windows, gathered, other),
        scalars=1, flops=work, given=(1, 2, 3),
    )
    grad_input = call(
        functools.partial(late_input_kernel, 2 * rows),
        [((count, width), BF16, None)], (windows, early, chosen, *late),
        flops=work, given=range(7),
        scratch=(pltpu.VMEM((count, width), BF16), pltpu.SemaphoreType.DMA((2,))),
    ).reshape(seqs, length, width)
    return grad_input, grad_weight


def solution(mesh):
    plan = Plan(mesh.shape["dp"], mesh.shape["pos"])
    placed = (
        P("dp", "pos", None),
        P("dp", "pos", None),
        P("dp", "pos", None),
        P(("dp", "pos"), None, None),
    )
    return jax.shard_map(
        functools.partial(on_device, plan),
        mesh=mesh,
        in_specs=placed,
        out_specs=(P("dp", "pos", None), P(("dp", "pos"), None, None)),
        check_vma=False,
    )
```

```python
import functools
import math

import jax
import jax.numpy as jnp
from jax import lax
from jax.experimental import pallas as pl
from jax.experimental.pallas import tpu as pltpu
from jax.sharding import PartitionSpec as P


AXES = ("dp", "pos")
F32 = jnp.float32
BF16 = jnp.bfloat16
NT = (((1,), (1,)), ((), ()))


def gelu_slope(values):
    cdf = 0.5 * (1.0 + lax.erf(values * 0.7071067811865476))
    return cdf + values * jnp.exp(-0.5 * values * values) * 0.3989422804014327


def grad_pre_of(pre_act, grad_out):
    return (grad_out.astype(F32) * gelu_slope(pre_act.astype(F32))).astype(BF16)


class Plan:
    def __init__(self, dp, pos):
        self.dp, self.pos, self.count = dp, pos, dp * pos
        assert self.count & (self.count - 1) == 0
        dp_bits = [pos << b for b in range(dp.bit_length() - 1)]
        pos_bits = [1 << b for b in range(pos.bit_length() - 1)]
        self.core = dp_bits[0]
        self.cross = (dp_bits[1], pos_bits[0])
        rest = (dp_bits[2:] + pos_bits[1:])[:-1]
        self.groups = [rest[i : i + 2] for i in range(0, len(rest), 2)]

    def mask(self, device, stage):
        if stage == "core":
            return self.core
        parity = 1 if device & self.core else 0
        return self.cross[parity if stage == "a" else 1 - parity]

    def swap(self, block, stage):
        route = [(d, d ^ self.mask(d, stage)) for d in range(self.count)]
        return lax.ppermute(block, AXES, route)

    def group_masks(self, group):
        masks = [0]
        for bit in group:
            masks += [m | bit for m in masks]
        return masks

    def shift(self, block, mask):
        return lax.ppermute(block, AXES, [(d, d ^ mask) for d in range(self.count)])

    def complement(self, block):
        return self.shift(block, self.count - 1)

    def source(self, position, device, rows):
        shift = rows.bit_length() - 1
        slot, low = position >> shift, position & (rows - 1)
        bit = self.count.bit_length() - 2
        owner = device
        for turn in ("core", "a", "b", "rest", "mirror"):
            if turn == "rest":
                masks = [mask for group in self.groups for mask in reversed(group)]
            elif turn == "core":
                masks = [self.core]
            elif turn == "mirror":
                masks = [self.count - 1]
            else:
                odd = jnp.where((owner & self.core) != 0, 1, 0)
                odd = odd if turn == "a" else 1 - odd
                masks = [odd * self.cross[1] + (1 - odd) * self.cross[0]]
            for mask in masks:
                owner = owner ^ (((slot >> bit) & 1) * mask)
                bit -= 1
        return (owner << shift) + low


def anti_identity(size):
    row = lax.broadcasted_iota(jnp.int32, (size, size), 0)
    col = lax.broadcasted_iota(jnp.int32, (size, size), 1)
    return jnp.where(row + col == size - 1, 1.0, 0.0).astype(BF16)


def selection(plan, device, rows, width):
    position = lax.broadcasted_iota(jnp.int32, (width, 128), 0)
    lane = lax.broadcasted_iota(jnp.int32, (width, 128), 1)
    source = plan.source(position, device, rows)

    def one_hot(index):
        return jnp.concatenate(
            [jnp.where(index == lane + start, 1.0, 0.0).astype(BF16) for start in range(0, width, 128)],
            axis=1,
        )

    return one_hot(source), one_hot(width - 1 - source)


def dot(left, right, dims=(((1,), (0,)), ((), ()))):
    return lax.dot_general(left, right, dims, preferred_element_type=F32)


EDGE = 8


def window_start(strand, tap, taps):
    reach = (taps - 1) // 2
    return EDGE + reach - tap if strand == 0 else EDGE - reach + tap


def prepare_kernel(
    plan, rows, taps, device_ref, values_hbm, pre_hbm, out_grad_hbm,
    first_ref, second_ref, padded_ref, windows_ref,
    values_ref, pre_ref, out_grad_ref, arrived,
):
    seqs, length, width = pre_ref.shape
    half, count = width // 2, seqs * length
    pairs = ((pre_hbm, pre_ref), (out_grad_hbm, out_grad_ref), (values_hbm, values_ref))
    copies = [pltpu.make_async_copy(far, near, arrived.at[i]) for i, (far, near) in enumerate(pairs)]
    for copy in copies:
        copy.start()
    direct, mirror = selection(plan, device_ref[0], rows, width)
    for copy in copies:
        copy.wait()
    values = values_ref[...]
    quarter = width // 4
    for chosen, cols in ((direct, slice(0, count)), (mirror, slice(count, 2 * count))):
        ordered = dot(chosen, values, NT).astype(BF16)
        for out_ref, begins in ((first_ref, (3, 1)), (second_ref, (2, 0))):
            for place, begin in enumerate(begins):
                out_ref[place * quarter : (place + 1) * quarter, cols] = ordered[begin * quarter : (begin + 1) * quarter]
    flip = anti_identity(half)
    for b in range(seqs):
        grads = grad_pre_of(pre_ref[b], out_grad_ref[b])
        for strand in range(2):
            place = strand * seqs + b
            inner = grads[:, :half].astype(F32) if strand == 0 else dot(grads[:, half:], flip)
            padded_ref[place, :EDGE, :] = jnp.zeros((EDGE, half), F32)
            padded_ref[place, EDGE + length :, :] = jnp.zeros((EDGE, half), F32)
            padded_ref[place, EDGE : EDGE + length, :] = inner
            for tap in range(taps):
                start = window_start(strand, tap, taps)
                windows_ref[place * length : (place + 1) * length, tap * half : (tap + 1) * half] = (
                    padded_ref[place, start : start + length, :].astype(BF16)
                )


def first_sums_kernel(taps, order_ref, halo_ref, _, __, sent_ref, kept_ref, padded_ref, windows_ref):
    seqs, both, width = halo_ref.shape
    half, reach = width // 2, both // 2
    length = padded_ref.shape[1] - 2 * EDGE
    strip = 16
    flip = anti_identity(half)
    for b in range(seqs):
        for strand in range(2):
            place = strand * seqs + b
            edge = halo_ref[b]
            outer = edge[:, :half].astype(F32) if strand == 0 else dot(edge[:, half:], flip)
            padded_ref[place, EDGE - reach : EDGE, :] = outer[:reach]
            padded_ref[place, EDGE + length : EDGE + length + reach, :] = outer[reach:]
            for tap in range(taps):
                start = window_start(strand, tap, taps)
                for begin in (0, length - strip):
                    windows_ref[
                        place * length + begin : place * length + begin + strip, tap * half : (tap + 1) * half
                    ] = padded_ref[place, start + begin : start + begin + strip, :].astype(BF16)
    sums_kernel(order_ref, windows_ref, sent_ref, kept_ref)


def sums_kernel(order_ref, windows_ref, sent_ref, kept_ref):
    sums = dot(order_ref[...], windows_ref[...])
    size = sent_ref.shape[0]
    sent_ref[...] = sums[:size].astype(BF16)
    kept_ref[...] = sums[size:]


def rounded_sums(group, windows_ref, weight_refs):
    count = windows_ref.shape[0] // 2
    weights = jnp.concatenate([ref[...] for ref in weight_refs], axis=0)
    size = weights.shape[0]
    row = lax.broadcasted_iota(jnp.int32, (size, size), 0)
    col = lax.broadcasted_iota(jnp.int32, (size, size), 1)
    turn = jnp.where(row == (col ^ (group - 1)), 1.0, 0.0).astype(BF16)
    mirrored = dot(turn, weights).astype(BF16)
    return (dot(windows_ref[:count, :], weights, NT) + dot(windows_ref[count:, :], mirrored, NT)).astype(BF16)


def chosen_rows(direct, places):
    return jnp.concatenate([direct[begin : begin + size, :] for begin, size in places], axis=0)


def early_input_kernel(plan, rows, places, late_places, device_ref, windows_ref, own_ref, other_ref, out_ref, late_ref):
    direct, _ = selection(plan, device_ref[0], rows, out_ref.shape[1])
    sums = rounded_sums(2 * rows, windows_ref, (own_ref, other_ref))
    out_ref[...] = dot(sums, chosen_rows(direct, places)).astype(BF16)
    late_ref[...] = chosen_rows(direct, late_places)


def late_input_kernel(group, windows_ref, early_ref, chosen_ref, *refs):
    weight_refs, (out_hbm, out_ref, stored) = refs[:-3], refs[-3:]
    sums = rounded_sums(group, windows_ref, weight_refs)
    half, copies = out_ref.shape[0] // 2, []
    for place in range(2):
        cut = slice(place * half, (place + 1) * half)
        out_ref[cut, :] = (early_ref[cut, :].astype(F32) + dot(sums[cut], chosen_ref[...])).astype(BF16)
        copies.append(pltpu.make_async_copy(out_ref.at[cut, :], out_hbm.at[cut, :], stored.at[place]))
        copies[-1].start()
    for copy in copies:
        copy.wait()


def reversed_taps(blocks):
    rows, half = blocks[0].shape
    far = dot(jnp.concatenate(blocks, axis=0), anti_identity(half)).astype(BF16)
    far = dot(anti_identity(len(blocks) * rows), far)
    return [far[k * rows : (k + 1) * rows] for k in range(len(blocks))]


def tied_kernel(own_ref, far_ref, out_ref):
    taps, rows, width = far_ref.shape
    half = width // 2
    for place, near_ref, other_ref in ((0, own_ref, far_ref), (1, far_ref, own_ref)):
        other = reversed_taps([other_ref[k, :, half:] for k in range(taps)])
        for k in range(taps):
            out_ref[place * rows : (place + 1) * rows, k * half : (k + 1) * half] = (
                near_ref[k, :, :half].astype(F32) + other[k]
            ).astype(BF16)


def finish_kernel(got_ref, *refs):
    out_ref = refs[-1]
    taps, rows, width = out_ref.shape
    half = width // 2
    cuts = [slice(k * half, (k + 1) * half) for k in range(taps)]
    own, got = jnp.concatenate([ref[...] for ref in refs[:-1]], axis=1), got_ref[...].astype(F32)
    far, near = own[rows:] + got[:rows], own[:rows] + got[rows:]
    high = far.astype(BF16)
    low = (far - high.astype(F32)).astype(BF16)
    high, low = (reversed_taps([part[:, cut] for cut in cuts]) for part in (high, low))
    for k, cut in enumerate(cuts):
        out_ref[k, :, :half] = near[:, cut]
        out_ref[k, :, half:] = high[k] + low[k]


ON_CHIP = pltpu.VMEM


def call(kernel, outs, args, scalars=0, flops=0, aliases=None, given=(), limit=24, off_chip=(), scratch=()):
    held = pl.BlockSpec(memory_space=ON_CHIP)
    spaces = {i: ON_CHIP for i in given} | {i: pltpu.HBM for i in off_chip}
    args = [pltpu.with_memory_space_constraint(a, spaces[i]) if i in spaces else a for i, a in enumerate(args)]
    result = pl.pallas_call(
        kernel,
        out_shape=[(ON_CHIP if stays else jax.ShapeDtypeStruct)(shape, dtype) for shape, dtype, stays in outs],
        in_specs=[pl.BlockSpec(memory_space=pltpu.SMEM)] * scalars
        + [pl.BlockSpec(memory_space=pltpu.HBM) if i in off_chip else held for i in range(scalars, len(args))],
        scratch_shapes=list(scratch),
        out_specs=[pl.BlockSpec(memory_space=pltpu.HBM) if out[2] is None else held for out in outs],
        input_output_aliases=aliases or {},
        cost_estimate=pl.CostEstimate(
            flops=flops,
            transcendentals=0,
            bytes_accessed=sum(math.prod(out[0]) * jnp.dtype(out[1]).itemsize for out in outs)
            + sum(a.size * a.dtype.itemsize for a in args[scalars:]),
        ),
        compiler_params=pltpu.CompilerParams(vmem_limit_bytes=limit << 20),
    )(*args)
    return result if len(outs) > 1 else result[0]


def edges(block, reach):
    count, where = lax.axis_size("pos"), lax.axis_index("pos")
    top, bottom = block[:, -reach:], block[:, :reach]
    if count == 2:
        got = lax.ppermute(jnp.where(where == 0, top, bottom), "pos", [(0, 1), (1, 0)])
        none = jnp.zeros_like(got)
        low, high = jnp.where(where == 0, none, got), jnp.where(where == 0, got, none)
    else:
        forward = [(i, i + 1) for i in range(count - 1)]
        low = lax.ppermute(top, "pos", forward)
        high = lax.ppermute(bottom, "pos", [(b, a) for a, b in forward])
    return jnp.concatenate([low, high], axis=1)


def on_device(plan, inputs, pre_act, grad_out, weight):
    return both_gradients(plan, inputs, pre_act, grad_out, weight)


def both_gradients(plan, inputs, pre_act, grad_out, weight):
    seqs, length, width = inputs.shape
    rows, taps, _ = weight.shape
    half, reach = width // 2, (taps - 1) // 2
    depth, count = taps * half, seqs * length
    work = 4 * count * depth * half
    device = (lax.axis_index("dp") * plan.pos + lax.axis_index("pos")).astype(jnp.int32).reshape(1)

    by_tap = jnp.transpose(weight, (1, 0, 2))
    far_weight = plan.complement(by_tap)
    ends = jnp.concatenate(
        [grad_pre_of(pre_act[:, :reach], grad_out[:, :reach]), grad_pre_of(pre_act[:, -reach:], grad_out[:, -reach:])],
        axis=1,
    )
    halo = edges(ends, reach)
    first_order, second_order, padded, windows = call(
        functools.partial(prepare_kernel, plan, rows, taps),
        [((half, 2 * count), BF16, True)] * 2
        + [((2 * seqs, length + 2 * EDGE, half), F32, True), ((2 * count, depth), BF16, True)],
        (device, inputs.reshape(count, width), pre_act, grad_out),
        scalars=1, flops=4 * count * width * width, off_chip=(1, 2, 3),
        scratch=(
            pltpu.VMEM((count, width), BF16), pltpu.VMEM((seqs, length, width), BF16),
            pltpu.VMEM((seqs, length, width), BF16), pltpu.SemaphoreType.DMA((3,)),
        ),
    )
    sums = [((half // 2, depth), BF16, True), ((half // 2, depth), F32, True)]
    sent, kept, _, windows = call(
        functools.partial(first_sums_kernel, taps),
        sums + [(padded.shape, F32, True), (windows.shape, BF16, True)],
        (first_order, halo, padded, windows), flops=work, aliases={2: 2, 3: 3}, given=(0, 1, 2, 3),
    )
    received = plan.swap(sent, "core")
    second_sent, second_kept = call(sums_kernel, sums, (second_order, windows), flops=work, given=(0, 1))
    cut = 4 * taps // 5 * half
    chunks = (slice(0, cut), slice(cut, depth))
    for place, chunk in enumerate(chunks):
        arrived = plan.swap((kept[:, chunk] + received[:, chunk].astype(F32)).astype(BF16), "a")
        late_sums = [arrived] if place == 0 else late_sums + [arrived]
    second_got = plan.swap(second_sent, "core")
    done = []
    for place, chunk in enumerate(chunks):
        arrived = late_sums[place]
        middle = second_kept.shape[0] // 2

        def part(rows_of):
            own = second_kept[rows_of, chunk] + second_got[rows_of, chunk].astype(F32)
            return own + arrived[rows_of].astype(F32)

        sums = part(slice(0, middle))
        arrived = plan.swap(part(slice(middle, None)).astype(BF16), "b")
        for number, group in enumerate(plan.groups):
            if number == 0:
                sums = sums + arrived.astype(F32)
            masks = plan.group_masks(group)
            size = sums.shape[0] // len(masks)
            pieces = [
                plan.shift(sums[j * size : (j + 1) * size].astype(BF16), masks[j]).astype(F32)
                for j in range(1, len(masks))
            ]
            sums = functools.reduce(jnp.add, pieces, sums[:size])
        done.append(sums)
    got = plan.complement(jnp.concatenate([sums.astype(BF16) for sums in done], axis=1))
    grad_weight = jnp.transpose(
        call(
            finish_kernel, [((taps, rows, width), F32, False)], (got, *done),
            flops=4 * rows * depth * half, given=range(3),
        ),
        (1, 0, 2),
    )

    gathered = call(
        tied_kernel, [((2 * rows, depth), BF16, True)], (by_tap, far_weight),
        flops=4 * rows * depth * half, given=(1,),
    )
    parts = [gathered, plan.swap(gathered, "b")]
    for place in range(len(plan.groups) - 1, 0, -1):
        masks = plan.group_masks(plan.groups[place])[1:]
        parts = [jnp.concatenate([part] + [plan.shift(part, mask) for mask in masks], axis=0) for part in parts]
    masks = plan.group_masks(plan.groups[0])
    relayed = []
    for place in range(2):
        relayed.append(jnp.concatenate([plan.shift(parts[place], mask) for mask in masks[1:]], axis=0))
    late = [plan.swap(jnp.concatenate(parts, axis=0), "a")]
    late.append(plan.swap(jnp.concatenate(relayed, axis=0), "a"))
    gathered = jnp.concatenate(parts + relayed, axis=0)
    span, size = gathered.shape[0], parts[0].shape[0]

    def places(base):
        return [
            (base + side * span // 2 + begin, n)
            for begin, n in ((0, size), (size, span // 2 - size)) for side in range(2)
        ]

    other = plan.swap(gathered, "core")
    for place in range(2):
        late.append(plan.swap(late[place], "core"))
    early_places, late_places = places(0) + places(2 * span), places(span) + places(3 * span)
    early, chosen = call(
        functools.partial(early_input_kernel, plan, rows, early_places, late_places),
        [((count, width), BF16, True), ((half, width), BF16, True)], (device, windows, gathered, other),
        scalars=1, flops=work, given=(1, 2, 3),
    )
    grad_input = call(
        functools.partial(late_input_kernel, 2 * rows),
        [((count, width), BF16, None)], (windows, early, chosen, *late),
        flops=work, given=range(7),
        scratch=(pltpu.VMEM((count, width), BF16), pltpu.SemaphoreType.DMA((2,))),
    ).reshape(seqs, length, width)
    return grad_input, grad_weight


def solution(mesh):
    plan = Plan(mesh.shape["dp"], mesh.shape["pos"])
    placed = (
        P("dp", "pos", None),
        P("dp", "pos", None),
        P("dp", "pos", None),
        P(("dp", "pos"), None, None),
    )
    return jax.shard_map(
        functools.partial(on_device, plan),
        mesh=mesh,
        in_specs=placed,
        out_specs=(P("dp", "pos", None), P(("dp", "pos"), None, None)),
        check_vma=False,
    )
```
